512 devices in a mesh: ctrl: 16 (over y, x_lo), shelf: 32 (over z, x_hi, core).
Axes of the slice: x: 4 (x_hi: 2, x_lo: 2; x = x_hi * 2 + x_lo), y: 8, z: 8, core: 2. Of those that a mesh axis runs over, the one named last changes fastest.
Arguments:
- prob: float32 [768, 1024, 256], P('ctrl', 'shelf'), as said below
- ctrl_rates: float32 [768, 768], P('shelf'), as said below
- shelf_rates: float32 [1024, 1024], P('shelf'), as said below
- disk_rates: float32 [256, 256], replicated, as said below
- labels: int32 [768, 1024], P('ctrl', 'shelf'), may hold values from 0 to 255, as said below
Outputs:
- refined: float32 [768, 1024, 256], P('ctrl', 'shelf')
- coarse: float32 [256], replicated
The draws below stay inside these ranges and needn't reach their ends.
Inputs may be any that keep to these rules, and one draw needn't show every extreme that they name: `prob`: positive. `ctrl_rates`: nonnegative entries. `shelf_rates`: nonnegative entries. `disk_rates`: nonnegative entries. Every block number from 0 to 255 labels at least one pair.
All inputs are finite; a program needn't handle non-finite values.
Results may differ from the reference program's by a relative error of at most 0.004.
Values may be sent and summed in bfloat16 or wider, within the bound.
A program may use at most 64 MiB of HBM per device.

```python
import jax
import jax.numpy as jnp
from jax import lax

CTRL = 768
SHELF = 1024
DISK = 256
NBLK = 256
STEPS = 2


def rates_matrix(key, size):
    first_key, second_key = jax.random.split(jax.random.fold_in(key, 5))
    places = jnp.arange(size).astype(jnp.float32)
    spacing = jnp.abs(places[:, None] - places[None, :])
    reach = jnp.exp(-spacing / (size / 4.0)) * (4.0 / size)
    rough = jax.random.uniform(first_key, (size, size), jnp.float32, 0.0, 1.0)
    diagonal = jax.random.uniform(second_key, (size,), jnp.float32, 0.5, 1.5)
    identity = jnp.eye(size, dtype=jnp.float32)
    return rough * reach * (1.0 - identity) + identity * diagonal[None, :]


def draw_ctrl_rates(key, part):
    return rates_matrix(jax.random.fold_in(key, 21), CTRL)


def draw_shelf_rates(key, part):
    return rates_matrix(jax.random.fold_in(key, 22), SHELF)


def draw_disk_rates(key, part):
    return rates_matrix(jax.random.fold_in(key, 23), DISK)


def draw_prob(key, part):
    first_key = jax.random.fold_in(jax.random.fold_in(key, 3), 0)
    ctrl_pos = jnp.arange(CTRL).astype(jnp.float32) / CTRL
    shelf_pos = jnp.arange(SHELF).astype(jnp.float32) / SHELF
    disk_pos = jnp.arange(DISK).astype(jnp.float32) / DISK
    trend = jnp.power(3.0, ctrl_pos)[:, None, None] * jnp.power(3.0, shelf_pos)[None, :, None] * jnp.power(2.0, disk_pos)[None, None, :]
    base = jnp.exp(0.6 * jnp.clip(jax.random.normal(first_key, (CTRL, SHELF, DISK), jnp.float32), -3.0, 3.0))
    return base * trend


def draw_labels(key, part):
    first_key, second_key, third_key = jax.random.split(jax.random.fold_in(key, 11), 3)
    tile_rows = CTRL // 32
    tile_cols = SHELF // 16
    order = jax.random.permutation(first_key, 512)
    tile_label = (order % NBLK).reshape(32, 16)
    ctrl_idx = jnp.arange(CTRL)[:, None]
    shelf_idx = jnp.arange(SHELF)[None, :]
    base = tile_label[ctrl_idx // tile_rows, shelf_idx // tile_cols]
    others = jax.random.randint(second_key, (CTRL, SHELF), 0, NBLK)
    dice = jax.random.randint(third_key, (CTRL, SHELF), 0, 8)
    flip = jnp.logical_and(dice == 0, ctrl_idx % tile_rows != 0)
    return jnp.where(flip, others, base).astype(jnp.int32)


def setup_inputs(seed: int = 0) -> dict:
    seeds = jax.random.split(jax.random.key(seed), 6)
    return {
        "prob": draw_prob(jax.random.fold_in(seeds[5], 71), 0),
        "ctrl_rates": draw_ctrl_rates(jax.random.fold_in(seeds[5], 71), 0),
        "shelf_rates": draw_shelf_rates(jax.random.fold_in(seeds[5], 71), 0),
        "disk_rates": draw_disk_rates(jax.random.fold_in(seeds[5], 71), 0),
        "labels": draw_labels(jax.random.fold_in(seeds[5], 71), 0),
    }


def reference(prob, ctrl_rates, shelf_rates, disk_rates, labels):
    ctrl_bf = ctrl_rates.astype(jnp.bfloat16)
    shelf_bf = shelf_rates.astype(jnp.bfloat16)
    disk_bf = disk_rates.astype(jnp.bfloat16)
    ctrl_out = jnp.sum(ctrl_bf.astype(jnp.float32), axis=1)
    shelf_out = jnp.sum(shelf_bf.astype(jnp.float32), axis=1)
    disk_out = jnp.sum(disk_bf.astype(jnp.float32), axis=1)
    uniform_rate = 1.05 * (jnp.max(ctrl_out) * jnp.max(shelf_out)) * jnp.max(disk_out)
    retain = 1.0 - ctrl_out[:, None, None] * shelf_out[None, :, None] * disk_out[None, None, :] / uniform_rate
    iterate = prob
    for repeat in range(STEPS):
        rounded = iterate.astype(jnp.bfloat16)
        section_one = jnp.dot(ctrl_bf.T.astype(jnp.float32), rounded.reshape(CTRL, SHELF * DISK).astype(jnp.float32), preferred_element_type=jnp.float32).astype(jnp.bfloat16)
        section_two = jnp.dot(section_one.reshape(CTRL * SHELF, DISK).astype(jnp.float32), disk_bf.astype(jnp.float32), preferred_element_type=jnp.float32).astype(jnp.bfloat16)
        across = jnp.transpose(section_two.reshape(CTRL, SHELF, DISK), (1, 0, 2)).reshape(SHELF, CTRL * DISK)
        section_three = jnp.dot(shelf_bf.T.astype(jnp.float32), across.astype(jnp.float32), preferred_element_type=jnp.float32).astype(jnp.bfloat16)
        section_three = jnp.transpose(section_three.reshape(SHELF, CTRL, DISK), (1, 0, 2))
        iterate = section_three.astype(jnp.float32) / uniform_rate + iterate * retain
    blocks = jnp.arange(NBLK, dtype=jnp.int32)
    member = (labels[:, :, None] == blocks[None, None, :]).astype(jnp.bfloat16)
    first_pass = jnp.dot(ctrl_bf.astype(jnp.float32), member.reshape(CTRL, SHELF * NBLK).astype(jnp.float32), preferred_element_type=jnp.float32).astype(jnp.bfloat16)
    across_ops = jnp.transpose(first_pass.reshape(CTRL, SHELF, NBLK), (1, 0, 2)).reshape(SHELF, CTRL * NBLK)
    coarse_op = jnp.dot(shelf_bf.astype(jnp.float32), across_ops.astype(jnp.float32), preferred_element_type=jnp.float32).astype(jnp.bfloat16)
    coarse_op = jnp.transpose(coarse_op.reshape(SHELF, CTRL, NBLK), (1, 0, 2))
    pair_mass = jnp.sum(iterate, axis=2).reshape(-1)
    pair_kept = jnp.sum(iterate * retain, axis=2).reshape(-1)
    weighted = jnp.dot(iterate.reshape(CTRL * SHELF, DISK), disk_out, precision=lax.Precision.HIGHEST)
    flat_labels = labels.reshape(-1)
    block_mass = jax.ops.segment_sum(pair_mass, flat_labels, num_segments=NBLK)
    block_kept = jax.ops.segment_sum(pair_kept, flat_labels, num_segments=NBLK)
    flow = jax.ops.segment_sum(weighted[:, None] * coarse_op.reshape(CTRL * SHELF, NBLK).astype(jnp.float32), flat_labels, num_segments=NBLK)
    identity = jnp.eye(NBLK, dtype=jnp.float32)
    transit = (flow / uniform_rate + identity * block_kept[:, None]) / block_mass[:, None]
    system = identity - transit + 1.0 / NBLK
    target = jnp.full((NBLK,), 1.0 / NBLK, dtype=jnp.float32)
    balance = jnp.linalg.solve(system.T, target)
    ratio_share = balance / block_mass
    refined = iterate * ratio_share[labels][:, :, None] * float(CTRL * SHELF * DISK)
    coarse = balance * NBLK
    return (refined, coarse)
```

```python
import functools

import jax
import jax.numpy as jnp
from jax import lax
from jax.experimental import pallas as pl
from jax.experimental.pallas import tpu as pltpu
from jax.sharding import PartitionSpec as P

CTRL = 768
SHELF = 1024
DISK = 256
NBLK = 256
STEPS = 2
GROUP = 8
MESH = pl.DeviceIdType.MESH
VMEM = pltpu.MemorySpace.VMEM
HIGHEST = lax.Precision.HIGHEST


def place():
    ctrl = lax.axis_index("ctrl")
    shelf = lax.axis_index("shelf")
    plane_me = (ctrl % 2) * 4 + shelf % 4
    deep_me = shelf // 4
    high_me = ctrl // 2

    def plane(member):
        return (ctrl - ctrl % 2 + member // 4, shelf - shelf % 4 + member % 4)

    def deep(member):
        return (ctrl, member * 4 + shelf % 4)

    def high(member):
        return (member * 2 + ctrl % 2, shelf)

    return (plane_me, plane), (deep_me, deep), (high_me, high)


def greet(groups):
    barrier = pltpu.get_barrier_semaphore()
    for me, peer in groups:

        def signal(step, carry, me=me, peer=peer):
            pl.semaphore_signal(
                barrier, inc=1, device_id=peer((me + step) % GROUP), device_id_type=MESH
            )
            return carry

        lax.fori_loop(1, GROUP, signal, 0)
    pl.semaphore_wait(barrier, len(groups) * (GROUP - 1))


def exchange(group, streams, send_sem, recv_sem):
    me, peer = group

    def copy(step, index):
        source, target = streams[index]
        member = (me + step) % GROUP
        return pltpu.make_async_remote_copy(
            src_ref=source(member),
            dst_ref=target,
            send_sem=send_sem.at[index, step],
            recv_sem=recv_sem.at[index, step],
            device_id=peer(member),
            device_id_type=MESH,
        )

    def start(step, carry):
        for index in range(len(streams)):
            copy(step, index).start()
        return carry

    def finish(step, carry):
        for index in range(len(streams)):
            copy(step, index).wait()
        return carry

    lax.fori_loop(1, GROUP, start, 0)
    lax.fori_loop(1, GROUP, finish, 0)


def reduce_kernel(
    part_ref, mass_ref, sum_ref, total_ref,
    rows, tiles, highs, deeps, blocks, mass_plane, mass_deep, mass_high,
    send_sem, recv_sem,
):
    plane, deep, high = place()
    greet((plane, deep, high))
    plane_me, deep_me, high_me = plane[0], deep[0], high[0]

    exchange(
        plane,
        (
            (lambda m: part_ref.at[pl.ds(pl.multiple_of(m * 32, 32), 32)], rows.at[plane_me]),
            (lambda m: mass_ref, mass_plane.at[plane_me]),
        ),
        send_sem.at[0], recv_sem.at[0],
    )
    rows[plane_me] = part_ref[pl.ds(pl.multiple_of(plane_me * 32, 32), 32)]
    mass_plane[plane_me] = mass_ref[...]
    mine = jnp.sum(rows[...], axis=0)
    for tile in range(GROUP):
        r, h = tile // 2, tile % 2
        tiles[tile] = mine[r * 8 : r * 8 + 8, h * 128 : h * 128 + 128]
    total_ref[...] = jnp.sum(mass_plane[...], axis=0)

    exchange(
        deep,
        (
            (lambda m: tiles.at[m], deeps.at[deep_me]),
            (lambda m: total_ref, mass_deep.at[deep_me]),
        ),
        send_sem.at[1], recv_sem.at[1],
    )
    deeps[deep_me] = tiles[deep_me]
    mass_deep[deep_me] = total_ref[...]
    highs[high_me] = jnp.sum(deeps[...], axis=0)
    mass_high[high_me] = jnp.sum(mass_deep[...], axis=0)

    exchange(
        high,
        (
            (lambda m: highs.at[high_me], highs.at[high_me]),
            (lambda m: mass_high.at[high_me], mass_high.at[high_me]),
        ),
        send_sem.at[2], recv_sem.at[2],
    )
    total_ref[...] = jnp.sum(mass_high[...], axis=0)
    blocks[deep_me] = jnp.sum(highs[...], axis=0)

    exchange(
        deep,
        ((lambda m: blocks.at[deep_me], blocks.at[deep_me]),),
        send_sem.at[3], recv_sem.at[3],
    )
    for tile in range(GROUP):
        r, h = tile // 2, tile % 2
        sum_ref[
            pl.ds(pl.multiple_of(plane_me * 32 + r * 8, 8), 8), h * 128 : h * 128 + 128
        ] = blocks[tile]
    own = sum_ref.at[pl.ds(pl.multiple_of(plane_me * 32, 32), 32)]
    exchange(plane, ((lambda m: own, own),), send_sem.at[4], recv_sem.at[4])


def reduce_all(part, mass):
    tile = (8, 128)
    return pl.pallas_call(
        reduce_kernel,
        out_shape=(
            jax.ShapeDtypeStruct((NBLK, NBLK), jnp.float32),
            jax.ShapeDtypeStruct(tile, jnp.float32),
        ),
        in_specs=[pl.BlockSpec(memory_space=VMEM)] * 2,
        out_specs=(pl.BlockSpec(memory_space=VMEM), pl.BlockSpec(memory_space=VMEM)),
        scratch_shapes=[
            pltpu.VMEM((GROUP, 32, NBLK), jnp.float32),
            pltpu.VMEM((GROUP, *tile), jnp.float32),
            pltpu.VMEM((GROUP, *tile), jnp.float32),
            pltpu.VMEM((GROUP, *tile), jnp.float32),
            pltpu.VMEM((GROUP, *tile), jnp.float32),
            pltpu.VMEM((GROUP, *tile), jnp.float32),
            pltpu.VMEM((GROUP, *tile), jnp.float32),
            pltpu.VMEM((GROUP, *tile), jnp.float32),
            pltpu.SemaphoreType.DMA((5, 2, GROUP)),
            pltpu.SemaphoreType.DMA((5, 2, GROUP)),
        ],
        compiler_params=pltpu.CompilerParams(collective_id=1, has_side_effects=True),
        name="reduce_all",
    )(part, mass)


def member_kernel(labels_ref, factor_ref, out_ref):
    count = labels_ref.shape[1]
    blocks = lax.broadcasted_iota(jnp.int32, (NBLK, count), 0).astype(jnp.float32)

    def body(row, carry):
        names = jnp.broadcast_to(labels_ref[pl.ds(row, 1), :], (NBLK, count))
        member = jnp.where(names == blocks, 1.0, 0.0).astype(jnp.bfloat16)
        out_ref[row] = lax.dot_general(
            factor_ref[...], member, (((1,), (1,)), ((), ())), preferred_element_type=jnp.float32
        ).astype(out_ref.dtype)
        return carry

    lax.fori_loop(0, labels_ref.shape[0], body, 0)


def member_product(labels, factor):
    return pl.pallas_call(
        member_kernel,
        out_shape=jax.ShapeDtypeStruct((labels.shape[0], factor.shape[0], NBLK), jnp.bfloat16),
        in_specs=[pl.BlockSpec(memory_space=VMEM)] * 2,
        out_specs=pl.BlockSpec(memory_space=VMEM),
        compiler_params=pltpu.CompilerParams(vmem_limit_bytes=40 << 20),
        name="member_product",
    )(labels, factor)


def flow_kernel(labels_ref, weight_ref, factor_ref, first_ref, out_ref, wide, held):
    count = labels_ref.shape[1]
    depth = factor_ref.shape[0]
    blocks = lax.broadcasted_iota(jnp.int32, (NBLK, count), 0).astype(jnp.float32)

    def body(row, carry):
        names = jnp.broadcast_to(labels_ref[pl.ds(row, 1), :], (NBLK, count))
        member = jnp.where(names == blocks, 1.0, 0.0).astype(jnp.bfloat16)
        scaled = factor_ref[...] * weight_ref[pl.ds(row, 1), :]
        upper = scaled.astype(jnp.bfloat16)
        wide[0:depth, :] = upper
        wide[depth : 2 * depth, :] = (scaled - upper.astype(jnp.float32)).astype(jnp.bfloat16)
        both = lax.dot_general(
            wide[...], member, (((1,), (1,)), ((), ())), preferred_element_type=jnp.float32
        )
        held[:, pl.ds(row, 1), :] = (both[0:depth] + both[depth:]).reshape(depth, 1, NBLK)
        return carry

    lax.fori_loop(0, labels_ref.shape[0], body, 0)
    rows = held.shape[0] * held.shape[1]
    mine = held[...].reshape(rows, NBLK)
    first = first_ref[...].reshape(rows, NBLK)
    upper = mine.astype(jnp.bfloat16)
    lower = (mine - upper.astype(jnp.float32)).astype(jnp.bfloat16)
    dims = (((0,), (0,)), ((), ()))
    out_ref[...] = lax.dot_general(
        upper, first, dims, preferred_element_type=jnp.float32
    ) + lax.dot_general(lower, first, dims, preferred_element_type=jnp.float32)


def flow_product(labels, weight, factor, first):
    depth, count = factor.shape
    return pl.pallas_call(
        flow_kernel,
        out_shape=jax.ShapeDtypeStruct((NBLK, NBLK), jnp.float32),
        in_specs=[pl.BlockSpec(memory_space=VMEM)] * 4,
        out_specs=pl.BlockSpec(memory_space=VMEM),
        scratch_shapes=[
            pltpu.VMEM((2 * depth, count), jnp.bfloat16),
            pltpu.VMEM((depth, labels.shape[0], NBLK), jnp.float32),
        ],
        compiler_params=pltpu.CompilerParams(vmem_limit_bytes=40 << 20),
        name="flow_product",
    )(labels, weight, factor, first)


def balance_kernel(numer_ref, mass_ref, out_ref, power):
    size = NBLK
    power[...] = numer_ref[...] / mass_ref[...] - 1.0 / size
    start = jnp.full((8, size), 1.0 / size, jnp.float32)

    def going(state):
        turn, height, row = state
        return jnp.logical_and(turn < 40, height > 1e-10)

    def turn_once(state):
        turn, height, row = state
        now = power[...]
        row = row + jnp.dot(row, now, precision=HIGHEST, preferred_element_type=jnp.float32)
        after = jnp.dot(now, now, precision=HIGHEST, preferred_element_type=jnp.float32)
        power[...] = after
        return turn + 1, jnp.max(jnp.abs(after)), row

    state = (jnp.int32(0), jnp.max(jnp.abs(power[...])), start)
    out_ref[...] = lax.while_loop(going, turn_once, state)[2]


def balance_of(numer, mass):
    return pl.pallas_call(
        balance_kernel,
        out_shape=jax.ShapeDtypeStruct((8, NBLK), jnp.float32),
        in_specs=[pl.BlockSpec(memory_space=VMEM)] * 2,
        out_specs=pl.BlockSpec(memory_space=VMEM),
        scratch_shapes=[pltpu.VMEM((NBLK, NBLK), jnp.float32)],
        name="balance",
    )(numer, mass)[0]


def ctrl_product(tensor, factor, pattern):
    result = jnp.einsum(
        pattern,
        lax.all_to_all(tensor, "ctrl", split_axis=0, concat_axis=1, tiled=True),
        factor,
        preferred_element_type=jnp.float32,
    ).astype(jnp.bfloat16)
    return lax.all_to_all(result, "ctrl", split_axis=1, concat_axis=0, tiled=True)


def shelf_product(tensor, factor, pattern):
    flattened = tensor.reshape(tensor.shape[0], tensor.shape[1] * tensor.shape[2])
    regrouped = lax.all_to_all(flattened, "shelf", split_axis=1, concat_axis=0, tiled=True)
    result = jnp.einsum(pattern, regrouped, factor, preferred_element_type=jnp.float32).astype(
        jnp.bfloat16
    )
    returned = lax.all_to_all(result, "shelf", split_axis=0, concat_axis=1, tiled=True)
    return returned.reshape(tensor.shape)


def local(prob, ctrl_rates, shelf_rates, disk_rates, labels):
    ctrl_bf = lax.all_gather(ctrl_rates.astype(jnp.bfloat16), "shelf", axis=0, tiled=True)
    shelf_bf = lax.all_gather(shelf_rates.astype(jnp.bfloat16), "shelf", axis=0, tiled=True)
    disk_bf = disk_rates.astype(jnp.bfloat16)
    ctrl_out = jnp.sum(ctrl_bf.astype(jnp.float32), axis=1)
    shelf_out = jnp.sum(shelf_bf.astype(jnp.float32), axis=1)
    disk_out = jnp.sum(disk_bf.astype(jnp.float32), axis=1)
    uniform_rate = 1.05 * (jnp.max(ctrl_out) * jnp.max(shelf_out)) * jnp.max(disk_out)
    ctrl_rows = prob.shape[0]
    shelf_rows = prob.shape[1]
    ctrl_at = lax.axis_index("ctrl") * ctrl_rows
    shelf_at = lax.axis_index("shelf") * shelf_rows
    ctrl_loc = lax.dynamic_slice_in_dim(ctrl_out, ctrl_at, ctrl_rows)
    shelf_loc = lax.dynamic_slice_in_dim(shelf_out, shelf_at, shelf_rows)
    retain = (
        1.0
        - ctrl_loc[None, :, None]
        * shelf_loc[:, None, None]
        * disk_out[None, None, :]
        / uniform_rate
    )
    label_f = labels.astype(jnp.bfloat16)
    ctrl_labels = lax.all_gather(label_f.T, "ctrl", axis=1, tiled=True).astype(jnp.float32)
    shelf_labels = lax.all_gather(label_f, "shelf", axis=1, tiled=True).astype(jnp.float32)

    iterate = jnp.transpose(prob, (1, 0, 2))
    for repeat in range(STEPS):
        rounded = iterate.astype(jnp.bfloat16)
        section_one = ctrl_product(rounded, ctrl_bf, "bac,ad->bdc")
        section_two = jnp.dot(
            section_one.reshape(shelf_rows * ctrl_rows, DISK),
            disk_bf,
            preferred_element_type=jnp.float32,
        )
        section_two = section_two.astype(jnp.bfloat16).reshape(section_one.shape)
        section_three = shelf_product(section_two, shelf_bf, "bq,bd->dq")
        iterate = section_three.astype(jnp.float32) / uniform_rate + iterate * retain

    first = member_product(ctrl_labels, lax.dynamic_slice_in_dim(ctrl_bf, ctrl_at, ctrl_rows))
    shelf_columns = lax.dynamic_slice_in_dim(shelf_bf, shelf_at, shelf_rows, axis=1)
    shelf_columns = shelf_columns.T.astype(jnp.float32)

    pair_mass = jnp.sum(iterate, axis=2)
    pair_kept = jnp.sum(iterate * retain, axis=2)
    weighted = jnp.sum(iterate * disk_out, axis=2)
    shelf_weight = lax.all_gather(weighted.T, "shelf", axis=1, tiled=True)
    part = flow_product(shelf_labels, shelf_weight, shelf_columns, first) / uniform_rate
    pair_count = shelf_rows * ctrl_rows
    own_labels = labels.T
    blocks = jnp.arange(NBLK, dtype=jnp.int32)
    member_table = (own_labels.reshape(pair_count)[:, None] == blocks[None, :]).astype(
        jnp.float32
    )
    terms = jnp.dot(
        jnp.stack([pair_mass.reshape(pair_count), pair_kept.reshape(pair_count)]),
        member_table,
        precision=HIGHEST,
    )
    identity = jnp.eye(NBLK, dtype=jnp.float32)
    part = part + identity * terms[1][:, None]
    mass_tile = jnp.zeros((8, 128), jnp.float32).at[0:2].set(terms[0].reshape(2, 128))
    numer, mass_sum = reduce_all(part, mass_tile)
    block_mass = mass_sum[0:2].reshape(NBLK)
    balance = balance_of(numer, jnp.broadcast_to(block_mass[:, None], (NBLK, NBLK)))
    ratio_share = balance / block_mass
    pair_share = jnp.dot(member_table, ratio_share, precision=HIGHEST).reshape(
        shelf_rows, ctrl_rows
    )
    scaled = iterate * pair_share[:, :, None] * float(CTRL * SHELF * DISK)
    refined = jnp.transpose(scaled, (1, 0, 2))
    coarse = balance * NBLK
    return (refined, coarse)


def solution(mesh):
    placed = (P("ctrl", "shelf", None), P("shelf", None), P("shelf", None), P(), P("ctrl", "shelf"))
    return jax.shard_map(
        local,
        mesh=mesh,
        in_specs=placed,
        out_specs=(P("ctrl", "shelf", None), P()),
        check_vma=False,
    )
```

```python
import functools

import jax
import jax.numpy as jnp
from jax import lax
from jax.experimental import pallas as pl
from jax.experimental.pallas import tpu as pltpu
from jax.sharding import PartitionSpec as P

CTRL = 768
SHELF = 1024
DISK = 256
NBLK = 256
STEPS = 2
GROUP = 8
MESH = pl.DeviceIdType.MESH
VMEM = pltpu.MemorySpace.VMEM
HIGHEST = lax.Precision.HIGHEST


def place():
    ctrl = lax.axis_index("ctrl")
    shelf = lax.axis_index("shelf")
    plane_me = (ctrl % 2) * 4 + shelf % 4
    deep_me = shelf // 4
    high_me = ctrl // 2

    def plane(member):
        return (ctrl - ctrl % 2 + member // 4, shelf - shelf % 4 + member % 4)

    def deep(member):
        return (ctrl, member * 4 + shelf % 4)

    def high(member):
        return (member * 2 + ctrl % 2, shelf)

    return (plane_me, plane), (deep_me, deep), (high_me, high)


def greet(groups):
    barrier = pltpu.get_barrier_semaphore()
    for me, peer in groups:

        def signal(step, carry, me=me, peer=peer):
            pl.semaphore_signal(
                barrier, inc=1, device_id=peer((me + step) % GROUP), device_id_type=MESH
            )
            return carry

        lax.fori_loop(1, GROUP, signal, 0)
    pl.semaphore_wait(barrier, len(groups) * (GROUP - 1))


def exchange(group, streams, send_sem, recv_sem):
    me, peer = group

    def copy(step, index):
        source, target = streams[index]
        member = (me + step) % GROUP
        return pltpu.make_async_remote_copy(
            src_ref=source(member),
            dst_ref=target,
            send_sem=send_sem.at[index, step],
            recv_sem=recv_sem.at[index, step],
            device_id=peer(member),
            device_id_type=MESH,
        )

    def start(step, carry):
        for index in range(len(streams)):
            copy(step, index).start()
        return carry

    def finish(step, carry):
        for index in range(len(streams)):
            copy(step, index).wait()
        return carry

    lax.fori_loop(1, GROUP, start, 0)
    lax.fori_loop(1, GROUP, finish, 0)


def reduce_kernel(
    part_ref, mass_ref, sum_ref, total_ref,
    rows, tiles, highs, deeps, blocks, mass_plane, mass_deep, mass_high,
    send_sem, recv_sem,
):
    plane, deep, high = place()
    greet((plane, deep, high))
    plane_me, deep_me, high_me = plane[0], deep[0], high[0]

    exchange(
        plane,
        (
            (lambda m: part_ref.at[pl.ds(pl.multiple_of(m * 32, 32), 32)], rows.at[plane_me]),
            (lambda m: mass_ref, mass_plane.at[plane_me]),
        ),
        send_sem.at[0], recv_sem.at[0],
    )
    rows[plane_me] = part_ref[pl.ds(pl.multiple_of(plane_me * 32, 32), 32)]
    mass_plane[plane_me] = mass_ref[...]
    mine = jnp.sum(rows[...], axis=0)
    for tile in range(GROUP):
        r, h = tile // 2, tile % 2
        tiles[tile] = mine[r * 8 : r * 8 + 8, h * 128 : h * 128 + 128]
    total_ref[...] = jnp.sum(mass_plane[...], axis=0)

    exchange(
        deep,
        (
            (lambda m: tiles.at[m], deeps.at[deep_me]),
            (lambda m: total_ref, mass_deep.at[deep_me]),
        ),
        send_sem.at[1], recv_sem.at[1],
    )
    deeps[deep_me] = tiles[deep_me]
    mass_deep[deep_me] = total_ref[...]
    highs[high_me] = jnp.sum(deeps[...], axis=0)
    mass_high[high_me] = jnp.sum(mass_deep[...], axis=0)

    exchange(
        high,
        (
            (lambda m: highs.at[high_me], highs.at[high_me]),
            (lambda m: mass_high.at[high_me], mass_high.at[high_me]),
        ),
        send_sem.at[2], recv_sem.at[2],
    )
    total_ref[...] = jnp.sum(mass_high[...], axis=0)
    blocks[deep_me] = jnp.sum(highs[...], axis=0)

    exchange(
        deep,
        ((lambda m: blocks.at[deep_me], blocks.at[deep_me]),),
        send_sem.at[3], recv_sem.at[3],
    )
    for tile in range(GROUP):
        r, h = tile // 2, tile % 2
        sum_ref[
            pl.ds(pl.multiple_of(plane_me * 32 + r * 8, 8), 8), h * 128 : h * 128 + 128
        ] = blocks[tile]
    own = sum_ref.at[pl.ds(pl.multiple_of(plane_me * 32, 32), 32)]
    exchange(plane, ((lambda m: own, own),), send_sem.at[4], recv_sem.at[4])


def reduce_all(part, mass):
    tile = (8, 128)
    return pl.pallas_call(
        reduce_kernel,
        out_shape=(
            jax.ShapeDtypeStruct((NBLK, NBLK), jnp.float32),
            jax.ShapeDtypeStruct(tile, jnp.float32),
        ),
        in_specs=[pl.BlockSpec(memory_space=VMEM)] * 2,
        out_specs=(pl.BlockSpec(memory_space=VMEM), pl.BlockSpec(memory_space=VMEM)),
        scratch_shapes=[
            pltpu.VMEM((GROUP, 32, NBLK), jnp.float32),
            pltpu.VMEM((GROUP, *tile), jnp.float32),
            pltpu.VMEM((GROUP, *tile), jnp.float32),
            pltpu.VMEM((GROUP, *tile), jnp.float32),
            pltpu.VMEM((GROUP, *tile), jnp.float32),
            pltpu.VMEM((GROUP, *tile), jnp.float32),
            pltpu.VMEM((GROUP, *tile), jnp.float32),
            pltpu.VMEM((GROUP, *tile), jnp.float32),
            pltpu.SemaphoreType.DMA((5, 2, GROUP)),
            pltpu.SemaphoreType.DMA((5, 2, GROUP)),
        ],
        compiler_params=pltpu.CompilerParams(collective_id=1, has_side_effects=True),
        name="reduce_all",
    )(part, mass)


def member_kernel(labels_ref, factor_ref, out_ref):
    count = labels_ref.shape[1]
    blocks = lax.broadcasted_iota(jnp.int32, (NBLK, count), 0).astype(jnp.float32)

    def body(row, carry):
        names = jnp.broadcast_to(labels_ref[pl.ds(row, 1), :], (NBLK, count))
        member = jnp.where(names == blocks, 1.0, 0.0).astype(jnp.bfloat16)
        out_ref[row] = lax.dot_general(
            factor_ref[...], member, (((1,), (1,)), ((), ())), preferred_element_type=jnp.float32
        ).astype(out_ref.dtype)
        return carry

    lax.fori_loop(0, labels_ref.shape[0], body, 0)


def member_product(labels, factor):
    return pl.pallas_call(
        member_kernel,
        out_shape=jax.ShapeDtypeStruct((labels.shape[0], factor.shape[0], NBLK), jnp.bfloat16),
        in_specs=[pl.BlockSpec(memory_space=VMEM)] * 2,
        out_specs=pl.BlockSpec(memory_space=VMEM),
        compiler_params=pltpu.CompilerParams(vmem_limit_bytes=40 << 20),
        name="member_product",
    )(labels, factor)


def flow_kernel(labels_ref, weight_ref, factor_ref, first_ref, out_ref, wide, held):
    count = labels_ref.shape[1]
    depth = factor_ref.shape[0]
    blocks = lax.broadcasted_iota(jnp.int32, (NBLK, count), 0).astype(jnp.float32)

    def body(row, carry):
        names = jnp.broadcast_to(labels_ref[pl.ds(row, 1), :], (NBLK, count))
        member = jnp.where(names == blocks, 1.0, 0.0).astype(jnp.bfloat16)
        scaled = factor_ref[...] * weight_ref[pl.ds(row, 1), :]
        upper = scaled.astype(jnp.bfloat16)
        wide[0:depth, :] = upper
        wide[depth : 2 * depth, :] = (scaled - upper.astype(jnp.float32)).astype(jnp.bfloat16)
        both = lax.dot_general(
            wide[...], member, (((1,), (1,)), ((), ())), preferred_element_type=jnp.float32
        )
        held[:, pl.ds(row, 1), :] = (both[0:depth] + both[depth:]).reshape(depth, 1, NBLK)
        return carry

    lax.fori_loop(0, labels_ref.shape[0], body, 0)
    rows = held.shape[0] * held.shape[1]
    mine = held[...].reshape(rows, NBLK)
    first = first_ref[...].reshape(rows, NBLK)
    upper = mine.astype(jnp.bfloat16)
    lower = (mine - upper.astype(jnp.float32)).astype(jnp.bfloat16)
    dims = (((0,), (0,)), ((), ()))
    out_ref[...] = lax.dot_general(
        upper, first, dims, preferred_element_type=jnp.float32
    ) + lax.dot_general(lower, first, dims, preferred_element_type=jnp.float32)


def flow_product(labels, weight, factor, first):
    depth, count = factor.shape
    return pl.pallas_call(
        flow_kernel,
        out_shape=jax.ShapeDtypeStruct((NBLK, NBLK), jnp.float32),
        in_specs=[pl.BlockSpec(memory_space=VMEM)] * 4,
        out_specs=pl.BlockSpec(memory_space=VMEM),
        scratch_shapes=[
            pltpu.VMEM((2 * depth, count), jnp.bfloat16),
            pltpu.VMEM((depth, labels.shape[0], NBLK), jnp.float32),
        ],
        compiler_params=pltpu.CompilerParams(vmem_limit_bytes=40 << 20),
        name="flow_product",
    )(labels, weight, factor, first)


def balance_kernel(numer_ref, mass_ref, out_ref, power):
    size = NBLK
    power[...] = numer_ref[...] / mass_ref[...] - 1.0 / size
    start = jnp.full((8, size), 1.0 / size, jnp.float32)

    def going(state):
        turn, height, row = state
        return jnp.logical_and(turn < 40, height > 1e-10)

    def turn_once(state):
        turn, height, row = state
        now = power[...]
        row = row + jnp.dot(row, now, precision=HIGHEST, preferred_element_type=jnp.float32)
        after = jnp.dot(now, now, precision=HIGHEST, preferred_element_type=jnp.float32)
        power[...] = after
        return turn + 1, jnp.max(jnp.abs(after)), row

    state = (jnp.int32(0), jnp.max(jnp.abs(power[...])), start)
    out_ref[...] = lax.while_loop(going, turn_once, state)[2]


def balance_of(numer, mass):
    return pl.pallas_call(
        balance_kernel,
        out_shape=jax.ShapeDtypeStruct((8, NBLK), jnp.float32),
        in_specs=[pl.BlockSpec(memory_space=VMEM)] * 2,
        out_specs=pl.BlockSpec(memory_space=VMEM),
        scratch_shapes=[pltpu.VMEM((NBLK, NBLK), jnp.float32)],
        name="balance",
    )(numer, mass)[0]


def spread_small(own, wide, stages, send_sem, recv_sem):
    (outer_me, outer_size, outer_peer), (inner_me, inner_size, inner_peer) = stages

    def stage(which, me, size, peer, piece):
        def copy(step):
            return pltpu.make_async_remote_copy(
                src_ref=piece,
                dst_ref=piece,
                send_sem=send_sem.at[which, step],
                recv_sem=recv_sem.at[which, step],
                device_id=peer((me + step) % size),
                device_id_type=MESH,
            )

        def start(step, carry):
            copy(step).start()
            return carry

        def finish(step, carry):
            copy(step).wait()
            return carry

        return start, finish, size

    wide[inner_me, outer_me] = own
    first = stage(0, outer_me, outer_size, outer_peer, wide.at[inner_me, outer_me])
    second = stage(1, inner_me, inner_size, inner_peer, wide.at[inner_me])
    return first, second


def run_loop(part):
    start, finish, size = part
    lax.fori_loop(1, size, start, 0)
    lax.fori_loop(1, size, finish, 0)


def greet_each(peers):
    barrier = pltpu.get_barrier_semaphore()
    count = 0
    for me, size, peer in peers:

        def signal(step, carry, me=me, size=size, peer=peer):
            pl.semaphore_signal(
                barrier, inc=1, device_id=peer((me + step) % size), device_id_type=MESH
            )
            return carry

        lax.fori_loop(1, size, signal, 0)
        count += size - 1
    pl.semaphore_wait(barrier, count)


def shelf_stages():
    ctrl = lax.axis_index("ctrl")
    shelf = lax.axis_index("shelf")
    return (
        (shelf // 4, 8, lambda m: (ctrl, m * 4 + shelf % 4)),
        (shelf % 4, 4, lambda m: (ctrl, shelf - shelf % 4 + m)),
    )


def ctrl_stages():
    ctrl = lax.axis_index("ctrl")
    shelf = lax.axis_index("shelf")
    return (
        (ctrl // 2, 8, lambda m: (m * 2 + ctrl % 2, shelf)),
        (ctrl % 2, 2, lambda m: (ctrl - ctrl % 2 + m, shelf)),
    )


def weight_kernel(own_ref, wide_ref, send_sem, recv_sem):
    stages = shelf_stages()
    greet_each(stages)
    first, second = spread_small(own_ref[...], wide_ref, stages, send_sem, recv_sem)
    run_loop(first)
    run_loop(second)


def gather_weight(own):
    return pl.pallas_call(
        weight_kernel,
        out_shape=jax.ShapeDtypeStruct((4, 8, 16, 128), jnp.float32),
        in_specs=[pl.BlockSpec(memory_space=VMEM)],
        out_specs=pl.BlockSpec(memory_space=VMEM),
        scratch_shapes=[pltpu.SemaphoreType.DMA((2, 8)), pltpu.SemaphoreType.DMA((2, 8))],
        compiler_params=pltpu.CompilerParams(collective_id=2, has_side_effects=True),
        name="gather_weight",
    )(own)


def rows_kernel(
    ctrl_ref, shelf_ref, label_ref, ctrl_all, shelf_all, by_shelf, by_ctrl,
    swap_send, swap_recv, ring_send, ring_recv, pair_send, pair_recv,
    send_a, recv_a, send_b, recv_b,
):
    ctrl = lax.axis_index("ctrl")
    shelf = lax.axis_index("shelf")
    deep, side, core = shelf // 4, (shelf // 2) % 2, shelf % 2
    stages_a, stages_b = shelf_stages(), ctrl_stages()
    greet_each(stages_a + stages_b)

    wides = (ctrl_all, shelf_all)
    ctrl_all[deep, side, core] = ctrl_ref[...]
    shelf_all[deep, side, core] = shelf_ref[...]

    def remote(piece, send_sem, recv_sem, target):
        return pltpu.make_async_remote_copy(
            src_ref=piece, dst_ref=piece, send_sem=send_sem, recv_sem=recv_sem,
            device_id=(ctrl, target), device_id_type=MESH,
        )

    across = shelf + 2 - 4 * side
    swaps = [
        remote(wide.at[deep, side, core], swap_send.at[n], swap_recv.at[n], across)
        for n, wide in enumerate(wides)
    ]
    for swap in swaps:
        swap.start()
    label_a = spread_small(label_ref[...], by_shelf, stages_a, send_a, recv_a)
    label_b = spread_small(label_ref[...], by_ctrl, stages_b, send_b, recv_b)
    run_loop(label_a[0])
    run_loop(label_b[0])
    for swap in swaps:
        swap.wait()

    right = ((deep + 1) % 8) * 4 + shelf % 4
    left = ((deep + 7) % 8) * 4 + shelf % 4
    sibling = shelf + 1 - 2 * core

    def pair(n, block):
        return remote(wides[n].at[block, :, core], pair_send.at[n, block], pair_recv.at[n, block], sibling)

    def hop(n, way, count):
        block = (deep + 8 - count + 1) % 8 if way == 0 else (deep + count - 1) % 8
        return remote(
            wides[n].at[block, :, core],
            ring_send.at[n, way, count - 1],
            ring_recv.at[n, way, count - 1],
            right if way == 0 else left,
        )

    def used(n, way, count):
        return count < 4 or n == way

    for n in range(2):
        for way in range(2):
            hop(n, way, 1).start()
        pair(n, deep).start()
    for count in range(1, 5):
        for n in range(2):
            for way in range(2):
                if not used(n, way, count):
                    continue
                hop(n, way, count).wait_recv()
                if count < 4 and used(n, way, count + 1):
                    hop(n, way, count + 1).start()
                pair(n, (deep + 8 - count) % 8 if way == 0 else (deep + count) % 8).start()
    run_loop(label_a[1])
    run_loop(label_b[1])
    for count in range(1, 5):
        for n in range(2):
            for way in range(2):
                if used(n, way, count):
                    hop(n, way, count).wait_send()
    for block in range(8):
        for n in range(2):
            pltpu.make_async_remote_copy(
                src_ref=wides[n].at[block, :, core],
                dst_ref=wides[n].at[block, :, 1 - core],
                send_sem=pair_send.at[n, block], recv_sem=pair_recv.at[n, block],
                device_id=(ctrl, sibling), device_id_type=MESH,
            ).wait()


def gather_rows(ctrl_rows, shelf_rows, label_tile):
    return pl.pallas_call(
        rows_kernel,
        out_shape=(
            jax.ShapeDtypeStruct((8, 2, 2, *ctrl_rows.shape), jnp.bfloat16),
            jax.ShapeDtypeStruct((8, 2, 2, *shelf_rows.shape), jnp.bfloat16),
            jax.ShapeDtypeStruct((4, 8, 16, 128), jnp.float32),
            jax.ShapeDtypeStruct((2, 8, 16, 128), jnp.float32),
        ),
        in_specs=[pl.BlockSpec(memory_space=VMEM)] * 3,
        out_specs=tuple([pl.BlockSpec(memory_space=VMEM)] * 4),
        scratch_shapes=[
            pltpu.SemaphoreType.DMA((2,)),
            pltpu.SemaphoreType.DMA((2,)),
            pltpu.SemaphoreType.DMA((2, 2, 4)),
            pltpu.SemaphoreType.DMA((2, 2, 4)),
            pltpu.SemaphoreType.DMA((2, 8)),
            pltpu.SemaphoreType.DMA((2, 8)),
            pltpu.SemaphoreType.DMA((2, 8)),
            pltpu.SemaphoreType.DMA((2, 8)),
            pltpu.SemaphoreType.DMA((2, 8)),
            pltpu.SemaphoreType.DMA((2, 8)),
        ],
        compiler_params=pltpu.CompilerParams(
            collective_id=3, has_side_effects=True, vmem_limit_bytes=32 << 20
        ),
        name="gather_rows",
    )(ctrl_rows, shelf_rows, label_tile)


def as_tile(values):
    return jnp.pad(values.reshape(12, 128), ((0, 4), (0, 0)))


def shelf_wide(tiles):
    kept = tiles[:, :, 0:12].reshape(4, 8, 48, 32)
    return jnp.transpose(kept, (2, 1, 0, 3)).reshape(48, SHELF)


def ctrl_wide(tiles):
    kept = tiles[:, :, 0:12].reshape(2, 8, 48, 32)
    return jnp.transpose(kept, (3, 1, 0, 2)).reshape(32, CTRL)


def ctrl_product(tensor, factor, pattern):
    result = jnp.einsum(
        pattern,
        lax.all_to_all(tensor, "ctrl", split_axis=0, concat_axis=1, tiled=True),
        factor,
        preferred_element_type=jnp.float32,
    ).astype(jnp.bfloat16)
    return lax.all_to_all(result, "ctrl", split_axis=1, concat_axis=0, tiled=True)


def shelf_product(tensor, factor, pattern):
    flattened = tensor.reshape(tensor.shape[0], tensor.shape[1] * tensor.shape[2])
    regrouped = lax.all_to_all(flattened, "shelf", split_axis=1, concat_axis=0, tiled=True)
    result = jnp.einsum(pattern, regrouped, factor, preferred_element_type=jnp.float32).astype(
        jnp.bfloat16
    )
    returned = lax.all_to_all(result, "shelf", split_axis=0, concat_axis=1, tiled=True)
    return returned.reshape(tensor.shape)


def local(prob, ctrl_rates, shelf_rates, disk_rates, labels):
    ctrl_all, shelf_all, by_shelf, by_ctrl = gather_rows(
        ctrl_rates.astype(jnp.bfloat16),
        shelf_rates.astype(jnp.bfloat16),
        as_tile(labels.astype(jnp.float32)),
    )
    ctrl_bf = ctrl_all.reshape(CTRL, CTRL)
    shelf_bf = shelf_all.reshape(SHELF, SHELF)
    shelf_labels = shelf_wide(by_shelf)
    ctrl_labels = ctrl_wide(by_ctrl)
    disk_bf = disk_rates.astype(jnp.bfloat16)
    ctrl_out = jnp.sum(ctrl_bf.astype(jnp.float32), axis=1)
    shelf_out = jnp.sum(shelf_bf.astype(jnp.float32), axis=1)
    disk_out = jnp.sum(disk_bf.astype(jnp.float32), axis=1)
    uniform_rate = 1.05 * (jnp.max(ctrl_out) * jnp.max(shelf_out)) * jnp.max(disk_out)
    ctrl_rows = prob.shape[0]
    shelf_rows = prob.shape[1]
    ctrl_at = lax.axis_index("ctrl") * ctrl_rows
    shelf_at = lax.axis_index("shelf") * shelf_rows
    ctrl_loc = lax.dynamic_slice_in_dim(ctrl_out, ctrl_at, ctrl_rows)
    shelf_loc = lax.dynamic_slice_in_dim(shelf_out, shelf_at, shelf_rows)
    retain = (
        1.0
        - ctrl_loc[None, :, None]
        * shelf_loc[:, None, None]
        * disk_out[None, None, :]
        / uniform_rate
    )
    iterate = jnp.transpose(prob, (1, 0, 2))
    for repeat in range(STEPS):
        rounded = iterate.astype(jnp.bfloat16)
        section_one = ctrl_product(rounded, ctrl_bf, "bac,ad->bdc")
        section_two = jnp.dot(
            section_one.reshape(shelf_rows * ctrl_rows, DISK),
            disk_bf,
            preferred_element_type=jnp.float32,
        )
        section_two = section_two.astype(jnp.bfloat16).reshape(section_one.shape)
        section_three = shelf_product(section_two, shelf_bf, "bq,bd->dq")
        iterate = section_three.astype(jnp.float32) / uniform_rate + iterate * retain

    first = member_product(ctrl_labels, lax.dynamic_slice_in_dim(ctrl_bf, ctrl_at, ctrl_rows))
    shelf_columns = lax.dynamic_slice_in_dim(shelf_bf, shelf_at, shelf_rows, axis=1)
    shelf_columns = shelf_columns.T.astype(jnp.float32)

    pair_mass = jnp.sum(iterate, axis=2)
    pair_kept = jnp.sum(iterate * retain, axis=2)
    weighted = jnp.sum(iterate * disk_out, axis=2)
    shelf_weight = shelf_wide(gather_weight(as_tile(weighted.T)))
    part = flow_product(shelf_labels, shelf_weight, shelf_columns, first) / uniform_rate
    pair_count = shelf_rows * ctrl_rows
    own_labels = labels.T
    blocks = jnp.arange(NBLK, dtype=jnp.int32)
    member_table = (own_labels.reshape(pair_count)[:, None] == blocks[None, :]).astype(
        jnp.float32
    )
    terms = jnp.dot(
        jnp.stack([pair_mass.reshape(pair_count), pair_kept.reshape(pair_count)]),
        member_table,
        precision=HIGHEST,
    )
    identity = jnp.eye(NBLK, dtype=jnp.float32)
    part = part + identity * terms[1][:, None]
    mass_tile = jnp.zeros((8, 128), jnp.float32).at[0:2].set(terms[0].reshape(2, 128))
    numer, mass_sum = reduce_all(part, mass_tile)
    block_mass = mass_sum[0:2].reshape(NBLK)
    balance = balance_of(numer, jnp.broadcast_to(block_mass[:, None], (NBLK, NBLK)))
    ratio_share = balance / block_mass
    pair_share = jnp.dot(member_table, ratio_share, precision=HIGHEST).reshape(
        shelf_rows, ctrl_rows
    )
    scaled = iterate * pair_share[:, :, None] * float(CTRL * SHELF * DISK)
    refined = jnp.transpose(scaled, (1, 0, 2))
    coarse = balance * NBLK
    return (refined, coarse)


def solution(mesh):
    placed = (P("ctrl", "shelf", None), P("shelf", None), P("shelf", None), P(), P("ctrl", "shelf"))
    return jax.shard_map(
        local,
        mesh=mesh,
        in_specs=placed,
        out_specs=(P("ctrl", "shelf", None), P()),
        check_vma=False,
    )
```

```python
import functools

import jax
import jax.numpy as jnp
from jax import lax
from jax.experimental import pallas as pl
from jax.experimental.pallas import tpu as pltpu
from jax.sharding import PartitionSpec as P

CTRL = 768
SHELF = 1024
DISK = 256
NBLK = 256
STEPS = 2
GROUP = 8
MESH = pl.DeviceIdType.MESH
VMEM = pltpu.MemorySpace.VMEM
HIGHEST = lax.Precision.HIGHEST


def place():
    ctrl = lax.axis_index("ctrl")
    shelf = lax.axis_index("shelf")
    plane_me = (ctrl % 2) * 4 + shelf % 4
    deep_me = shelf // 4
    high_me = ctrl // 2

    def plane(member):
        return (ctrl - ctrl % 2 + member // 4, shelf - shelf % 4 + member % 4)

    def deep(member):
        return (ctrl, member * 4 + shelf % 4)

    def high(member):
        return (member * 2 + ctrl % 2, shelf)

    return (plane_me, plane), (deep_me, deep), (high_me, high)


def greet(groups):
    barrier = pltpu.get_barrier_semaphore()
    for me, peer in groups:

        def signal(step, carry, me=me, peer=peer):
            pl.semaphore_signal(
                barrier, inc=1, device_id=peer((me + step) % GROUP), device_id_type=MESH
            )
            return carry

        lax.fori_loop(1, GROUP, signal, 0)
    pl.semaphore_wait(barrier, len(groups) * (GROUP - 1))


def exchange(group, streams, send_sem, recv_sem):
    me, peer = group

    def copy(step, index):
        source, target = streams[index]
        member = (me + step) % GROUP
        return pltpu.make_async_remote_copy(
            src_ref=source(member),
            dst_ref=target,
            send_sem=send_sem.at[index, step],
            recv_sem=recv_sem.at[index, step],
            device_id=peer(member),
            device_id_type=MESH,
        )

    def start(step, carry):
        for index in range(len(streams)):
            copy(step, index).start()
        return carry

    def finish(step, carry):
        for index in range(len(streams)):
            copy(step, index).wait()
        return carry

    lax.fori_loop(1, GROUP, start, 0)
    lax.fori_loop(1, GROUP, finish, 0)


def reduce_kernel(
    part_ref, mass_ref, sum_ref, total_ref,
    rows, tiles, highs, deeps, blocks, mass_plane, mass_deep, mass_high,
    send_sem, recv_sem,
):
    plane, deep, high = place()
    greet((plane, deep, high))
    plane_me, deep_me, high_me = plane[0], deep[0], high[0]

    exchange(
        plane,
        (
            (lambda m: part_ref.at[pl.ds(pl.multiple_of(m * 32, 32), 32)], rows.at[plane_me]),
            (lambda m: mass_ref, mass_plane.at[plane_me]),
        ),
        send_sem.at[0], recv_sem.at[0],
    )
    rows[plane_me] = part_ref[pl.ds(pl.multiple_of(plane_me * 32, 32), 32)]
    mass_plane[plane_me] = mass_ref[...]
    mine = jnp.sum(rows[...], axis=0)
    for tile in range(GROUP):
        r, h = tile // 2, tile % 2
        tiles[tile] = mine[r * 8 : r * 8 + 8, h * 128 : h * 128 + 128]
    total_ref[...] = jnp.sum(mass_plane[...], axis=0)

    exchange(
        deep,
        (
            (lambda m: tiles.at[m], deeps.at[deep_me]),
            (lambda m: total_ref, mass_deep.at[deep_me]),
        ),
        send_sem.at[1], recv_sem.at[1],
    )
    deeps[deep_me] = tiles[deep_me]
    mass_deep[deep_me] = total_ref[...]
    highs[high_me] = jnp.sum(deeps[...], axis=0)
    mass_high[high_me] = jnp.sum(mass_deep[...], axis=0)

    exchange(
        high,
        (
            (lambda m: highs.at[high_me], highs.at[high_me]),
            (lambda m: mass_high.at[high_me], mass_high.at[high_me]),
        ),
        send_sem.at[2], recv_sem.at[2],
    )
    total_ref[...] = jnp.sum(mass_high[...], axis=0)
    blocks[deep_me] = jnp.sum(highs[...], axis=0)

    exchange(
        deep,
        ((lambda m: blocks.at[deep_me], blocks.at[deep_me]),),
        send_sem.at[3], recv_sem.at[3],
    )
    for tile in range(GROUP):
        r, h = tile // 2, tile % 2
        sum_ref[
            pl.ds(pl.multiple_of(plane_me * 32 + r * 8, 8), 8), h * 128 : h * 128 + 128
        ] = blocks[tile]
    own = sum_ref.at[pl.ds(pl.multiple_of(plane_me * 32, 32), 32)]
    exchange(plane, ((lambda m: own, own),), send_sem.at[4], recv_sem.at[4])


def reduce_all(part, mass):
    tile = (8, 128)
    return pl.pallas_call(
        reduce_kernel,
        out_shape=(
            jax.ShapeDtypeStruct((NBLK, NBLK), jnp.float32),
            jax.ShapeDtypeStruct(tile, jnp.float32),
        ),
        in_specs=[pl.BlockSpec(memory_space=VMEM)] * 2,
        out_specs=(pl.BlockSpec(memory_space=VMEM), pl.BlockSpec(memory_space=VMEM)),
        scratch_shapes=[
            pltpu.VMEM((GROUP, 32, NBLK), jnp.float32),
            pltpu.VMEM((GROUP, *tile), jnp.float32),
            pltpu.VMEM((GROUP, *tile), jnp.float32),
            pltpu.VMEM((GROUP, *tile), jnp.float32),
            pltpu.VMEM((GROUP, *tile), jnp.float32),
            pltpu.VMEM((GROUP, *tile), jnp.float32),
            pltpu.VMEM((GROUP, *tile), jnp.float32),
            pltpu.VMEM((GROUP, *tile), jnp.float32),
            pltpu.SemaphoreType.DMA((5, 2, GROUP)),
            pltpu.SemaphoreType.DMA((5, 2, GROUP)),
        ],
        compiler_params=pltpu.CompilerParams(collective_id=1, has_side_effects=True),
        name="reduce_all",
    )(part, mass)


def member_kernel(labels_ref, factor_ref, out_ref):
    count = labels_ref.shape[1]
    blocks = lax.broadcasted_iota(jnp.int32, (NBLK, count), 0).astype(jnp.float32)

    def body(row, carry):
        names = jnp.broadcast_to(labels_ref[pl.ds(row, 1), :], (NBLK, count))
        member = jnp.where(names == blocks, 1.0, 0.0).astype(jnp.bfloat16)
        out_ref[row] = lax.dot_general(
            factor_ref[...], member, (((1,), (1,)), ((), ())), preferred_element_type=jnp.float32
        ).astype(out_ref.dtype)
        return carry

    lax.fori_loop(0, labels_ref.shape[0], body, 0)


def member_product(labels, factor):
    return pl.pallas_call(
        member_kernel,
        out_shape=jax.ShapeDtypeStruct((labels.shape[0], factor.shape[0], NBLK), jnp.bfloat16),
        in_specs=[pl.BlockSpec(memory_space=VMEM)] * 2,
        out_specs=pl.BlockSpec(memory_space=VMEM),
        compiler_params=pltpu.CompilerParams(vmem_limit_bytes=40 << 20),
        name="member_product",
    )(labels, factor)


def flow_kernel(labels_ref, weight_ref, factor_ref, first_ref, out_ref, wide, held):
    count = labels_ref.shape[1]
    depth = factor_ref.shape[0]
    blocks = lax.broadcasted_iota(jnp.int32, (NBLK, count), 0).astype(jnp.float32)

    def body(row, carry):
        names = jnp.broadcast_to(labels_ref[pl.ds(row, 1), :], (NBLK, count))
        member = jnp.where(names == blocks, 1.0, 0.0).astype(jnp.bfloat16)
        scaled = factor_ref[...] * weight_ref[pl.ds(row, 1), :]
        upper = scaled.astype(jnp.bfloat16)
        wide[0:depth, :] = upper
        wide[depth : 2 * depth, :] = (scaled - upper.astype(jnp.float32)).astype(jnp.bfloat16)
        both = lax.dot_general(
            wide[...], member, (((1,), (1,)), ((), ())), preferred_element_type=jnp.float32
        )
        held[:, pl.ds(row, 1), :] = (both[0:depth] + both[depth:]).reshape(depth, 1, NBLK)
        return carry

    lax.fori_loop(0, labels_ref.shape[0], body, 0)
    rows = held.shape[0] * held.shape[1]
    mine = held[...].reshape(rows, NBLK)
    first = first_ref[...].reshape(rows, NBLK)
    upper = mine.astype(jnp.bfloat16)
    lower = (mine - upper.astype(jnp.float32)).astype(jnp.bfloat16)
    dims = (((0,), (0,)), ((), ()))
    out_ref[...] = lax.dot_general(
        upper, first, dims, preferred_element_type=jnp.float32
    ) + lax.dot_general(lower, first, dims, preferred_element_type=jnp.float32)


def flow_product(labels, weight, factor, first):
    depth, count = factor.shape
    return pl.pallas_call(
        flow_kernel,
        out_shape=jax.ShapeDtypeStruct((NBLK, NBLK), jnp.float32),
        in_specs=[pl.BlockSpec(memory_space=VMEM)] * 4,
        out_specs=pl.BlockSpec(memory_space=VMEM),
        scratch_shapes=[
            pltpu.VMEM((2 * depth, count), jnp.bfloat16),
            pltpu.VMEM((depth, labels.shape[0], NBLK), jnp.float32),
        ],
        compiler_params=pltpu.CompilerParams(vmem_limit_bytes=40 << 20),
        name="flow_product",
    )(labels, weight, factor, first)


def balance_kernel(numer_ref, mass_ref, out_ref, power):
    size = NBLK
    power[...] = numer_ref[...] / mass_ref[...] - 1.0 / size
    start = jnp.full((8, size), 1.0 / size, jnp.float32)

    def going(state):
        turn, height, row = state
        return jnp.logical_and(turn < 40, height > 1e-10)

    def turn_once(state):
        turn, height, row = state
        now = power[...]
        row = row + jnp.dot(row, now, precision=HIGHEST, preferred_element_type=jnp.float32)
        after = jnp.dot(now, now, precision=HIGHEST, preferred_element_type=jnp.float32)
        power[...] = after
        return turn + 1, jnp.max(jnp.abs(after)), row

    state = (jnp.int32(0), jnp.max(jnp.abs(power[...])), start)
    out_ref[...] = lax.while_loop(going, turn_once, state)[2]


def balance_of(numer, mass):
    return pl.pallas_call(
        balance_kernel,
        out_shape=jax.ShapeDtypeStruct((8, NBLK), jnp.float32),
        in_specs=[pl.BlockSpec(memory_space=VMEM)] * 2,
        out_specs=pl.BlockSpec(memory_space=VMEM),
        scratch_shapes=[pltpu.VMEM((NBLK, NBLK), jnp.float32)],
        name="balance",
    )(numer, mass)[0]


def spread_small(own, wide, stages, send_sem, recv_sem):
    (outer_me, outer_size, outer_peer), (inner_me, inner_size, inner_peer) = stages

    def stage(which, me, size, peer, piece):
        def copy(step):
            return pltpu.make_async_remote_copy(
                src_ref=piece,
                dst_ref=piece,
                send_sem=send_sem.at[which, step],
                recv_sem=recv_sem.at[which, step],
                device_id=peer((me + step) % size),
                device_id_type=MESH,
            )

        def start(step, carry):
            copy(step).start()
            return carry

        def finish(step, carry):
            copy(step).wait()
            return carry

        return start, finish, size

    wide[inner_me, outer_me] = own
    first = stage(0, outer_me, outer_size, outer_peer, wide.at[inner_me, outer_me])
    second = stage(1, inner_me, inner_size, inner_peer, wide.at[inner_me])
    return first, second


def run_loop(part):
    start, finish, size = part
    lax.fori_loop(1, size, start, 0)
    lax.fori_loop(1, size, finish, 0)


def greet_each(peers):
    barrier = pltpu.get_barrier_semaphore()
    count = 0
    for me, size, peer in peers:

        def signal(step, carry, me=me, size=size, peer=peer):
            pl.semaphore_signal(
                barrier, inc=1, device_id=peer((me + step) % size), device_id_type=MESH
            )
            return carry

        lax.fori_loop(1, size, signal, 0)
        count += size - 1
    pl.semaphore_wait(barrier, count)


def shelf_stages():
    ctrl = lax.axis_index("ctrl")
    shelf = lax.axis_index("shelf")
    return (
        (shelf // 4, 8, lambda m: (ctrl, m * 4 + shelf % 4)),
        (shelf % 4, 4, lambda m: (ctrl, shelf - shelf % 4 + m)),
    )


def ctrl_stages():
    ctrl = lax.axis_index("ctrl")
    shelf = lax.axis_index("shelf")
    return (
        (ctrl // 2, 8, lambda m: (m * 2 + ctrl % 2, shelf)),
        (ctrl % 2, 2, lambda m: (ctrl - ctrl % 2 + m, shelf)),
    )


def weight_kernel(own_ref, wide_ref, send_sem, recv_sem):
    stages = shelf_stages()
    greet_each(stages)
    first, second = spread_small(own_ref[...], wide_ref, stages, send_sem, recv_sem)
    run_loop(first)
    run_loop(second)


def gather_weight(own):
    return pl.pallas_call(
        weight_kernel,
        out_shape=jax.ShapeDtypeStruct((4, 8, 16, 128), jnp.float32),
        in_specs=[pl.BlockSpec(memory_space=VMEM)],
        out_specs=pl.BlockSpec(memory_space=VMEM),
        scratch_shapes=[pltpu.SemaphoreType.DMA((2, 8)), pltpu.SemaphoreType.DMA((2, 8))],
        compiler_params=pltpu.CompilerParams(collective_id=2, has_side_effects=True),
        name="gather_weight",
    )(own)


def rows_kernel(
    ctrl_ref, shelf_ref, label_ref, ctrl_all, shelf_all, by_shelf, by_ctrl,
    swap_send, swap_recv, ring_send, ring_recv, pair_send, pair_recv,
    send_a, recv_a, send_b, recv_b,
):
    ctrl = lax.axis_index("ctrl")
    shelf = lax.axis_index("shelf")
    deep, side, core = shelf // 4, (shelf // 2) % 2, shelf % 2
    stages_a, stages_b = shelf_stages(), ctrl_stages()
    greet_each(stages_a + stages_b)

    wides = (ctrl_all, shelf_all)
    ctrl_all[deep, side, core] = ctrl_ref[...]
    shelf_all[deep, side, core] = shelf_ref[...]

    def remote(piece, send_sem, recv_sem, target):
        return pltpu.make_async_remote_copy(
            src_ref=piece, dst_ref=piece, send_sem=send_sem, recv_sem=recv_sem,
            device_id=(ctrl, target), device_id_type=MESH,
        )

    across = shelf + 2 - 4 * side
    swaps = [
        remote(wide.at[deep, side, core], swap_send.at[n], swap_recv.at[n], across)
        for n, wide in enumerate(wides)
    ]
    for swap in swaps:
        swap.start()
    label_a = spread_small(label_ref[...], by_shelf, stages_a, send_a, recv_a)
    label_b = spread_small(label_ref[...], by_ctrl, stages_b, send_b, recv_b)
    run_loop(label_a[0])
    run_loop(label_b[0])
    for swap in swaps:
        swap.wait()

    right = ((deep + 1) % 8) * 4 + shelf % 4
    left = ((deep + 7) % 8) * 4 + shelf % 4
    sibling = shelf + 1 - 2 * core

    def pair(n, block):
        return remote(wides[n].at[block, :, core], pair_send.at[n, block], pair_recv.at[n, block], sibling)

    def hop(n, way, count):
        block = (deep + 8 - count + 1) % 8 if way == 0 else (deep + count - 1) % 8
        return remote(
            wides[n].at[block, :, core],
            ring_send.at[n, way, count - 1],
            ring_recv.at[n, way, count - 1],
            right if way == 0 else left,
        )

    def used(n, way, count):
        return count < 4 or n == way

    for n in range(2):
        for way in range(2):
            hop(n, way, 1).start()
        pair(n, deep).start()
    for count in range(1, 5):
        for n in range(2):
            for way in range(2):
                if not used(n, way, count):
                    continue
                hop(n, way, count).wait_recv()
                if count < 4 and used(n, way, count + 1):
                    hop(n, way, count + 1).start()
                pair(n, (deep + 8 - count) % 8 if way == 0 else (deep + count) % 8).start()
    run_loop(label_a[1])
    run_loop(label_b[1])
    for count in range(1, 5):
        for n in range(2):
            for way in range(2):
                if used(n, way, count):
                    hop(n, way, count).wait_send()
    for block in range(8):
        for n in range(2):
            pltpu.make_async_remote_copy(
                src_ref=wides[n].at[block, :, core],
                dst_ref=wides[n].at[block, :, 1 - core],
                send_sem=pair_send.at[n, block], recv_sem=pair_recv.at[n, block],
                device_id=(ctrl, sibling), device_id_type=MESH,
            ).wait()


def gather_rows(ctrl_rows, shelf_rows, label_tile):
    return pl.pallas_call(
        rows_kernel,
        out_shape=(
            jax.ShapeDtypeStruct((8, 2, 2, *ctrl_rows.shape), jnp.bfloat16),
            jax.ShapeDtypeStruct((8, 2, 2, *shelf_rows.shape), jnp.bfloat16),
            jax.ShapeDtypeStruct((4, 8, 16, 128), jnp.float32),
            jax.ShapeDtypeStruct((2, 8, 16, 128), jnp.float32),
        ),
        in_specs=[pl.BlockSpec(memory_space=VMEM)] * 3,
        out_specs=tuple([pl.BlockSpec(memory_space=VMEM)] * 4),
        scratch_shapes=[
            pltpu.SemaphoreType.DMA((2,)),
            pltpu.SemaphoreType.DMA((2,)),
            pltpu.SemaphoreType.DMA((2, 2, 4)),
            pltpu.SemaphoreType.DMA((2, 2, 4)),
            pltpu.SemaphoreType.DMA((2, 8)),
            pltpu.SemaphoreType.DMA((2, 8)),
            pltpu.SemaphoreType.DMA((2, 8)),
            pltpu.SemaphoreType.DMA((2, 8)),
            pltpu.SemaphoreType.DMA((2, 8)),
            pltpu.SemaphoreType.DMA((2, 8)),
        ],
        compiler_params=pltpu.CompilerParams(
            collective_id=3, has_side_effects=True, vmem_limit_bytes=32 << 20
        ),
        name="gather_rows",
    )(ctrl_rows, shelf_rows, label_tile)


def as_tile(values):
    return jnp.pad(values.reshape(12, 128), ((0, 4), (0, 0)))


def shelf_wide(tiles):
    kept = tiles[:, :, 0:12].reshape(4, 8, 48, 32)
    return jnp.transpose(kept, (2, 1, 0, 3)).reshape(48, SHELF)


def ctrl_wide(tiles):
    kept = tiles[:, :, 0:12].reshape(2, 8, 48, 32)
    return jnp.transpose(kept, (3, 1, 0, 2)).reshape(32, CTRL)


def steps_kernel(
    prob_ref, ctrl_ref, shelf_ref, disk_ref, rate_ref, shelf_rate_ref, scale_ref, state_ref,
    home_y, home_z, at_y, made_y, at_z, made_z, back_y, back_z,
    send_sem, recv_sem,
):
    ctrl = lax.axis_index("ctrl")
    shelf = lax.axis_index("shelf")
    chip, core = shelf // 2, shelf % 2
    ctrls, shelves = 16, 32
    chips = shelves // 2
    rows_c, rows_s = state_ref.shape[0], state_ref.shape[1]
    per_y, per_z = rows_s // ctrls, rows_c // chips
    lanes = 128

    barrier = pltpu.get_barrier_semaphore()

    def signal_y(step, carry):
        target = ((ctrl + step) % ctrls, shelf)
        pl.semaphore_signal(barrier, inc=1, device_id=target, device_id_type=MESH)
        return carry

    def signal_z(step, carry):
        target = (ctrl, (shelf + step) % shelves)
        pl.semaphore_signal(barrier, inc=1, device_id=target, device_id_type=MESH)
        return carry

    lax.fori_loop(1, ctrls, signal_y, 0)
    lax.fori_loop(1, shelves, signal_z, 0)
    state_ref[...] = prob_ref[...]

    order = lax.broadcasted_iota(jnp.int32, (256, 256), 0)
    other = lax.broadcasted_iota(jnp.int32, (256, 256), 1)
    swap = jnp.where(
        jnp.logical_and(order // 16 == other % 16, order % 16 == other // 16), 1.0, 0.0
    ).astype(jnp.bfloat16)
    pl.semaphore_wait(barrier, ctrls - 1 + shelves - 1)

    def swapped(block):
        flat = jnp.dot(swap, block.reshape(256, lanes), preferred_element_type=jnp.float32)
        return flat.astype(jnp.bfloat16).reshape(16, 16, lanes)

    def exchange_rows(source, target):
        first, second = source.shape[0], source.shape[1]
        for p in range(0, first, 16):
            for q in range(0, second, 16):
                target[q : q + 16, p : p + 16, :] = swapped(source[p : p + 16, q : q + 16, :])

    def part_c(ref, owner):
        return ref.at[:, pl.ds(pl.multiple_of(owner * rows_c, 16), rows_c), :]

    def part_s(ref, owner):
        return ref.at[:, pl.ds(pl.multiple_of(owner * rows_s, 16), rows_s), :]

    def remote(source, target, stream, mine, theirs, device):
        return pltpu.make_async_remote_copy(
            src_ref=source, dst_ref=target,
            send_sem=send_sem.at[stream, theirs], recv_sem=recv_sem.at[stream, mine],
            device_id=device, device_id_type=MESH,
        )

    def each(count, first, act):
        def body(step, carry):
            act((first + step) % count)
            return carry

        lax.fori_loop(1, count, body, 0)

    def y_forward(half):
        def act(peer):
            remote(
                home_y.at[half, pl.ds(peer * per_y, per_y)], part_c(at_y.at[half], ctrl),
                4 * half, ctrl, peer, (peer, shelf),
            ).start()

        each(ctrls, ctrl, act)
        part_c(at_y.at[half], ctrl)[...] = home_y[half, pl.ds(ctrl * per_y, per_y)]

    def y_forward_wait(half):
        def act(peer):
            remote(
                home_y.at[half, pl.ds(peer * per_y, per_y)], part_c(at_y.at[half], peer),
                4 * half, peer, peer, (peer, shelf),
            ).wait()

        each(ctrls, ctrl, act)

    def y_product(half):
        both = jnp.concatenate([at_y[half, n] for n in range(per_y)], axis=1)
        for m in range(0, ctrls * rows_c, 256):
            made = jnp.dot(ctrl_ref[m : m + 256], both, preferred_element_type=jnp.float32)
            for n in range(per_y):
                made_y[half, n, m : m + 256, :] = made[:, n * lanes : (n + 1) * lanes].astype(
                    jnp.bfloat16
                )

    def y_back(half):
        def act(peer):
            remote(
                part_c(made_y.at[half], peer), back_y.at[half, pl.ds(ctrl * per_y, per_y)],
                4 * half + 1, ctrl, peer, (peer, shelf),
            ).start()

        each(ctrls, ctrl, act)
        back_y[half, pl.ds(ctrl * per_y, per_y)] = part_c(made_y.at[half], ctrl)[...]

    def y_back_wait(half):
        def act(peer):
            remote(
                part_c(made_y.at[half], peer), back_y.at[half, pl.ds(peer * per_y, per_y)],
                4 * half + 1, peer, peer, (peer, shelf),
            ).wait()

        each(ctrls, ctrl, act)

    def z_forward_copy(half, to):
        return remote(
            home_z.at[half, pl.ds(to * per_z, per_z)], part_s(at_z, shelf),
            4 * half + 2, shelf, to, (ctrl, 2 * to + half),
        )

    def z_forward(half):
        each(chips, chip, lambda to: z_forward_copy(half, to).start())

        @pl.when(core != half)
        def _():
            z_forward_copy(half, chip).start()

        @pl.when(core == half)
        def _():
            part_s(at_z, shelf)[...] = home_z[half, pl.ds(chip * per_z, per_z)]

    def z_forward_sent(half):
        each(chips, chip, lambda to: z_forward_copy(half, to).wait_send())

        @pl.when(core != half)
        def _():
            z_forward_copy(half, chip).wait_send()

    def z_middle(half):
        @pl.when(core == half)
        def _():
            def arrived(peer):
                remote(
                    home_z.at[half, pl.ds(0, per_z)], part_s(at_z, peer),
                    4 * half + 2, peer, 0, (ctrl, peer),
                ).wait_recv()

            each(shelves, shelf, arrived)
            wide = jnp.concatenate([at_z[n] for n in range(per_z)], axis=1)
            for m in range(0, shelves * rows_s, 256):
                made = jnp.dot(shelf_ref[m : m + 256], wide, preferred_element_type=jnp.float32)
                for n in range(per_z):
                    made_z[n, m : m + 256, :] = made[:, n * lanes : (n + 1) * lanes].astype(
                        jnp.bfloat16
                    )

            def act(peer):
                remote(
                    part_s(made_z, peer), back_z.at[half, pl.ds(chip * per_z, per_z)],
                    4 * half + 3, chip, peer, (ctrl, peer),
                ).start()

            each(shelves, shelf, act)
            back_z[half, pl.ds(chip * per_z, per_z)] = part_s(made_z, shelf)[...]

    def z_back_from(half, source):
        return remote(
            part_s(made_z, shelf), back_z.at[half, pl.ds(source * per_z, per_z)],
            4 * half + 3, source, 0, (ctrl, 2 * source + half),
        )

    def z_back_wait(half):
        each(chips, chip, lambda source: z_back_from(half, source).wait_recv())

        @pl.when(core != half)
        def _():
            z_back_from(half, chip).wait_recv()

    def z_back_sent(half):
        @pl.when(core == half)
        def _():
            def act(peer):
                remote(
                    part_s(made_z, peer), back_z.at[half, pl.ds(chip * per_z, per_z)],
                    4 * half + 3, chip, peer, (ctrl, peer),
                ).wait_send()

            each(shelves, shelf, act)

    def one_step(repeat, carry):
        for p in range(0, rows_c, 16):
            rounded = state_ref[p : p + 16].astype(jnp.bfloat16).reshape(16 * rows_s, 256)
            made = jnp.dot(rounded, disk_ref[...], preferred_element_type=jnp.float32)
            made = made.astype(jnp.bfloat16).reshape(16, rows_s, 256)
            home_z[1, p : p + 16] = made[:, :, lanes:]
            for q in range(0, rows_s, 16):
                home_y[0, q : q + 16, p : p + 16, :] = swapped(made[:, q : q + 16, :lanes])
        z_forward(1)
        y_forward(0)
        y_forward_wait(0)
        y_product(0)
        y_back(0)
        z_middle(1)
        y_back_wait(0)
        exchange_rows(back_y.at[0], home_z.at[0])
        z_forward(0)
        z_back_wait(1)
        exchange_rows(back_z.at[1], home_y.at[1])
        y_forward(1)
        z_middle(0)
        y_forward_wait(1)
        y_product(1)
        y_back(1)
        z_back_wait(0)
        y_back_wait(1)
        z_forward_sent(1)
        exchange_rows(back_y.at[1], home_z.at[1])

        def update(row, inner):
            kept = 1.0 - rate_ref[pl.ds(row, 1), :] * shelf_rate_ref[...]
            third = jnp.concatenate([back_z[0, row], home_z[1, row]], axis=1)
            state_ref[row] = third.astype(jnp.float32) * scale_ref[...] + state_ref[row] * kept
            return inner

        lax.fori_loop(0, rows_c, update, 0)
        z_forward_sent(0)
        z_back_sent(0)
        z_back_sent(1)
        return carry

    lax.fori_loop(0, STEPS, one_step, 0)


def power_steps(prob, ctrl_t, shelf_t, disk_bf, rate, shelf_rate, scale):
    rows_c, rows_s, _ = prob.shape
    bf = jnp.bfloat16
    return pl.pallas_call(
        steps_kernel,
        out_shape=jax.ShapeDtypeStruct(prob.shape, jnp.float32),
        in_specs=[pl.BlockSpec(memory_space=VMEM)] * 7,
        out_specs=pl.BlockSpec(memory_space=VMEM),
        scratch_shapes=[
            pltpu.VMEM((2, rows_s, rows_c, 128), bf),
            pltpu.VMEM((2, rows_c, rows_s, 128), bf),
            pltpu.VMEM((2, 2, CTRL, 128), bf),
            pltpu.VMEM((2, 2, CTRL, 128), bf),
            pltpu.VMEM((3, SHELF, 128), bf),
            pltpu.VMEM((3, SHELF, 128), bf),
            pltpu.VMEM((2, rows_s, rows_c, 128), bf),
            pltpu.VMEM((2, rows_c, rows_s, 128), bf),
            pltpu.SemaphoreType.DMA((8, 32)),
            pltpu.SemaphoreType.DMA((8, 32)),
        ],
        compiler_params=pltpu.CompilerParams(
            collective_id=4, has_side_effects=True, vmem_limit_bytes=48 << 20
        ),
        name="power_steps",
    )(prob, ctrl_t, shelf_t, disk_bf, rate, shelf_rate, scale)


def local(prob, ctrl_rates, shelf_rates, disk_rates, labels):
    ctrl_all, shelf_all, by_shelf, by_ctrl = gather_rows(
        ctrl_rates.astype(jnp.bfloat16),
        shelf_rates.astype(jnp.bfloat16),
        as_tile(labels.astype(jnp.float32)),
    )
    ctrl_bf = ctrl_all.reshape(CTRL, CTRL)
    shelf_bf = shelf_all.reshape(SHELF, SHELF)
    shelf_labels = shelf_wide(by_shelf)
    ctrl_labels = ctrl_wide(by_ctrl)
    disk_bf = disk_rates.astype(jnp.bfloat16)
    ctrl_out = jnp.sum(ctrl_bf.astype(jnp.float32), axis=1)
    shelf_out = jnp.sum(shelf_bf.astype(jnp.float32), axis=1)
    disk_out = jnp.sum(disk_bf.astype(jnp.float32), axis=1)
    uniform_rate = 1.05 * (jnp.max(ctrl_out) * jnp.max(shelf_out)) * jnp.max(disk_out)
    ctrl_rows = prob.shape[0]
    shelf_rows = prob.shape[1]
    ctrl_at = lax.axis_index("ctrl") * ctrl_rows
    shelf_at = lax.axis_index("shelf") * shelf_rows
    ctrl_loc = lax.dynamic_slice_in_dim(ctrl_out, ctrl_at, ctrl_rows)
    shelf_loc = lax.dynamic_slice_in_dim(shelf_out, shelf_at, shelf_rows)
    rate = ctrl_loc[:, None] * disk_out[None, :] / uniform_rate
    shelf_rate = jnp.broadcast_to(shelf_loc[:, None], (shelf_rows, DISK))
    iterate = power_steps(
        prob,
        ctrl_bf.T,
        shelf_bf.T,
        disk_bf,
        rate,
        shelf_rate,
        jnp.full((1, DISK), 1.0, jnp.float32) / uniform_rate,
    )

    first = member_product(ctrl_labels, lax.dynamic_slice_in_dim(ctrl_bf, ctrl_at, ctrl_rows))
    shelf_columns = lax.dynamic_slice_in_dim(shelf_bf, shelf_at, shelf_rows, axis=1)
    shelf_columns = shelf_columns.T.astype(jnp.float32)

    pair_mass = jnp.sum(iterate, axis=2)
    weighted = jnp.sum(iterate * disk_out, axis=2)
    pair_kept = pair_mass - weighted * (ctrl_loc[:, None] * shelf_loc[None, :] / uniform_rate)
    shelf_weight = shelf_wide(gather_weight(as_tile(weighted)))
    part = flow_product(shelf_labels, shelf_weight, shelf_columns, first) / uniform_rate
    pair_count = shelf_rows * ctrl_rows
    blocks = jnp.arange(NBLK, dtype=jnp.int32)
    member_table = (labels.reshape(pair_count)[:, None] == blocks[None, :]).astype(
        jnp.float32
    )
    terms = jnp.dot(
        jnp.stack([pair_mass.reshape(pair_count), pair_kept.reshape(pair_count)]),
        member_table,
        precision=HIGHEST,
    )
    identity = jnp.eye(NBLK, dtype=jnp.float32)
    part = part + identity * terms[1][:, None]
    mass_tile = jnp.zeros((8, 128), jnp.float32).at[0:2].set(terms[0].reshape(2, 128))
    numer, mass_sum = reduce_all(part, mass_tile)
    block_mass = mass_sum[0:2].reshape(NBLK)
    balance = balance_of(numer, jnp.broadcast_to(block_mass[:, None], (NBLK, NBLK)))
    ratio_share = balance / block_mass
    pair_share = jnp.dot(member_table, ratio_share, precision=HIGHEST).reshape(
        ctrl_rows, shelf_rows
    )
    refined = iterate * pair_share[:, :, None] * float(CTRL * SHELF * DISK)
    coarse = balance * NBLK
    return (refined, coarse)


def solution(mesh):
    placed = (P("ctrl", "shelf", None), P("shelf", None), P("shelf", None), P(), P("ctrl", "shelf"))
    return jax.shard_map(
        local,
        mesh=mesh,
        in_specs=placed,
        out_specs=(P("ctrl", "shelf", None), P()),
        check_vma=False,
    )
```

```python
import functools

import jax
import jax.numpy as jnp
from jax import lax
from jax.experimental import pallas as pl
from jax.experimental.pallas import tpu as pltpu
from jax.sharding import PartitionSpec as P

CTRL = 768
SHELF = 1024
DISK = 256
NBLK = 256
STEPS = 2
GROUP = 8
MESH = pl.DeviceIdType.MESH
VMEM = pltpu.MemorySpace.VMEM
HIGHEST = lax.Precision.HIGHEST


def place():
    ctrl = lax.axis_index("ctrl")
    shelf = lax.axis_index("shelf")
    plane_me = (ctrl % 2) * 4 + shelf % 4
    deep_me = shelf // 4
    high_me = ctrl // 2

    def plane(member):
        return (ctrl - ctrl % 2 + member // 4, shelf - shelf % 4 + member % 4)

    def deep(member):
        return (ctrl, member * 4 + shelf % 4)

    def high(member):
        return (member * 2 + ctrl % 2, shelf)

    return (plane_me, plane), (deep_me, deep), (high_me, high)


def greet(groups):
    barrier = pltpu.get_barrier_semaphore()
    for me, peer in groups:

        def signal(step, carry, me=me, peer=peer):
            pl.semaphore_signal(
                barrier, inc=1, device_id=peer((me + step) % GROUP), device_id_type=MESH
            )
            return carry

        lax.fori_loop(1, GROUP, signal, 0)
    pl.semaphore_wait(barrier, len(groups) * (GROUP - 1))


def exchange(group, streams, send_sem, recv_sem):
    me, peer = group

    def copy(step, index):
        source, target = streams[index]
        member = (me + step) % GROUP
        return pltpu.make_async_remote_copy(
            src_ref=source(member),
            dst_ref=target,
            send_sem=send_sem.at[index, step],
            recv_sem=recv_sem.at[index, step],
            device_id=peer(member),
            device_id_type=MESH,
        )

    def start(step, carry):
        for index in range(len(streams)):
            copy(step, index).start()
        return carry

    def finish(step, carry):
        for index in range(len(streams)):
            copy(step, index).wait()
        return carry

    lax.fori_loop(1, GROUP, start, 0)
    lax.fori_loop(1, GROUP, finish, 0)


def reduce_kernel(
    part_ref, mass_ref, sum_ref, total_ref,
    rows, tiles, highs, deeps, blocks, mass_plane, mass_deep, mass_high,
    send_sem, recv_sem,
):
    plane, deep, high = place()
    greet((plane, deep, high))
    plane_me, deep_me, high_me = plane[0], deep[0], high[0]

    exchange(
        plane,
        (
            (lambda m: part_ref.at[pl.ds(pl.multiple_of(m * 32, 32), 32)], rows.at[plane_me]),
            (lambda m: mass_ref, mass_plane.at[plane_me]),
        ),
        send_sem.at[0], recv_sem.at[0],
    )
    rows[plane_me] = part_ref[pl.ds(pl.multiple_of(plane_me * 32, 32), 32)]
    mass_plane[plane_me] = mass_ref[...]
    mine = jnp.sum(rows[...], axis=0)
    for tile in range(GROUP):
        r, h = tile // 2, tile % 2
        tiles[tile] = mine[r * 8 : r * 8 + 8, h * 128 : h * 128 + 128]
    total_ref[...] = jnp.sum(mass_plane[...], axis=0)

    exchange(
        deep,
        (
            (lambda m: tiles.at[m], deeps.at[deep_me]),
            (lambda m: total_ref, mass_deep.at[deep_me]),
        ),
        send_sem.at[1], recv_sem.at[1],
    )
    deeps[deep_me] = tiles[deep_me]
    mass_deep[deep_me] = total_ref[...]
    highs[high_me] = jnp.sum(deeps[...], axis=0)
    mass_high[high_me] = jnp.sum(mass_deep[...], axis=0)

    exchange(
        high,
        (
            (lambda m: highs.at[high_me], highs.at[high_me]),
            (lambda m: mass_high.at[high_me], mass_high.at[high_me]),
        ),
        send_sem.at[2], recv_sem.at[2],
    )
    total_ref[...] = jnp.sum(mass_high[...], axis=0)
    blocks[deep_me] = jnp.sum(highs[...], axis=0)

    exchange(
        deep,
        ((lambda m: blocks.at[deep_me], blocks.at[deep_me]),),
        send_sem.at[3], recv_sem.at[3],
    )
    for tile in range(GROUP):
        r, h = tile // 2, tile % 2
        sum_ref[
            pl.ds(pl.multiple_of(plane_me * 32 + r * 8, 8), 8), h * 128 : h * 128 + 128
        ] = blocks[tile]
    own = sum_ref.at[pl.ds(pl.multiple_of(plane_me * 32, 32), 32)]
    exchange(plane, ((lambda m: own, own),), send_sem.at[4], recv_sem.at[4])


def reduce_all(part, mass):
    tile = (8, 128)
    return pl.pallas_call(
        reduce_kernel,
        out_shape=(
            jax.ShapeDtypeStruct((NBLK, NBLK), jnp.float32),
            jax.ShapeDtypeStruct(tile, jnp.float32),
        ),
        in_specs=[pl.BlockSpec(memory_space=VMEM)] * 2,
        out_specs=(pl.BlockSpec(memory_space=VMEM), pl.BlockSpec(memory_space=VMEM)),
        scratch_shapes=[
            pltpu.VMEM((GROUP, 32, NBLK), jnp.float32),
            pltpu.VMEM((GROUP, *tile), jnp.float32),
            pltpu.VMEM((GROUP, *tile), jnp.float32),
            pltpu.VMEM((GROUP, *tile), jnp.float32),
            pltpu.VMEM((GROUP, *tile), jnp.float32),
            pltpu.VMEM((GROUP, *tile), jnp.float32),
            pltpu.VMEM((GROUP, *tile), jnp.float32),
            pltpu.VMEM((GROUP, *tile), jnp.float32),
            pltpu.SemaphoreType.DMA((5, 2, GROUP)),
            pltpu.SemaphoreType.DMA((5, 2, GROUP)),
        ],
        compiler_params=pltpu.CompilerParams(collective_id=1, has_side_effects=True),
        name="reduce_all",
    )(part, mass)


def flow_kernel(labels_ref, weight_ref, factor_ref, first_ref, out_ref, wide, held):
    count = labels_ref.shape[1]
    depth = factor_ref.shape[0]
    blocks = lax.broadcasted_iota(jnp.int32, (NBLK, count), 0).astype(jnp.float32)

    def body(row, carry):
        names = jnp.broadcast_to(labels_ref[pl.ds(row, 1), :], (NBLK, count))
        member = jnp.where(names == blocks, 1.0, 0.0).astype(jnp.bfloat16)
        scaled = factor_ref[...] * weight_ref[pl.ds(row, 1), :]
        upper = scaled.astype(jnp.bfloat16)
        wide[0:depth, :] = upper
        wide[depth : 2 * depth, :] = (scaled - upper.astype(jnp.float32)).astype(jnp.bfloat16)
        both = lax.dot_general(
            wide[...], member, (((1,), (1,)), ((), ())), preferred_element_type=jnp.float32
        )
        held[:, pl.ds(row, 1), :] = (both[0:depth] + both[depth:]).reshape(depth, 1, NBLK)
        return carry

    lax.fori_loop(0, labels_ref.shape[0], body, 0)
    rows = held.shape[0] * held.shape[1]
    mine = held[...].reshape(rows, NBLK)
    first = first_ref[...].reshape(rows, NBLK)
    upper = mine.astype(jnp.bfloat16)
    lower = (mine - upper.astype(jnp.float32)).astype(jnp.bfloat16)
    dims = (((0,), (0,)), ((), ()))
    out_ref[...] = lax.dot_general(
        upper, first, dims, preferred_element_type=jnp.float32
    ) + lax.dot_general(lower, first, dims, preferred_element_type=jnp.float32)


def flow_product(labels, weight, factor, first):
    depth, count = factor.shape
    return pl.pallas_call(
        flow_kernel,
        out_shape=jax.ShapeDtypeStruct((NBLK, NBLK), jnp.float32),
        in_specs=[pl.BlockSpec(memory_space=VMEM)] * 4,
        out_specs=pl.BlockSpec(memory_space=VMEM),
        scratch_shapes=[
            pltpu.VMEM((2 * depth, count), jnp.bfloat16),
            pltpu.VMEM((depth, labels.shape[0], NBLK), jnp.float32),
        ],
        compiler_params=pltpu.CompilerParams(vmem_limit_bytes=40 << 20),
        name="flow_product",
    )(labels, weight, factor, first)


def balance_kernel(numer_ref, mass_ref, out_ref, power):
    size = NBLK
    power[...] = numer_ref[...] / mass_ref[...] - 1.0 / size
    start = jnp.full((8, size), 1.0 / size, jnp.float32)

    def going(state):
        turn, height, row = state
        return jnp.logical_and(turn < 40, height > 1e-10)

    def turn_once(state):
        turn, height, row = state
        now = power[...]
        row = row + jnp.dot(row, now, precision=HIGHEST, preferred_element_type=jnp.float32)
        after = jnp.dot(now, now, precision=HIGHEST, preferred_element_type=jnp.float32)
        power[...] = after
        return turn + 1, jnp.max(jnp.abs(after)), row

    state = (jnp.int32(0), jnp.max(jnp.abs(power[...])), start)
    out_ref[...] = lax.while_loop(going, turn_once, state)[2]


def balance_of(numer, mass):
    return pl.pallas_call(
        balance_kernel,
        out_shape=jax.ShapeDtypeStruct((8, NBLK), jnp.float32),
        in_specs=[pl.BlockSpec(memory_space=VMEM)] * 2,
        out_specs=pl.BlockSpec(memory_space=VMEM),
        scratch_shapes=[pltpu.VMEM((NBLK, NBLK), jnp.float32)],
        name="balance",
    )(numer, mass)[0]


def spread_small(own, wide, stages, send_sem, recv_sem):
    (outer_me, outer_size, outer_peer), (inner_me, inner_size, inner_peer) = stages

    def stage(which, me, size, peer, piece):
        def copy(step):
            return pltpu.make_async_remote_copy(
                src_ref=piece,
                dst_ref=piece,
                send_sem=send_sem.at[which, step],
                recv_sem=recv_sem.at[which, step],
                device_id=peer((me + step) % size),
                device_id_type=MESH,
            )

        def start(step, carry):
            copy(step).start()
            return carry

        def finish(step, carry):
            copy(step).wait()
            return carry

        return start, finish, size

    wide[inner_me, outer_me] = own
    first = stage(0, outer_me, outer_size, outer_peer, wide.at[inner_me, outer_me])
    second = stage(1, inner_me, inner_size, inner_peer, wide.at[inner_me])
    return first, second


def run_loop(part):
    start, finish, size = part
    lax.fori_loop(1, size, start, 0)
    lax.fori_loop(1, size, finish, 0)


def greet_each(peers):
    barrier = pltpu.get_barrier_semaphore()
    count = 0
    for me, size, peer in peers:

        def signal(step, carry, me=me, size=size, peer=peer):
            pl.semaphore_signal(
                barrier, inc=1, device_id=peer((me + step) % size), device_id_type=MESH
            )
            return carry

        lax.fori_loop(1, size, signal, 0)
        count += size - 1
    pl.semaphore_wait(barrier, count)


def shelf_stages():
    ctrl = lax.axis_index("ctrl")
    shelf = lax.axis_index("shelf")
    return (
        (shelf // 4, 8, lambda m: (ctrl, m * 4 + shelf % 4)),
        (shelf % 4, 4, lambda m: (ctrl, shelf - shelf % 4 + m)),
    )


def ctrl_stages():
    ctrl = lax.axis_index("ctrl")
    shelf = lax.axis_index("shelf")
    return (
        (ctrl // 2, 8, lambda m: (m * 2 + ctrl % 2, shelf)),
        (ctrl % 2, 2, lambda m: (ctrl - ctrl % 2 + m, shelf)),
    )


def weight_kernel(own_ref, wide_ref, send_sem, recv_sem):
    stages = shelf_stages()
    greet_each(stages)
    first, second = spread_small(own_ref[...], wide_ref, stages, send_sem, recv_sem)
    run_loop(first)
    run_loop(second)


def gather_weight(own):
    return pl.pallas_call(
        weight_kernel,
        out_shape=jax.ShapeDtypeStruct((4, 8, 16, 128), jnp.float32),
        in_specs=[pl.BlockSpec(memory_space=VMEM)],
        out_specs=pl.BlockSpec(memory_space=VMEM),
        scratch_shapes=[pltpu.SemaphoreType.DMA((2, 8)), pltpu.SemaphoreType.DMA((2, 8))],
        compiler_params=pltpu.CompilerParams(collective_id=2, has_side_effects=True),
        name="gather_weight",
    )(own)


def as_tile(values):
    return jnp.pad(values.reshape(12, 128), ((0, 4), (0, 0)))


def shelf_wide(tiles):
    kept = tiles[:, :, 0:12].reshape(4, 8, 48, 32)
    return jnp.transpose(kept, (2, 1, 0, 3)).reshape(48, SHELF)


def steps_kernel(
    prob_ref, ctrl_rows_ref, shelf_rows_ref, disk_in_ref, label_ref,
    state_ref, first_ref, shelf_labels_ref, shelf_cols_ref, weight_ref, mass_ref, out_c_ref, out_s_ref,
    base_ref,
    ctrl_all, shelf_all, by_shelf, by_ctrl, ctrl_wide, ctrl_own, ctrl_ref, shelf_ref, disk_ref,
    label_rows, shelf_wide_rows, ctrl_labels, rate_ref, shelf_rate_ref, scale_ref, disk_row,
    home_y, home_z, at_y, made_y, at_z, made_z, back_y, back_z,
    swap_send, swap_recv, ring_send, ring_recv, pair_send, pair_recv,
    send_a, recv_a, send_b, recv_b, send_sem, recv_sem,
):
    ctrl = lax.axis_index("ctrl")
    shelf = lax.axis_index("shelf")
    chip, core = shelf // 2, shelf % 2
    ctrls, shelves = 16, 32
    chips = shelves // 2
    rows_c, rows_s = state_ref.shape[0], state_ref.shape[1]
    per_y, per_z = rows_s // ctrls, rows_c // chips
    lanes = 128

    barrier = pltpu.get_barrier_semaphore()

    def signal_y(step, carry):
        target = ((ctrl + step) % ctrls, shelf)
        pl.semaphore_signal(barrier, inc=1, device_id=target, device_id_type=MESH)
        return carry

    def signal_z(step, carry):
        target = (ctrl, (shelf + step) % shelves)
        pl.semaphore_signal(barrier, inc=1, device_id=target, device_id_type=MESH)
        return carry

    lax.fori_loop(1, ctrls, signal_y, 0)
    lax.fori_loop(1, shelves, signal_z, 0)
    state_ref[...] = prob_ref[...]
    disk_ref[...] = disk_in_ref[...].astype(jnp.bfloat16)
    deep, side = shelf // 4, (shelf // 2) % 2
    wides = (ctrl_all, shelf_all)
    ctrl_all[deep, side, core] = ctrl_rows_ref[...].astype(jnp.bfloat16)
    shelf_all[deep, side, core] = shelf_rows_ref[...].astype(jnp.bfloat16)
    label_a = spread_small(label_ref[...], by_shelf, shelf_stages(), send_a, recv_a)
    label_b = spread_small(label_ref[...], by_ctrl, ctrl_stages(), send_b, recv_b)

    order = lax.broadcasted_iota(jnp.int32, (256, 256), 0)
    other = lax.broadcasted_iota(jnp.int32, (256, 256), 1)
    swap = jnp.where(
        jnp.logical_and(order // 16 == other % 16, order % 16 == other // 16), 1.0, 0.0
    ).astype(jnp.bfloat16)
    pl.semaphore_wait(barrier, ctrls - 1 + shelves - 1)

    def along_shelf(piece, send, recv, target):
        return pltpu.make_async_remote_copy(
            src_ref=piece, dst_ref=piece, send_sem=send, recv_sem=recv,
            device_id=(ctrl, target), device_id_type=MESH,
        )

    swaps = [
        along_shelf(
            wide.at[deep, side, core], swap_send.at[n], swap_recv.at[n], shelf + 2 - 4 * side
        )
        for n, wide in enumerate(wides)
    ]
    for copy in swaps:
        copy.start()
    for start, _, size in (label_a[0], label_b[0]):
        lax.fori_loop(1, size, start, 0)

    right = ((deep + 1) % 8) * 4 + shelf % 4
    left = ((deep + 7) % 8) * 4 + shelf % 4
    sibling = shelf + 1 - 2 * core

    def pair(n, block, side_core):
        piece = wides[n].at[block, :, side_core]
        return along_shelf(piece, pair_send.at[n, block], pair_recv.at[n, block], sibling)

    def hop(n, way, count):
        block = (deep + 8 - count + 1) % 8 if way == 0 else (deep + count - 1) % 8
        return along_shelf(
            wides[n].at[block, :, core],
            ring_send.at[n, way, count - 1],
            ring_recv.at[n, way, count - 1],
            right if way == 0 else left,
        )

    def used(n, way, count):
        return count < 4 or n == way

    def gather_rows():
        for copy in swaps:
            copy.wait()
        for n in range(2):
            for way in range(2):
                hop(n, way, 1).start()
            pair(n, deep, core).start()
        for _, finish, size in (label_a[0], label_b[0]):
            lax.fori_loop(1, size, finish, 0)
        for start, _, size in (label_a[1], label_b[1]):
            lax.fori_loop(1, size, start, 0)
        for count in range(1, 5):
            for n in range(2):
                for way in range(2):
                    if not used(n, way, count):
                        continue
                    hop(n, way, count).wait_recv()
                    if count < 4 and used(n, way, count + 1):
                        hop(n, way, count + 1).start()
                    pair(n, (deep + 8 - count) % 8 if way == 0 else (deep + count) % 8, core).start()
        for _, finish, size in (label_a[1], label_b[1]):
            lax.fori_loop(1, size, finish, 0)
        for count in range(1, 5):
            for n in range(2):
                for way in range(2):
                    if used(n, way, count):
                        hop(n, way, count).wait_send()

        def settle(block, carry):
            for n in range(2):
                pair(n, block, 1 - core).wait_recv()
                pair(n, block, core).wait_send()
            return carry

        lax.fori_loop(0, 8, settle, 0)

    def prepare():
        unit = jnp.where(order == other, 1.0, 0.0).astype(jnp.bfloat16)
        dims = (((1,), (1,)), ((), ()))
        for n in range(shelves):
            wide = ctrl_all[n // 4, (n // 2) % 2, n % 2].astype(jnp.float32)
            ctrl_wide[n * 24 : n * 24 + 24] = wide
        for m in range(0, CTRL, 256):
            block = ctrl_wide[:, m : m + 256].astype(jnp.bfloat16)
            turned = lax.dot_general(unit, block, dims, preferred_element_type=jnp.float32)
            ctrl_ref[m : m + 256] = turned.astype(jnp.bfloat16)
        shelf_sum = jnp.zeros((SHELF, 1), jnp.float32)
        for m in range(0, SHELF, 256):
            block = shelf_all[:, :, :, :, m : m + 256].reshape(SHELF, 256)
            turned = lax.dot_general(unit, block, dims, preferred_element_type=jnp.float32)
            shelf_ref[m : m + 256] = turned.astype(jnp.bfloat16)
            shelf_sum += jnp.sum(block.astype(jnp.float32), axis=1, keepdims=True)
        shelf_cols_ref[...] = shelf_ref[
            pl.ds(pl.multiple_of(shelf * rows_s, 16), rows_s)
        ].astype(jnp.float32)

        ctrl_max = jnp.max(
            jnp.sum(ctrl_wide[...], axis=1, keepdims=True), axis=0, keepdims=True
        )
        shelf_max = jnp.max(shelf_sum, axis=0, keepdims=True)
        ones = jnp.ones((8, 256), jnp.bfloat16)
        disk_sum = lax.dot_general(ones, disk_ref[...], dims, preferred_element_type=jnp.float32)
        disk_max = jnp.max(disk_sum[0:1], axis=1, keepdims=True)
        base = 1.05 * (ctrl_max * shelf_max) * disk_max
        own_rows = ctrl_wide[pl.ds(pl.multiple_of(ctrl * rows_c, 8), rows_c)]
        ctrl_own[...] = own_rows.astype(jnp.bfloat16)
        own_c = jnp.sum(own_rows, axis=1, keepdims=True)
        own_s = jnp.sum(
            shelf_rows_ref[...].astype(jnp.bfloat16).astype(jnp.float32), axis=1, keepdims=True
        )
        rate_ref[...] = own_c * disk_sum[0:1] / base
        shelf_rate_ref[...] = jnp.broadcast_to(own_s, (rows_s, 256))
        scale_ref[...] = jnp.broadcast_to(1.0 / base, (8, 256))
        disk_row[...] = disk_sum
        base_ref[...] = jnp.broadcast_to(base, (8, lanes))
        out_c_ref[...] = jnp.broadcast_to(own_c, (rows_c, lanes))
        out_s_ref[...] = jnp.broadcast_to(own_s, (rows_s, lanes))

        spread_pairs(by_shelf, shelf_wide_rows)
        for z in range(8):
            shelf_labels_ref[:, z * lanes : (z + 1) * lanes] = shelf_wide_rows[z, 0:rows_c]
        for i in range(ctrls):
            tile = by_ctrl[i % 2, i // 2]
            for q in range(4):
                moved = tile if q == 0 else pltpu.roll(tile, lanes - 32 * q, 1)
                label_rows[i, pl.ds(q, 16, stride=4), :] = moved
        turned = jnp.transpose(label_rows[:, 0:rows_c, :].reshape(CTRL, lanes))
        ctrl_labels[...] = turned[0:rows_s]

    names = lax.broadcasted_iota(jnp.int32, (NBLK, CTRL), 0).astype(jnp.float32)

    def fill(slot):
        part = rows_s // 8

        def body(row, carry):
            have = jnp.broadcast_to(ctrl_labels[pl.ds(row, 1), :], (NBLK, CTRL))
            member = jnp.where(have == names, 1.0, 0.0).astype(jnp.bfloat16)
            first_ref[row] = lax.dot_general(
                ctrl_own[...], member, (((1,), (1,)), ((), ())), preferred_element_type=jnp.float32
            ).astype(first_ref.dtype)
            return carry

        lax.fori_loop(slot * part, slot * part + part, body, 0)

    def swapped(block):
        flat = jnp.dot(swap, block.reshape(256, lanes), preferred_element_type=jnp.float32)
        return flat.astype(jnp.bfloat16).reshape(16, 16, lanes)

    def exchange_rows(source, target):
        first, second = source.shape[0], source.shape[1]
        for p in range(0, first, 16):
            for q in range(0, second, 16):
                target[q : q + 16, p : p + 16, :] = swapped(source[p : p + 16, q : q + 16, :])

    def part_c(ref, owner):
        return ref.at[:, pl.ds(pl.multiple_of(owner * rows_c, 16), rows_c), :]

    def part_s(ref, owner):
        return ref.at[:, pl.ds(pl.multiple_of(owner * rows_s, 16), rows_s), :]

    def remote(source, target, stream, mine, theirs, device):
        return pltpu.make_async_remote_copy(
            src_ref=source, dst_ref=target,
            send_sem=send_sem.at[stream, theirs], recv_sem=recv_sem.at[stream, mine],
            device_id=device, device_id_type=MESH,
        )

    def each(count, first, act):
        def body(step, carry):
            act((first + step) % count)
            return carry

        lax.fori_loop(1, count, body, 0)

    def y_forward(half):
        def act(peer):
            remote(
                home_y.at[half, pl.ds(peer * per_y, per_y)], part_c(at_y.at[half], ctrl),
                4 * half, ctrl, peer, (peer, shelf),
            ).start()

        each(ctrls, ctrl, act)
        part_c(at_y.at[half], ctrl)[...] = home_y[half, pl.ds(ctrl * per_y, per_y)]

    def y_forward_wait(half):
        def act(peer):
            remote(
                home_y.at[half, pl.ds(peer * per_y, per_y)], part_c(at_y.at[half], peer),
                4 * half, peer, peer, (peer, shelf),
            ).wait()

        each(ctrls, ctrl, act)

    def y_product(half):
        both = jnp.concatenate([at_y[half, n] for n in range(per_y)], axis=1)
        for m in range(0, ctrls * rows_c, 256):
            made = jnp.dot(ctrl_ref[m : m + 256], both, preferred_element_type=jnp.float32)
            for n in range(per_y):
                made_y[half, n, m : m + 256, :] = made[:, n * lanes : (n + 1) * lanes].astype(
                    jnp.bfloat16
                )

    def y_back(half):
        def act(peer):
            remote(
                part_c(made_y.at[half], peer), back_y.at[half, pl.ds(ctrl * per_y, per_y)],
                4 * half + 1, ctrl, peer, (peer, shelf),
            ).start()

        each(ctrls, ctrl, act)
        back_y[half, pl.ds(ctrl * per_y, per_y)] = part_c(made_y.at[half], ctrl)[...]

    def y_back_wait(half):
        def act(peer):
            remote(
                part_c(made_y.at[half], peer), back_y.at[half, pl.ds(peer * per_y, per_y)],
                4 * half + 1, peer, peer, (peer, shelf),
            ).wait()

        each(ctrls, ctrl, act)

    def z_forward_copy(half, to):
        return remote(
            home_z.at[half, pl.ds(to * per_z, per_z)], part_s(at_z, shelf),
            4 * half + 2, shelf, to, (ctrl, 2 * to + half),
        )

    def z_forward(half):
        each(chips, chip, lambda to: z_forward_copy(half, to).start())

        @pl.when(core != half)
        def _():
            z_forward_copy(half, chip).start()

        @pl.when(core == half)
        def _():
            part_s(at_z, shelf)[...] = home_z[half, pl.ds(chip * per_z, per_z)]

    def z_forward_sent(half):
        each(chips, chip, lambda to: z_forward_copy(half, to).wait_send())

        @pl.when(core != half)
        def _():
            z_forward_copy(half, chip).wait_send()

    def z_middle(half):
        @pl.when(core == half)
        def _():
            def arrived(peer):
                remote(
                    home_z.at[half, pl.ds(0, per_z)], part_s(at_z, peer),
                    4 * half + 2, peer, 0, (ctrl, peer),
                ).wait_recv()

            each(shelves, shelf, arrived)
            wide = jnp.concatenate([at_z[n] for n in range(per_z)], axis=1)
            for m in range(0, shelves * rows_s, 256):
                made = jnp.dot(shelf_ref[m : m + 256], wide, preferred_element_type=jnp.float32)
                for n in range(per_z):
                    made_z[n, m : m + 256, :] = made[:, n * lanes : (n + 1) * lanes].astype(
                        jnp.bfloat16
                    )

            def act(peer):
                remote(
                    part_s(made_z, peer), back_z.at[half, pl.ds(chip * per_z, per_z)],
                    4 * half + 3, chip, peer, (ctrl, peer),
                ).start()

            each(shelves, shelf, act)
            back_z[half, pl.ds(chip * per_z, per_z)] = part_s(made_z, shelf)[...]

    def z_back_from(half, source):
        return remote(
            part_s(made_z, shelf), back_z.at[half, pl.ds(source * per_z, per_z)],
            4 * half + 3, source, 0, (ctrl, 2 * source + half),
        )

    def z_back_wait(half):
        each(chips, chip, lambda source: z_back_from(half, source).wait_recv())

        @pl.when(core != half)
        def _():
            z_back_from(half, chip).wait_recv()

    def z_back_sent(half):
        @pl.when(core == half)
        def _():
            def act(peer):
                remote(
                    part_s(made_z, peer), back_z.at[half, pl.ds(chip * per_z, per_z)],
                    4 * half + 3, chip, peer, (ctrl, peer),
                ).wait_send()

            each(shelves, shelf, act)

    def one_step(repeat, carry):
        for p in range(0, rows_c, 16):
            rounded = state_ref[p : p + 16].astype(jnp.bfloat16).reshape(16 * rows_s, 256)
            made = jnp.dot(rounded, disk_ref[...], preferred_element_type=jnp.float32)
            made = made.astype(jnp.bfloat16).reshape(16, rows_s, 256)
            home_z[1, p : p + 16] = made[:, :, lanes:]
            for q in range(0, rows_s, 16):
                home_y[0, q : q + 16, p : p + 16, :] = swapped(made[:, q : q + 16, :lanes])
        z_forward(1)
        y_forward(0)

        @pl.when(repeat == 0)
        def _():
            gather_rows()
            prepare()

        fill(repeat * 4)
        y_forward_wait(0)
        y_product(0)
        y_back(0)
        z_middle(1)
        fill(repeat * 4 + 1)
        y_back_wait(0)
        exchange_rows(back_y.at[0], home_z.at[0])
        z_forward(0)
        z_back_wait(1)
        exchange_rows(back_z.at[1], home_y.at[1])
        y_forward(1)
        fill(repeat * 4 + 2)
        z_middle(0)
        y_forward_wait(1)
        y_product(1)
        y_back(1)
        fill(repeat * 4 + 3)
        z_back_wait(0)
        y_back_wait(1)
        z_forward_sent(1)
        exchange_rows(back_y.at[1], home_z.at[1])

        def update(row, inner):
            kept = 1.0 - rate_ref[pl.ds(row, 1), :] * shelf_rate_ref[...]
            third = jnp.concatenate([back_z[0, row], home_z[1, row]], axis=1)
            state_ref[row] = third.astype(jnp.float32) * scale_ref[0:1] + state_ref[row] * kept
            return inner

        lax.fori_loop(0, rows_c, update, 0)
        z_forward_sent(0)
        z_back_sent(0)
        z_back_sent(1)
        return carry

    lax.fori_loop(0, STEPS, one_step, 0)

    lead = lax.broadcasted_iota(jnp.int32, (8, 256), 0) == 0
    sums = jnp.where(lead, 1.0, disk_row[...])
    weight_ref[...] = jnp.zeros_like(weight_ref)
    mass_ref[...] = jnp.zeros_like(mass_ref)
    for r in range(rows_c // 4):
        both = lax.dot_general(
            sums,
            state_ref[4 * r : 4 * r + 4].reshape(4 * rows_s, 256),
            (((1,), (1,)), ((), ())),
            precision=HIGHEST,
            preferred_element_type=jnp.float32,
        )
        mass_ref[r : r + 1] = both[0:1]
        weight_ref[r : r + 1] = both[1:2]


def spread_pairs(tiles, wide):
    lane = lax.broadcasted_iota(jnp.int32, (16, 128), 1) // 32
    for z in range(8):
        for q in range(4):
            made = jnp.zeros((16, 128), jnp.float32)
            for p in range(4):
                tile = tiles[p, z]
                moved = tile if p == q else pltpu.roll(tile, (32 * (p - q)) % 128, 1)
                made = jnp.where(lane == p, moved, made)
            wide[z, pl.ds(q, 16, stride=4), :] = made


def power_steps(prob, ctrl_rows, shelf_rows, disk, label_tile):
    rows_c, rows_s, _ = prob.shape
    bf, f32 = jnp.bfloat16, jnp.float32
    outs = [
        (prob.shape, f32), ((rows_s, rows_c, NBLK), bf), ((rows_c, SHELF), f32), ((rows_s, SHELF), f32),
        ((16, 128), f32), ((16, 128), f32), ((rows_c, 128), f32), ((rows_s, 128), f32), ((8, 128), f32),
    ]
    dma = pltpu.SemaphoreType.DMA
    return pl.pallas_call(
        steps_kernel,
        out_shape=tuple(jax.ShapeDtypeStruct(*out) for out in outs),
        in_specs=[pl.BlockSpec(memory_space=VMEM)] * 5,
        out_specs=tuple([pl.BlockSpec(memory_space=VMEM)] * len(outs)),
        scratch_shapes=[
            pltpu.VMEM((8, 2, 2, 24, CTRL), bf),
            pltpu.VMEM((8, 2, 2, 32, SHELF), bf),
            pltpu.VMEM((4, 8, 16, 128), f32),
            pltpu.VMEM((2, 8, 16, 128), f32),
            pltpu.VMEM((CTRL, CTRL), f32),
            pltpu.VMEM((rows_c, CTRL), bf),
            pltpu.VMEM((CTRL, CTRL), bf),
            pltpu.VMEM((SHELF, SHELF), bf),
            pltpu.VMEM((DISK, DISK), bf),
            pltpu.VMEM((16, 64, 128), f32),
            pltpu.VMEM((8, 64, 128), f32),
            pltpu.VMEM((rows_s, CTRL), f32),
            pltpu.VMEM((rows_c, DISK), f32),
            pltpu.VMEM((rows_s, DISK), f32),
            pltpu.VMEM((8, DISK), f32),
            pltpu.VMEM((8, DISK), f32),
            pltpu.VMEM((2, rows_s, rows_c, 128), bf),
            pltpu.VMEM((2, rows_c, rows_s, 128), bf),
            pltpu.VMEM((2, 2, CTRL, 128), bf),
            pltpu.VMEM((2, 2, CTRL, 128), bf),
            pltpu.VMEM((3, SHELF, 128), bf),
            pltpu.VMEM((3, SHELF, 128), bf),
            pltpu.VMEM((2, rows_s, rows_c, 128), bf),
            pltpu.VMEM((2, rows_c, rows_s, 128), bf),
            dma((2,)), dma((2,)), dma((2, 2, 4)), dma((2, 2, 4)), dma((2, 8)), dma((2, 8)),
            dma((2, 8)), dma((2, 8)), dma((2, 8)), dma((2, 8)), dma((8, 32)), dma((8, 32)),
        ],
        compiler_params=pltpu.CompilerParams(
            collective_id=4, has_side_effects=True, vmem_limit_bytes=56 << 20
        ),
        name="power_steps",
    )(prob, ctrl_rows, shelf_rows, disk, label_tile)


def local(prob, ctrl_rates, shelf_rates, disk_rates, labels):
    ctrl_rows, shelf_rows = prob.shape[0], prob.shape[1]
    outs = power_steps(
        prob, ctrl_rates, shelf_rates, disk_rates, as_tile(labels.astype(jnp.float32))
    )
    iterate, first, shelf_labels, shelf_columns, weight_tile, mass_tile, out_c, out_s, base = outs
    uniform_rate = base[0, 0]
    pair_mass = mass_tile[0:12].reshape(ctrl_rows, shelf_rows)
    weighted = weight_tile[0:12].reshape(ctrl_rows, shelf_rows)
    pair_kept = pair_mass - weighted * (out_c[:, 0:1] * out_s[:, 0][None, :] / uniform_rate)
    shelf_weight = shelf_wide(gather_weight(weight_tile))
    part = flow_product(shelf_labels, shelf_weight, shelf_columns, first) / uniform_rate
    pair_count = shelf_rows * ctrl_rows
    blocks = jnp.arange(NBLK, dtype=jnp.int32)
    member_table = (labels.reshape(pair_count)[:, None] == blocks[None, :]).astype(
        jnp.float32
    )
    terms = jnp.dot(
        jnp.stack([pair_mass.reshape(pair_count), pair_kept.reshape(pair_count)]),
        member_table,
        precision=HIGHEST,
    )
    identity = jnp.eye(NBLK, dtype=jnp.float32)
    part = part + identity * terms[1][:, None]
    mass_tile = jnp.zeros((8, 128), jnp.float32).at[0:2].set(terms[0].reshape(2, 128))
    numer, mass_sum = reduce_all(part, mass_tile)
    block_mass = mass_sum[0:2].reshape(NBLK)
    balance = balance_of(numer, jnp.broadcast_to(block_mass[:, None], (NBLK, NBLK)))
    ratio_share = balance / block_mass
    pair_share = jnp.dot(member_table, ratio_share, precision=HIGHEST).reshape(
        ctrl_rows, shelf_rows
    )
    refined = iterate * pair_share[:, :, None] * float(CTRL * SHELF * DISK)
    coarse = balance * NBLK
    return (refined, coarse)


def solution(mesh):
    placed = (P("ctrl", "shelf", None), P("shelf", None), P("shelf", None), P(), P("ctrl", "shelf"))
    return jax.shard_map(
        local,
        mesh=mesh,
        in_specs=placed,
        out_specs=(P("ctrl", "shelf", None), P()),
        check_vma=False,
    )
```

```python
import functools

import jax
import jax.numpy as jnp
from jax import lax
from jax.experimental import pallas as pl
from jax.experimental.pallas import tpu as pltpu
from jax.sharding import PartitionSpec as P

CTRL = 768
SHELF = 1024
DISK = 256
NBLK = 256
STEPS = 2
GROUP = 8
MESH = pl.DeviceIdType.MESH
VMEM = pltpu.MemorySpace.VMEM
HIGHEST = lax.Precision.HIGHEST


def place():
    ctrl = lax.axis_index("ctrl")
    shelf = lax.axis_index("shelf")
    plane_me = (ctrl % 2) * 4 + shelf % 4
    deep_me = shelf // 4
    high_me = ctrl // 2

    def plane(member):
        return (ctrl - ctrl % 2 + member // 4, shelf - shelf % 4 + member % 4)

    def deep(member):
        return (ctrl, member * 4 + shelf % 4)

    def high(member):
        return (member * 2 + ctrl % 2, shelf)

    return (plane_me, plane), (deep_me, deep), (high_me, high)


def greet(groups):
    barrier = pltpu.get_barrier_semaphore()
    for me, peer in groups:

        def signal(step, carry, me=me, peer=peer):
            pl.semaphore_signal(
                barrier, inc=1, device_id=peer((me + step) % GROUP), device_id_type=MESH
            )
            return carry

        lax.fori_loop(1, GROUP, signal, 0)
    return barrier, len(groups) * (GROUP - 1)


def exchange(group, streams, send_sem, recv_sem):
    me, peer = group

    def copy(step, index):
        source, target = streams[index]
        member = (me + step) % GROUP
        return pltpu.make_async_remote_copy(
            src_ref=source(member),
            dst_ref=target,
            send_sem=send_sem.at[index, step],
            recv_sem=recv_sem.at[index, step],
            device_id=peer(member),
            device_id_type=MESH,
        )

    def start(step, carry):
        for index in range(len(streams)):
            copy(step, index).start()
        return carry

    def finish(step, carry):
        for index in range(len(streams)):
            copy(step, index).wait()
        return carry

    lax.fori_loop(1, GROUP, start, 0)
    lax.fori_loop(1, GROUP, finish, 0)


NT = (((1,), (1,)), ((), ()))


def flow_part(labels_ref, weight_ref, factor_ref, first_ref, out_ref, wide, held):
    count = labels_ref.shape[1]
    depth = factor_ref.shape[0]
    blocks = lax.broadcasted_iota(jnp.int32, (NBLK, count), 0).astype(jnp.float32)

    def body(row, carry):
        names = jnp.broadcast_to(labels_ref[pl.ds(row, 1), :], (NBLK, count))
        member = jnp.where(names == blocks, 1.0, 0.0).astype(jnp.bfloat16)
        scaled = factor_ref[...] * weight_ref[pl.ds(row, 1), :]
        upper = scaled.astype(jnp.bfloat16)
        slot = row % 2
        wide[slot, 0:depth, :] = upper
        wide[slot, depth : 2 * depth, :] = (scaled - upper.astype(jnp.float32)).astype(jnp.bfloat16)
        both = lax.dot_general(wide[slot], member, NT, preferred_element_type=jnp.float32)
        held[:, pl.ds(row, 1), :] = (both[0:depth] + both[depth:]).reshape(depth, 1, NBLK)
        return carry

    lax.fori_loop(0, labels_ref.shape[0], body, 0, unroll=2)
    rows = held.shape[0] * held.shape[1]
    mine = held[...].reshape(rows, NBLK)
    first = first_ref[...].reshape(rows, NBLK)
    upper = mine.astype(jnp.bfloat16)
    lower = (mine - upper.astype(jnp.float32)).astype(jnp.bfloat16)
    dims = (((0,), (0,)), ((), ()))
    out_ref[...] = lax.dot_general(
        upper, first, dims, preferred_element_type=jnp.float32
    ) + lax.dot_general(lower, first, dims, preferred_element_type=jnp.float32)


def block_terms(label_ref, pair_mass_ref, pair_kept_ref):
    line = lax.broadcasted_iota(jnp.int32, (8, 128), 0)
    names = lax.broadcasted_iota(jnp.int32, (NBLK, 128), 0).astype(jnp.float32)
    terms = jnp.zeros((8, NBLK), jnp.float32)
    for r in range(12):
        have = jnp.broadcast_to(label_ref[r : r + 1], (NBLK, 128))
        member = jnp.where(have == names, 1.0, 0.0)
        pair = jnp.where(line == 0, pair_mass_ref[r : r + 1], 0.0)
        pair = jnp.where(line == 1, pair_kept_ref[r : r + 1], pair)
        terms += lax.dot_general(
            pair, member, NT, precision=HIGHEST, preferred_element_type=jnp.float32
        )
    return terms


def reduce_kernel(
    labels_ref, weight_ref, factor_ref, first_ref, label_ref, pair_mass_ref, pair_kept_ref, base_ref,
    sum_ref, total_ref,
    part_ref, mass_ref, wide, held,
    rows, tiles, highs, deeps, blocks, mass_plane, mass_deep, mass_high,
    send_sem, recv_sem,
):
    plane, deep, high = place()
    barrier, greetings = greet((plane, deep, high))
    plane_me, deep_me, high_me = plane[0], deep[0], high[0]

    flow_part(labels_ref, weight_ref, factor_ref, first_ref, part_ref, wide, held)
    terms = block_terms(label_ref, pair_mass_ref, pair_kept_ref)
    mass_ref[...] = jnp.zeros_like(mass_ref)
    mass_ref[0:1] = terms[0:1, 0:128]
    mass_ref[1:2] = terms[0:1, 128:256]
    row = lax.broadcasted_iota(jnp.int32, (NBLK, NBLK), 0)
    column = lax.broadcasted_iota(jnp.int32, (NBLK, NBLK), 1)
    kept = jnp.where(row == column, jnp.broadcast_to(terms[1:2], (NBLK, NBLK)), 0.0)
    part_ref[...] = part_ref[...] / base_ref[0:1, 0:1] + kept
    pl.semaphore_wait(barrier, greetings)

    exchange(
        plane,
        (
            (lambda m: part_ref.at[pl.ds(pl.multiple_of(m * 32, 32), 32)], rows.at[plane_me]),
            (lambda m: mass_ref, mass_plane.at[plane_me]),
        ),
        send_sem.at[0], recv_sem.at[0],
    )
    rows[plane_me] = part_ref[pl.ds(pl.multiple_of(plane_me * 32, 32), 32)]
    mass_plane[plane_me] = mass_ref[...]
    mine = jnp.sum(rows[...], axis=0)
    for tile in range(GROUP):
        r, h = tile // 2, tile % 2
        tiles[tile] = mine[r * 8 : r * 8 + 8, h * 128 : h * 128 + 128]
    total_ref[...] = jnp.sum(mass_plane[...], axis=0)

    exchange(
        deep,
        (
            (lambda m: tiles.at[m], deeps.at[deep_me]),
            (lambda m: total_ref, mass_deep.at[deep_me]),
        ),
        send_sem.at[1], recv_sem.at[1],
    )
    deeps[deep_me] = tiles[deep_me]
    mass_deep[deep_me] = total_ref[...]
    highs[high_me] = jnp.sum(deeps[...], axis=0)
    mass_high[high_me] = jnp.sum(mass_deep[...], axis=0)

    exchange(
        high,
        (
            (lambda m: highs.at[high_me], highs.at[high_me]),
            (lambda m: mass_high.at[high_me], mass_high.at[high_me]),
        ),
        send_sem.at[2], recv_sem.at[2],
    )
    total_ref[...] = jnp.sum(mass_high[...], axis=0)
    blocks[deep_me] = jnp.sum(highs[...], axis=0)

    exchange(
        deep,
        ((lambda m: blocks.at[deep_me], blocks.at[deep_me]),),
        send_sem.at[3], recv_sem.at[3],
    )
    for tile in range(GROUP):
        r, h = tile // 2, tile % 2
        sum_ref[
            pl.ds(pl.multiple_of(plane_me * 32 + r * 8, 8), 8), h * 128 : h * 128 + 128
        ] = blocks[tile]
    own = sum_ref.at[pl.ds(pl.multiple_of(plane_me * 32, 32), 32)]
    exchange(plane, ((lambda m: own, own),), send_sem.at[4], recv_sem.at[4])


def reduce_all(labels, weight, factor, first, label_tile, mass_tile, kept_tile, base):
    tile = (8, 128)
    depth, count = factor.shape
    return pl.pallas_call(
        reduce_kernel,
        out_shape=(
            jax.ShapeDtypeStruct((NBLK, NBLK), jnp.float32),
            jax.ShapeDtypeStruct(tile, jnp.float32),
        ),
        in_specs=[pl.BlockSpec(memory_space=VMEM)] * 8,
        out_specs=(pl.BlockSpec(memory_space=VMEM), pl.BlockSpec(memory_space=VMEM)),
        scratch_shapes=[
            pltpu.VMEM((NBLK, NBLK), jnp.float32),
            pltpu.VMEM(tile, jnp.float32),
            pltpu.VMEM((2, 2 * depth, count), jnp.bfloat16),
            pltpu.VMEM((depth, labels.shape[0], NBLK), jnp.float32),
            pltpu.VMEM((GROUP, 32, NBLK), jnp.float32),
            pltpu.VMEM((GROUP, *tile), jnp.float32),
            pltpu.VMEM((GROUP, *tile), jnp.float32),
            pltpu.VMEM((GROUP, *tile), jnp.float32),
            pltpu.VMEM((GROUP, *tile), jnp.float32),
            pltpu.VMEM((GROUP, *tile), jnp.float32),
            pltpu.VMEM((GROUP, *tile), jnp.float32),
            pltpu.VMEM((GROUP, *tile), jnp.float32),
            pltpu.SemaphoreType.DMA((5, 2, GROUP)),
            pltpu.SemaphoreType.DMA((5, 2, GROUP)),
        ],
        compiler_params=pltpu.CompilerParams(
            collective_id=1, has_side_effects=True, vmem_limit_bytes=40 << 20
        ),
        name="reduce_all",
    )(labels, weight, factor, first, label_tile, mass_tile, kept_tile, base)


def balance_kernel(numer_ref, total_ref, label_ref, state_ref, refined_ref, coarse_ref, power, spread):
    size = NBLK
    line = lax.broadcasted_iota(jnp.int32, (size, size), 0)
    column = lax.broadcasted_iota(jnp.int32, (size, size), 1)
    mass = jnp.concatenate([total_ref[0:1], total_ref[1:2]], axis=1)
    mass_column = jnp.sum(
        jnp.where(line == column, jnp.broadcast_to(mass, (size, size)), 0.0), axis=1, keepdims=True
    )
    power[...] = numer_ref[...] / mass_column - 1.0 / size
    start = jnp.full((8, size), 1.0 / size, jnp.float32)

    def going(state):
        turn, height, row = state
        return jnp.logical_and(turn < 40, height > 1e-10)

    def turn_once(state):
        turn, height, row = state
        now = power[...]
        row = row + jnp.dot(row, now, precision=HIGHEST, preferred_element_type=jnp.float32)
        after = jnp.dot(now, now, precision=HIGHEST, preferred_element_type=jnp.float32)
        power[...] = after
        return turn + 1, jnp.max(jnp.abs(after)), row

    state = (jnp.int32(0), jnp.max(jnp.abs(power[...])), start)
    balance = lax.while_loop(going, turn_once, state)[2]
    coarse_ref[...] = balance * float(size)

    share = balance[0:1] / mass
    spread[...] = jnp.zeros_like(spread)
    for q in range(4):
        tile = label_ref[...]
        spread[pl.ds(q, 16, stride=4), :] = tile if q == 0 else pltpu.roll(tile, 128 - 32 * q, 1)
    names = jnp.transpose(spread[...])[0:32]
    lane = lax.broadcasted_iota(jnp.int32, (32, size), 1).astype(jnp.float32)
    for a in range(state_ref.shape[0]):
        picked = jnp.where(names[:, a : a + 1] == lane, share, 0.0)
        factor = jnp.sum(picked, axis=1, keepdims=True)
        refined_ref[a] = state_ref[a] * factor * float(CTRL * SHELF * DISK)


def balance_of(numer, total, label_tile, state):
    return pl.pallas_call(
        balance_kernel,
        out_shape=(
            jax.ShapeDtypeStruct(state.shape, jnp.float32),
            jax.ShapeDtypeStruct((8, NBLK), jnp.float32),
        ),
        in_specs=[pl.BlockSpec(memory_space=VMEM)] * 4,
        out_specs=(pl.BlockSpec(memory_space=VMEM), pl.BlockSpec(memory_space=VMEM)),
        scratch_shapes=[
            pltpu.VMEM((NBLK, NBLK), jnp.float32),
            pltpu.VMEM((128, 128), jnp.float32),
        ],
        compiler_params=pltpu.CompilerParams(vmem_limit_bytes=32 << 20),
        name="balance",
    )(numer, total, label_tile, state)


def spread_small(own, wide, stages, send_sem, recv_sem):
    (outer_me, outer_size, outer_peer), (inner_me, inner_size, inner_peer) = stages

    def stage(which, me, size, peer, piece):
        def copy(step):
            return pltpu.make_async_remote_copy(
                src_ref=piece,
                dst_ref=piece,
                send_sem=send_sem.at[which, step],
                recv_sem=recv_sem.at[which, step],
                device_id=peer((me + step) % size),
                device_id_type=MESH,
            )

        def start(step, carry):
            copy(step).start()
            return carry

        def finish(step, carry):
            copy(step).wait()
            return carry

        return start, finish, size

    wide[inner_me, outer_me] = own
    first = stage(0, outer_me, outer_size, outer_peer, wide.at[inner_me, outer_me])
    second = stage(1, inner_me, inner_size, inner_peer, wide.at[inner_me])
    return first, second


def shelf_stages():
    ctrl = lax.axis_index("ctrl")
    shelf = lax.axis_index("shelf")
    return (
        (shelf // 4, 8, lambda m: (ctrl, m * 4 + shelf % 4)),
        (shelf % 4, 4, lambda m: (ctrl, shelf - shelf % 4 + m)),
    )


def ctrl_stages():
    ctrl = lax.axis_index("ctrl")
    shelf = lax.axis_index("shelf")
    return (
        (ctrl // 2, 8, lambda m: (m * 2 + ctrl % 2, shelf)),
        (ctrl % 2, 2, lambda m: (ctrl - ctrl % 2 + m, shelf)),
    )


def as_tile(values):
    return jnp.pad(values.reshape(12, 128), ((0, 4), (0, 0)))


def steps_kernel(
    prob_ref, ctrl_rows_ref, shelf_rows_ref, disk_in_ref, label_ref,
    state_ref, first_ref, shelf_labels_ref, shelf_cols_ref, weight_wide_ref, mass_ref, kept_ref, base_ref,
    weight_ref, by_weight,
    ctrl_all, shelf_all, by_shelf, by_ctrl, ctrl_wide, ctrl_own, ctrl_ref, shelf_ref, disk_ref,
    label_rows, shelf_wide_rows, ctrl_labels, rate_ref, shelf_rate_ref, scale_ref, disk_row,
    home_y, home_z, at_y, made_y, at_z, made_z, back_y, back_z,
    swap_send, swap_recv, ring_send, ring_recv, pair_send, pair_recv,
    send_a, recv_a, send_b, recv_b, send_w, recv_w, send_y, recv_y, send_sem, recv_sem,
):
    ctrl = lax.axis_index("ctrl")
    shelf = lax.axis_index("shelf")
    chip, core = shelf // 2, shelf % 2
    ctrls, shelves = 16, 32
    chips = shelves // 2
    rows_c, rows_s = state_ref.shape[0], state_ref.shape[1]
    per_y, per_z = rows_s // ctrls, rows_c // chips
    lanes = 128

    barrier = pltpu.get_barrier_semaphore()

    def signal_y(step, carry):
        target = ((ctrl + step) % ctrls, shelf)
        pl.semaphore_signal(barrier, inc=1, device_id=target, device_id_type=MESH)
        return carry

    def signal_z(step, carry):
        target = (ctrl, (shelf + step) % shelves)
        pl.semaphore_signal(barrier, inc=1, device_id=target, device_id_type=MESH)
        return carry

    lax.fori_loop(1, ctrls, signal_y, 0)
    lax.fori_loop(1, shelves, signal_z, 0)
    state_ref[...] = prob_ref[...]
    disk_ref[...] = disk_in_ref[...].astype(jnp.bfloat16)
    deep, side = shelf // 4, (shelf // 2) % 2
    wides = (ctrl_all, shelf_all)
    ctrl_all[deep, side, core] = ctrl_rows_ref[...].astype(jnp.bfloat16)
    shelf_all[deep, side, core] = shelf_rows_ref[...].astype(jnp.bfloat16)
    label_a = spread_small(label_ref[...], by_shelf, shelf_stages(), send_a, recv_a)
    label_b = spread_small(label_ref[...], by_ctrl, ctrl_stages(), send_b, recv_b)

    order = lax.broadcasted_iota(jnp.int32, (256, 256), 0)
    other = lax.broadcasted_iota(jnp.int32, (256, 256), 1)
    swap = jnp.where(
        jnp.logical_and(order // 16 == other % 16, order % 16 == other // 16), 1.0, 0.0
    ).astype(jnp.bfloat16)
    pl.semaphore_wait(barrier, ctrls - 1 + shelves - 1)

    def along_shelf(piece, send, recv, target):
        return pltpu.make_async_remote_copy(
            src_ref=piece, dst_ref=piece, send_sem=send, recv_sem=recv,
            device_id=(ctrl, target), device_id_type=MESH,
        )

    swaps = [
        along_shelf(
            wide.at[deep, side, core], swap_send.at[n], swap_recv.at[n], shelf + 2 - 4 * side
        )
        for n, wide in enumerate(wides)
    ]
    for copy in swaps:
        copy.start()
    for start, _, size in (label_a[0], label_b[0]):
        lax.fori_loop(1, size, start, 0)

    right = ((deep + 1) % 8) * 4 + shelf % 4
    left = ((deep + 7) % 8) * 4 + shelf % 4
    sibling = shelf + 1 - 2 * core

    def pair(n, block, side_core):
        piece = wides[n].at[block, :, side_core]
        return along_shelf(piece, pair_send.at[n, block], pair_recv.at[n, block], sibling)

    def hop(n, way, count):
        block = (deep + 8 - count + 1) % 8 if way == 0 else (deep + count - 1) % 8
        return along_shelf(
            wides[n].at[block, :, core],
            ring_send.at[n, way, count - 1],
            ring_recv.at[n, way, count - 1],
            right if way == 0 else left,
        )

    def used(n, way, count):
        return count < 4 or n == way

    def gather_rows():
        for copy in swaps:
            copy.wait()
        for n in range(2):
            for way in range(2):
                hop(n, way, 1).start()
            pair(n, deep, core).start()
        for _, finish, size in (label_a[0], label_b[0]):
            lax.fori_loop(1, size, finish, 0)
        for start, _, size in (label_a[1], label_b[1]):
            lax.fori_loop(1, size, start, 0)
        for count in range(1, 5):
            for n in range(2):
                for way in range(2):
                    if not used(n, way, count):
                        continue
                    hop(n, way, count).wait_recv()
                    if count < 4 and used(n, way, count + 1):
                        hop(n, way, count + 1).start()
                    pair(n, (deep + 8 - count) % 8 if way == 0 else (deep + count) % 8, core).start()
        for _, finish, size in (label_a[1], label_b[1]):
            lax.fori_loop(1, size, finish, 0)
        for count in range(1, 5):
            for n in range(2):
                for way in range(2):
                    if used(n, way, count):
                        hop(n, way, count).wait_send()

        def settle(block, carry):
            for n in range(2):
                pair(n, block, 1 - core).wait_recv()
                pair(n, block, core).wait_send()
            return carry

        lax.fori_loop(0, 8, settle, 0)

    def prepare():
        unit = jnp.where(order == other, 1.0, 0.0).astype(jnp.bfloat16)
        dims = (((1,), (1,)), ((), ()))
        for n in range(shelves):
            wide = ctrl_all[n // 4, (n // 2) % 2, n % 2].astype(jnp.float32)
            ctrl_wide[n * 24 : n * 24 + 24] = wide
        for m in range(0, CTRL, 256):
            block = ctrl_wide[:, m : m + 256].astype(jnp.bfloat16)
            turned = lax.dot_general(unit, block, dims, preferred_element_type=jnp.float32)
            ctrl_ref[m : m + 256] = turned.astype(jnp.bfloat16)
        shelf_sum = jnp.zeros((SHELF, 1), jnp.float32)
        for m in range(0, SHELF, 256):
            block = shelf_all[:, :, :, :, m : m + 256].reshape(SHELF, 256)
            turned = lax.dot_general(unit, block, dims, preferred_element_type=jnp.float32)
            shelf_ref[m : m + 256] = turned.astype(jnp.bfloat16)
            shelf_sum += jnp.sum(block.astype(jnp.float32), axis=1, keepdims=True)
        shelf_cols_ref[...] = shelf_ref[
            pl.ds(pl.multiple_of(shelf * rows_s, 16), rows_s)
        ].astype(jnp.float32)

        ctrl_max = jnp.max(
            jnp.sum(ctrl_wide[...], axis=1, keepdims=True), axis=0, keepdims=True
        )
        shelf_max = jnp.max(shelf_sum, axis=0, keepdims=True)
        ones = jnp.ones((8, 256), jnp.bfloat16)
        disk_sum = lax.dot_general(ones, disk_ref[...], dims, preferred_element_type=jnp.float32)
        disk_max = jnp.max(disk_sum[0:1], axis=1, keepdims=True)
        base = 1.05 * (ctrl_max * shelf_max) * disk_max
        own_rows = ctrl_wide[pl.ds(pl.multiple_of(ctrl * rows_c, 8), rows_c)]
        ctrl_own[...] = own_rows.astype(jnp.bfloat16)
        own_c = jnp.sum(own_rows, axis=1, keepdims=True)
        own_s = jnp.sum(
            shelf_rows_ref[...].astype(jnp.bfloat16).astype(jnp.float32), axis=1, keepdims=True
        )
        rate_ref[...] = own_c * disk_sum[0:1] / base
        shelf_rate_ref[...] = jnp.broadcast_to(own_s, (rows_s, 256))
        scale_ref[...] = jnp.broadcast_to(1.0 / base, (8, 256))
        disk_row[...] = disk_sum
        base_ref[...] = jnp.broadcast_to(base, (8, lanes))

        spread_pairs(by_shelf, shelf_wide_rows)
        for z in range(8):
            shelf_labels_ref[:, z * lanes : (z + 1) * lanes] = shelf_wide_rows[z, 0:rows_c]
        for i in range(ctrls):
            tile = by_ctrl[i % 2, i // 2]
            for q in range(4):
                moved = tile if q == 0 else pltpu.roll(tile, lanes - 32 * q, 1)
                label_rows[i, pl.ds(q, 16, stride=4), :] = moved
        turned = jnp.transpose(label_rows[:, 0:rows_c, :].reshape(CTRL, lanes))
        ctrl_labels[...] = turned[0:rows_s]

    names = lax.broadcasted_iota(jnp.int32, (NBLK, CTRL), 0).astype(jnp.float32)

    def fill(slot):
        part = rows_s // 8

        def body(row, carry):
            have = jnp.broadcast_to(ctrl_labels[pl.ds(row, 1), :], (NBLK, CTRL))
            member = jnp.where(have == names, 1.0, 0.0).astype(jnp.bfloat16)
            first_ref[row] = lax.dot_general(
                ctrl_own[...], member, (((1,), (1,)), ((), ())), preferred_element_type=jnp.float32
            ).astype(first_ref.dtype)
            return carry

        lax.fori_loop(slot * part, slot * part + part, body, 0)

    def swapped(block):
        flat = jnp.dot(swap, block.reshape(256, lanes), preferred_element_type=jnp.float32)
        return flat.astype(jnp.bfloat16).reshape(16, 16, lanes)

    def exchange_rows(source, target):
        first, second = source.shape[0], source.shape[1]
        for p in range(0, first, 16):
            for q in range(0, second, 16):
                target[q : q + 16, p : p + 16, :] = swapped(source[p : p + 16, q : q + 16, :])

    def part_s(ref, owner):
        return ref.at[:, pl.ds(pl.multiple_of(owner * rows_s, 16), rows_s), :]

    def remote(source, target, stream, mine, theirs, device):
        return pltpu.make_async_remote_copy(
            src_ref=source, dst_ref=target,
            send_sem=send_sem.at[stream, theirs], recv_sem=recv_sem.at[stream, mine],
            device_id=device, device_id_type=MESH,
        )

    def remote_y(source, target, half, way, n, mine, peer):
        return pltpu.make_async_remote_copy(
            src_ref=source, dst_ref=target,
            send_sem=send_y.at[half, way, n, peer], recv_sem=recv_y.at[half, way, n, mine],
            device_id=(peer, shelf), device_id_type=MESH,
        )

    def each(count, first, act):
        def body(step, carry):
            act((first + step) % count)
            return carry

        lax.fori_loop(1, count, body, 0)

    def rows_of(ref, owner):
        return ref.at[pl.ds(pl.multiple_of(owner * rows_c, 16), rows_c), :]

    def y_forward(half):
        for n in range(per_y):

            def act(peer, n=n):
                remote_y(
                    home_y.at[half, peer * per_y + n], rows_of(at_y.at[half, n], ctrl),
                    half, 0, n, ctrl, peer,
                ).start()

            each(ctrls, ctrl, act)
            rows_of(at_y.at[half, n], ctrl)[...] = home_y[half, ctrl * per_y + n]

    def y_middle(half):
        for n in range(per_y):

            def arrived(peer, n=n):
                remote_y(
                    home_y.at[half, peer * per_y + n], rows_of(at_y.at[half, n], peer),
                    half, 0, n, peer, peer,
                ).wait()

            each(ctrls, ctrl, arrived)
            for m in range(0, ctrls * rows_c, 256):
                made = jnp.dot(
                    ctrl_ref[m : m + 256], at_y[half, n], preferred_element_type=jnp.float32
                )
                made_y[half, n, m : m + 256, :] = made.astype(jnp.bfloat16)

            def act(peer, n=n):
                remote_y(
                    rows_of(made_y.at[half, n], peer), back_y.at[half, ctrl * per_y + n],
                    half, 1, n, ctrl, peer,
                ).start()

            each(ctrls, ctrl, act)
            back_y[half, ctrl * per_y + n] = rows_of(made_y.at[half, n], ctrl)[...]

    def y_back_wait(half):
        for n in range(per_y):

            def act(peer, n=n):
                remote_y(
                    rows_of(made_y.at[half, n], peer), back_y.at[half, peer * per_y + n],
                    half, 1, n, peer, peer,
                ).wait()

            each(ctrls, ctrl, act)

    def z_forward_copy(half, to):
        return remote(
            home_z.at[half, pl.ds(to * per_z, per_z)], part_s(at_z, shelf),
            2 * half, shelf, to, (ctrl, 2 * to + half),
        )

    def z_forward(half):
        each(chips, chip, lambda to: z_forward_copy(half, to).start())

        @pl.when(core != half)
        def _():
            z_forward_copy(half, chip).start()

        @pl.when(core == half)
        def _():
            part_s(at_z, shelf)[...] = home_z[half, pl.ds(chip * per_z, per_z)]

    def z_forward_sent(half):
        each(chips, chip, lambda to: z_forward_copy(half, to).wait_send())

        @pl.when(core != half)
        def _():
            z_forward_copy(half, chip).wait_send()

    def z_middle(half):
        @pl.when(core == half)
        def _():
            def arrived(peer):
                remote(
                    home_z.at[half, pl.ds(0, per_z)], part_s(at_z, peer),
                    2 * half, peer, 0, (ctrl, peer),
                ).wait_recv()

            each(shelves, shelf, arrived)
            wide = jnp.concatenate([at_z[n] for n in range(per_z)], axis=1)
            for m in range(0, shelves * rows_s, 256):
                made = jnp.dot(shelf_ref[m : m + 256], wide, preferred_element_type=jnp.float32)
                for n in range(per_z):
                    made_z[n, m : m + 256, :] = made[:, n * lanes : (n + 1) * lanes].astype(
                        jnp.bfloat16
                    )

            def act(peer):
                remote(
                    part_s(made_z, peer), back_z.at[half, pl.ds(chip * per_z, per_z)],
                    2 * half + 1, chip, peer, (ctrl, peer),
                ).start()

            each(shelves, shelf, act)
            back_z[half, pl.ds(chip * per_z, per_z)] = part_s(made_z, shelf)[...]

    def z_back_from(half, source):
        return remote(
            part_s(made_z, shelf), back_z.at[half, pl.ds(source * per_z, per_z)],
            2 * half + 1, source, 0, (ctrl, 2 * source + half),
        )

    def z_back_wait(half):
        each(chips, chip, lambda source: z_back_from(half, source).wait_recv())

        @pl.when(core != half)
        def _():
            z_back_from(half, chip).wait_recv()

    def z_back_sent(half):
        @pl.when(core == half)
        def _():
            def act(peer):
                remote(
                    part_s(made_z, peer), back_z.at[half, pl.ds(chip * per_z, per_z)],
                    2 * half + 1, chip, peer, (ctrl, peer),
                ).wait_send()

            each(shelves, shelf, act)

    def one_step(repeat, carry):
        for p in range(0, rows_c, 16):
            rounded = state_ref[p : p + 16].astype(jnp.bfloat16).reshape(16 * rows_s, 256)
            made = jnp.dot(rounded, disk_ref[...], preferred_element_type=jnp.float32)
            made = made.astype(jnp.bfloat16).reshape(16, rows_s, 256)
            home_z[1, p : p + 16] = made[:, :, lanes:]
            for q in range(0, rows_s, 16):
                home_y[0, q : q + 16, p : p + 16, :] = swapped(made[:, q : q + 16, :lanes])
        z_forward(1)
        y_forward(0)

        @pl.when(repeat == 0)
        def _():
            gather_rows()
            prepare()

        fill(repeat * 4)
        y_middle(0)
        z_middle(1)
        fill(repeat * 4 + 1)
        y_back_wait(0)
        exchange_rows(back_y.at[0], home_z.at[0])
        z_forward(0)
        z_back_wait(1)
        exchange_rows(back_z.at[1], home_y.at[1])
        y_forward(1)
        fill(repeat * 4 + 2)
        z_middle(0)
        y_middle(1)
        fill(repeat * 4 + 3)
        z_back_wait(0)
        y_back_wait(1)
        z_forward_sent(1)
        exchange_rows(back_y.at[1], home_z.at[1])

        def update(row, inner):
            kept = 1.0 - rate_ref[pl.ds(row, 1), :] * shelf_rate_ref[...]
            third = jnp.concatenate([back_z[0, row], home_z[1, row]], axis=1)
            state_ref[row] = third.astype(jnp.float32) * scale_ref[0:1] + state_ref[row] * kept
            return inner

        lax.fori_loop(0, rows_c, update, 0)
        z_forward_sent(0)
        z_back_sent(0)
        z_back_sent(1)
        return carry

    lax.fori_loop(0, STEPS, one_step, 0)

    lead = lax.broadcasted_iota(jnp.int32, (8, 256), 0) == 0
    sums = jnp.where(lead, 1.0, disk_row[...])
    weight_ref[...] = jnp.zeros_like(weight_ref)
    mass_ref[...] = jnp.zeros_like(mass_ref)
    for r in range(rows_c // 4):
        both = lax.dot_general(
            sums,
            state_ref[4 * r : 4 * r + 4].reshape(4 * rows_s, 256),
            (((1,), (1,)), ((), ())),
            precision=HIGHEST,
            preferred_element_type=jnp.float32,
        )
        mass_ref[r : r + 1] = both[0:1]
        weight_ref[r : r + 1] = both[1:2]
    stages = spread_small(weight_ref[...], by_weight, shelf_stages(), send_w, recv_w)
    lax.fori_loop(1, stages[0][2], stages[0][0], 0)
    kept_ref[...] = jnp.zeros_like(kept_ref)
    ones = jnp.ones((8, 256), jnp.float32)
    for r in range(rows_c // 4):
        part = [
            state_ref[n] * (1.0 - rate_ref[n : n + 1] * shelf_rate_ref[...])
            for n in range(4 * r, 4 * r + 4)
        ]
        kept_ref[r : r + 1] = lax.dot_general(
            ones, jnp.concatenate(part, axis=0), NT,
            precision=HIGHEST, preferred_element_type=jnp.float32,
        )[0:1]
    lax.fori_loop(1, stages[0][2], stages[0][1], 0)
    lax.fori_loop(1, stages[1][2], stages[1][0], 0)
    lax.fori_loop(1, stages[1][2], stages[1][1], 0)
    spread_pairs(by_weight, shelf_wide_rows)
    for z in range(8):
        weight_wide_ref[:, z * lanes : (z + 1) * lanes] = shelf_wide_rows[z, 0:rows_c]


def spread_pairs(tiles, wide):
    lane = lax.broadcasted_iota(jnp.int32, (16, 128), 1) // 32
    for z in range(8):
        for q in range(4):
            made = jnp.zeros((16, 128), jnp.float32)
            for p in range(4):
                tile = tiles[p, z]
                moved = tile if p == q else pltpu.roll(tile, (32 * (p - q)) % 128, 1)
                made = jnp.where(lane == p, moved, made)
            wide[z, pl.ds(q, 16, stride=4), :] = made


def power_steps(prob, ctrl_rows, shelf_rows, disk, label_tile):
    rows_c, rows_s, _ = prob.shape
    bf, f32 = jnp.bfloat16, jnp.float32
    outs = [
        (prob.shape, f32), ((rows_s, rows_c, NBLK), bf), ((rows_c, SHELF), f32), ((rows_s, SHELF), f32),
        ((rows_c, SHELF), f32), ((16, 128), f32), ((16, 128), f32), ((8, 128), f32),
    ]
    dma = pltpu.SemaphoreType.DMA
    return pl.pallas_call(
        steps_kernel,
        out_shape=tuple(jax.ShapeDtypeStruct(*out) for out in outs),
        in_specs=[pl.BlockSpec(memory_space=VMEM)] * 5,
        out_specs=tuple([pl.BlockSpec(memory_space=VMEM)] * len(outs)),
        scratch_shapes=[
            pltpu.VMEM((16, 128), f32),
            pltpu.VMEM((4, 8, 16, 128), f32),
            pltpu.VMEM((8, 2, 2, 24, CTRL), bf),
            pltpu.VMEM((8, 2, 2, 32, SHELF), bf),
            pltpu.VMEM((4, 8, 16, 128), f32),
            pltpu.VMEM((2, 8, 16, 128), f32),
            pltpu.VMEM((CTRL, CTRL), f32),
            pltpu.VMEM((rows_c, CTRL), bf),
            pltpu.VMEM((CTRL, CTRL), bf),
            pltpu.VMEM((SHELF, SHELF), bf),
            pltpu.VMEM((DISK, DISK), bf),
            pltpu.VMEM((16, 64, 128), f32),
            pltpu.VMEM((8, 64, 128), f32),
            pltpu.VMEM((rows_s, CTRL), f32),
            pltpu.VMEM((rows_c, DISK), f32),
            pltpu.VMEM((rows_s, DISK), f32),
            pltpu.VMEM((8, DISK), f32),
            pltpu.VMEM((8, DISK), f32),
            pltpu.VMEM((2, rows_s, rows_c, 128), bf),
            pltpu.VMEM((2, rows_c, rows_s, 128), bf),
            pltpu.VMEM((2, 2, CTRL, 128), bf),
            pltpu.VMEM((2, 2, CTRL, 128), bf),
            pltpu.VMEM((3, SHELF, 128), bf),
            pltpu.VMEM((3, SHELF, 128), bf),
            pltpu.VMEM((2, rows_s, rows_c, 128), bf),
            pltpu.VMEM((2, rows_c, rows_s, 128), bf),
            dma((2,)), dma((2,)), dma((2, 2, 4)), dma((2, 2, 4)), dma((2, 8)), dma((2, 8)),
            dma((2, 8)), dma((2, 8)), dma((2, 8)), dma((2, 8)), dma((2, 8)), dma((2, 8)),
            dma((2, 2, 2, 16)), dma((2, 2, 2, 16)), dma((4, 32)), dma((4, 32)),
        ],
        compiler_params=pltpu.CompilerParams(
            collective_id=4, has_side_effects=True, vmem_limit_bytes=56 << 20
        ),
        name="power_steps",
    )(prob, ctrl_rows, shelf_rows, disk, label_tile)


def local(prob, ctrl_rates, shelf_rates, disk_rates, labels):
    label_tile = as_tile(labels.astype(jnp.float32))
    outs = power_steps(prob, ctrl_rates, shelf_rates, disk_rates, label_tile)
    iterate, first, shelf_labels, shelf_columns, shelf_weight, mass_tile, kept_tile, base = outs
    numer, total = reduce_all(
        shelf_labels, shelf_weight, shelf_columns, first, label_tile, mass_tile, kept_tile, base
    )
    refined, coarse = balance_of(numer, total, label_tile, iterate)
    return (refined, coarse[0])


def solution(mesh):
    placed = (P("ctrl", "shelf", None), P("shelf", None), P("shelf", None), P(), P("ctrl", "shelf"))
    return jax.shard_map(
        local,
        mesh=mesh,
        in_specs=placed,
        out_specs=(P("ctrl", "shelf", None), P()),
        check_vma=False,
    )
```

```python
import functools

import jax
import jax.numpy as jnp
from jax import lax
from jax.experimental import pallas as pl
from jax.experimental.pallas import tpu as pltpu
from jax.sharding import PartitionSpec as P

CTRL = 768
SHELF = 1024
DISK = 256
NBLK = 256
STEPS = 2
GROUP = 8
MESH = pl.DeviceIdType.MESH
VMEM = pltpu.MemorySpace.VMEM
HIGHEST = lax.Precision.HIGHEST


def place():
    ctrl = lax.axis_index("ctrl")
    shelf = lax.axis_index("shelf")
    plane_me = (ctrl % 2) * 4 + shelf % 4
    deep_me = shelf // 4
    high_me = ctrl // 2

    def plane(member):
        return (ctrl - ctrl % 2 + member // 4, shelf - shelf % 4 + member % 4)

    def deep(member):
        return (ctrl, member * 4 + shelf % 4)

    def high(member):
        return (member * 2 + ctrl % 2, shelf)

    return (plane_me, plane), (deep_me, deep), (high_me, high)


def exchange(group, streams, send_sem, recv_sem):
    me, peer = group

    def copy(step, index):
        source, target = streams[index]
        member = (me + step) % GROUP
        return pltpu.make_async_remote_copy(
            src_ref=source(member),
            dst_ref=target,
            send_sem=send_sem.at[index, step],
            recv_sem=recv_sem.at[index, step],
            device_id=peer(member),
            device_id_type=MESH,
        )

    def start(step, carry):
        for index in range(len(streams)):
            copy(step, index).start()
        return carry

    def finish(step, carry):
        for index in range(len(streams)):
            copy(step, index).wait()
        return carry

    lax.fori_loop(1, GROUP, start, 0)
    lax.fori_loop(1, GROUP, finish, 0)


NT = (((1,), (1,)), ((), ()))


def flow_part(labels_ref, weight_ref, factor_ref, first_ref, out_ref, wide, held):
    count = labels_ref.shape[1]
    depth = factor_ref.shape[0]
    blocks = lax.broadcasted_iota(jnp.int32, (NBLK, count), 0).astype(jnp.float32)

    def body(row, carry):
        names = jnp.broadcast_to(labels_ref[pl.ds(row, 1), :], (NBLK, count))
        member = jnp.where(names == blocks, 1.0, 0.0).astype(jnp.bfloat16)
        scaled = factor_ref[...] * weight_ref[pl.ds(row, 1), :]
        upper = scaled.astype(jnp.bfloat16)
        slot = row % 2
        wide[slot, 0:depth, :] = upper
        wide[slot, depth : 2 * depth, :] = (scaled - upper.astype(jnp.float32)).astype(jnp.bfloat16)
        both = lax.dot_general(wide[slot], member, NT, preferred_element_type=jnp.float32)
        held[:, pl.ds(row, 1), :] = (both[0:depth] + both[depth:]).reshape(depth, 1, NBLK)
        return carry

    lax.fori_loop(0, labels_ref.shape[0], body, 0, unroll=2)
    rows = held.shape[0] * held.shape[1]
    mine = held[...].reshape(rows, NBLK)
    first = first_ref[...].reshape(rows, NBLK)
    upper = mine.astype(jnp.bfloat16)
    lower = (mine - upper.astype(jnp.float32)).astype(jnp.bfloat16)
    dims = (((0,), (0,)), ((), ()))
    out_ref[...] = lax.dot_general(
        upper, first, dims, preferred_element_type=jnp.float32
    ) + lax.dot_general(lower, first, dims, preferred_element_type=jnp.float32)


def block_terms(label_ref, pair_mass_ref, pair_kept_ref):
    line = lax.broadcasted_iota(jnp.int32, (8, 128), 0)
    names = lax.broadcasted_iota(jnp.int32, (NBLK, 128), 0).astype(jnp.float32)
    terms = jnp.zeros((8, NBLK), jnp.float32)
    for r in range(12):
        have = jnp.broadcast_to(label_ref[r : r + 1], (NBLK, 128))
        member = jnp.where(have == names, 1.0, 0.0)
        pair = jnp.where(line == 0, pair_mass_ref[r : r + 1], 0.0)
        pair = jnp.where(line == 1, pair_kept_ref[r : r + 1], pair)
        terms += lax.dot_general(
            pair, member, NT, precision=HIGHEST, preferred_element_type=jnp.float32
        )
    return terms


def reduce_part(
    groups,
    labels_ref, weight_ref, factor_ref, first_ref, label_ref, pair_mass_ref, pair_kept_ref, base_ref,
    sum_ref, total_ref,
    part_ref, mass_ref, wide, held,
    rows, tiles, highs, deeps, blocks, mass_plane, mass_deep, mass_high,
    send_sem, recv_sem,
):
    plane, deep, high = groups
    plane_me, deep_me, high_me = plane[0], deep[0], high[0]

    flow_part(labels_ref, weight_ref, factor_ref, first_ref, part_ref, wide, held)
    terms = block_terms(label_ref, pair_mass_ref, pair_kept_ref)
    mass_ref[...] = jnp.zeros_like(mass_ref)
    mass_ref[0:1] = terms[0:1, 0:128]
    mass_ref[1:2] = terms[0:1, 128:256]
    row = lax.broadcasted_iota(jnp.int32, (NBLK, NBLK), 0)
    column = lax.broadcasted_iota(jnp.int32, (NBLK, NBLK), 1)
    kept = jnp.where(row == column, jnp.broadcast_to(terms[1:2], (NBLK, NBLK)), 0.0)
    part_ref[...] = part_ref[...] / base_ref[0:1, 0:1] + kept

    exchange(
        plane,
        (
            (lambda m: part_ref.at[pl.ds(pl.multiple_of(m * 32, 32), 32)], rows.at[plane_me]),
            (lambda m: mass_ref, mass_plane.at[plane_me]),
        ),
        send_sem.at[0], recv_sem.at[0],
    )
    rows[plane_me] = part_ref[pl.ds(pl.multiple_of(plane_me * 32, 32), 32)]
    mass_plane[plane_me] = mass_ref[...]
    mine = jnp.sum(rows[...], axis=0)
    for tile in range(GROUP):
        r, h = tile // 2, tile % 2
        tiles[tile] = mine[r * 8 : r * 8 + 8, h * 128 : h * 128 + 128]
    total_ref[...] = jnp.sum(mass_plane[...], axis=0)

    exchange(
        deep,
        (
            (lambda m: tiles.at[m], deeps.at[deep_me]),
            (lambda m: total_ref, mass_deep.at[deep_me]),
        ),
        send_sem.at[1], recv_sem.at[1],
    )
    deeps[deep_me] = tiles[deep_me]
    mass_deep[deep_me] = total_ref[...]
    highs[high_me] = jnp.sum(deeps[...], axis=0)
    mass_high[high_me] = jnp.sum(mass_deep[...], axis=0)

    exchange(
        high,
        (
            (lambda m: highs.at[high_me], highs.at[high_me]),
            (lambda m: mass_high.at[high_me], mass_high.at[high_me]),
        ),
        send_sem.at[2], recv_sem.at[2],
    )
    total_ref[...] = jnp.sum(mass_high[...], axis=0)
    blocks[deep_me] = jnp.sum(highs[...], axis=0)

    exchange(
        deep,
        ((lambda m: blocks.at[deep_me], blocks.at[deep_me]),),
        send_sem.at[3], recv_sem.at[3],
    )
    for tile in range(GROUP):
        r, h = tile // 2, tile % 2
        sum_ref[
            pl.ds(pl.multiple_of(plane_me * 32 + r * 8, 8), 8), h * 128 : h * 128 + 128
        ] = blocks[tile]
    own = sum_ref.at[pl.ds(pl.multiple_of(plane_me * 32, 32), 32)]
    exchange(plane, ((lambda m: own, own),), send_sem.at[4], recv_sem.at[4])


def balance_kernel(numer_ref, total_ref, label_ref, state_ref, refined_ref, coarse_ref, power, spread, held, sem):
    load = pltpu.make_async_copy(state_ref, held, sem)
    load.start()
    size = NBLK
    line = lax.broadcasted_iota(jnp.int32, (size, size), 0)
    column = lax.broadcasted_iota(jnp.int32, (size, size), 1)
    mass = jnp.concatenate([total_ref[0:1], total_ref[1:2]], axis=1)
    mass_column = jnp.sum(
        jnp.where(line == column, jnp.broadcast_to(mass, (size, size)), 0.0), axis=1, keepdims=True
    )
    power[...] = numer_ref[...] / mass_column - 1.0 / size
    start = jnp.full((8, size), 1.0 / size, jnp.float32)

    def going(state):
        turn, height, row = state
        return jnp.logical_and(turn < 40, height > 1e-10)

    def turn_once(state):
        turn, height, row = state
        now = power[...]
        row = row + jnp.dot(row, now, precision=HIGHEST, preferred_element_type=jnp.float32)
        after = jnp.dot(now, now, precision=HIGHEST, preferred_element_type=jnp.float32)
        power[...] = after
        return turn + 1, jnp.max(jnp.abs(after)), row

    state = (jnp.int32(0), jnp.max(jnp.abs(power[...])), start)
    balance = lax.while_loop(going, turn_once, state)[2]
    coarse_ref[...] = balance * float(size)

    share = balance[0:1] / mass
    spread[...] = jnp.zeros_like(spread)
    for q in range(4):
        tile = label_ref[...]
        spread[pl.ds(q, 16, stride=4), :] = tile if q == 0 else pltpu.roll(tile, 128 - 32 * q, 1)
    names = jnp.transpose(spread[...])[0:32]
    lane = lax.broadcasted_iota(jnp.int32, (32, size), 1).astype(jnp.float32)
    load.wait()
    for a in range(held.shape[0]):
        picked = jnp.where(names[:, a : a + 1] == lane, share, 0.0)
        factor = jnp.sum(picked, axis=1, keepdims=True)
        refined_ref[a] = held[a] * factor * float(CTRL * SHELF * DISK)


def balance_of(numer, total, label_tile, state):
    return pl.pallas_call(
        balance_kernel,
        out_shape=(
            jax.ShapeDtypeStruct(state.shape, jnp.float32),
            jax.ShapeDtypeStruct((8, NBLK), jnp.float32),
        ),
        in_specs=[pl.BlockSpec(memory_space=VMEM)] * 3 + [pl.BlockSpec(memory_space=pl.ANY)],
        out_specs=(pl.BlockSpec(memory_space=VMEM), pl.BlockSpec(memory_space=VMEM)),
        scratch_shapes=[
            pltpu.VMEM((NBLK, NBLK), jnp.float32),
            pltpu.VMEM((128, 128), jnp.float32),
            pltpu.VMEM(state.shape, jnp.float32),
            pltpu.SemaphoreType.DMA,
        ],
        compiler_params=pltpu.CompilerParams(vmem_limit_bytes=32 << 20),
        name="balance",
    )(numer, total, label_tile, state)


def spread_small(own, wide, stages, send_sem, recv_sem):
    (outer_me, outer_size, outer_peer), (inner_me, inner_size, inner_peer) = stages

    def stage(which, me, size, peer, piece):
        def copy(step):
            return pltpu.make_async_remote_copy(
                src_ref=piece,
                dst_ref=piece,
                send_sem=send_sem.at[which, step],
                recv_sem=recv_sem.at[which, step],
                device_id=peer((me + step) % size),
                device_id_type=MESH,
            )

        def start(step, carry):
            copy(step).start()
            return carry

        def finish(step, carry):
            copy(step).wait()
            return carry

        return start, finish, size

    wide[inner_me, outer_me] = own
    first = stage(0, outer_me, outer_size, outer_peer, wide.at[inner_me, outer_me])
    second = stage(1, inner_me, inner_size, inner_peer, wide.at[inner_me])
    return first, second


def shelf_stages():
    ctrl = lax.axis_index("ctrl")
    shelf = lax.axis_index("shelf")
    return (
        (shelf // 4, 8, lambda m: (ctrl, m * 4 + shelf % 4)),
        (shelf % 4, 4, lambda m: (ctrl, shelf - shelf % 4 + m)),
    )


def ctrl_stages():
    ctrl = lax.axis_index("ctrl")
    shelf = lax.axis_index("shelf")
    return (
        (ctrl // 2, 8, lambda m: (m * 2 + ctrl % 2, shelf)),
        (ctrl % 2, 2, lambda m: (ctrl - ctrl % 2 + m, shelf)),
    )


def as_tile(values):
    return jnp.pad(values.reshape(12, 128), ((0, 4), (0, 0)))


def steps_kernel(
    prob_ref, ctrl_rows_ref, shelf_rows_ref, disk_in_ref, label_ref,
    state_ref, sum_ref, total_ref,
    first_ref, shelf_labels_ref, shelf_cols_ref, weight_wide_ref, mass_ref, kept_ref, base_ref,
    part_ref, block_mass_ref, wide, held,
    rows, tiles, highs, deeps, blocks, mass_plane, mass_deep, mass_high,
    weight_ref, by_weight,
    ctrl_all, shelf_all, by_shelf, by_ctrl, ctrl_wide, ctrl_own, ctrl_ref, shelf_ref, disk_ref,
    label_rows, shelf_wide_rows, ctrl_labels, rate_ref, shelf_rate_ref, scale_ref, disk_row,
    home_y, home_z, at_y, made_y, at_z, made_z, back_y, back_z,
    swap_send, swap_recv, ring_send, ring_recv, pair_send, pair_recv,
    send_a, recv_a, send_b, recv_b, send_w, recv_w, send_y, recv_y, send_sem, recv_sem,
    send_r, recv_r,
):
    ctrl = lax.axis_index("ctrl")
    shelf = lax.axis_index("shelf")
    chip, core = shelf // 2, shelf % 2
    ctrls, shelves = 16, 32
    chips = shelves // 2
    rows_c, rows_s = state_ref.shape[0], state_ref.shape[1]
    per_y, per_z = rows_s // ctrls, rows_c // chips
    lanes = 128

    barrier = pltpu.get_barrier_semaphore()

    def signal_y(step, carry):
        target = ((ctrl + step) % ctrls, shelf)
        pl.semaphore_signal(barrier, inc=1, device_id=target, device_id_type=MESH)
        return carry

    def signal_z(step, carry):
        target = (ctrl, (shelf + step) % shelves)
        pl.semaphore_signal(barrier, inc=1, device_id=target, device_id_type=MESH)
        return carry

    lax.fori_loop(1, ctrls, signal_y, 0)
    lax.fori_loop(1, shelves, signal_z, 0)
    groups = place()
    plane_me, plane_peer = groups[0]

    def signal_plane(step, carry):
        target = plane_peer((plane_me + step) % GROUP)
        pl.semaphore_signal(barrier, inc=1, device_id=target, device_id_type=MESH)
        return carry

    lax.fori_loop(1, GROUP, signal_plane, 0)
    state_ref[...] = prob_ref[...]
    disk_ref[...] = disk_in_ref[...].astype(jnp.bfloat16)
    deep, side = shelf // 4, (shelf // 2) % 2
    wides = (ctrl_all, shelf_all)
    ctrl_all[deep, side, core] = ctrl_rows_ref[...].astype(jnp.bfloat16)
    shelf_all[deep, side, core] = shelf_rows_ref[...].astype(jnp.bfloat16)
    label_a = spread_small(label_ref[...], by_shelf, shelf_stages(), send_a, recv_a)
    label_b = spread_small(label_ref[...], by_ctrl, ctrl_stages(), send_b, recv_b)

    order = lax.broadcasted_iota(jnp.int32, (256, 256), 0)
    other = lax.broadcasted_iota(jnp.int32, (256, 256), 1)
    swap = jnp.where(
        jnp.logical_and(order // 16 == other % 16, order % 16 == other // 16), 1.0, 0.0
    ).astype(jnp.bfloat16)
    pl.semaphore_wait(barrier, ctrls - 1 + shelves - 1 + GROUP - 1)

    def along_shelf(piece, send, recv, target):
        return pltpu.make_async_remote_copy(
            src_ref=piece, dst_ref=piece, send_sem=send, recv_sem=recv,
            device_id=(ctrl, target), device_id_type=MESH,
        )

    swaps = [
        along_shelf(
            wide.at[deep, side, core], swap_send.at[n], swap_recv.at[n], shelf + 2 - 4 * side
        )
        for n, wide in enumerate(wides)
    ]
    for copy in swaps:
        copy.start()
    for start, _, size in (label_a[0], label_b[0]):
        lax.fori_loop(1, size, start, 0)

    right = ((deep + 1) % 8) * 4 + shelf % 4
    left = ((deep + 7) % 8) * 4 + shelf % 4
    sibling = shelf + 1 - 2 * core

    def pair(n, block, side_core):
        piece = wides[n].at[block, :, side_core]
        return along_shelf(piece, pair_send.at[n, block], pair_recv.at[n, block], sibling)

    def hop(n, way, count):
        block = (deep + 8 - count + 1) % 8 if way == 0 else (deep + count - 1) % 8
        return along_shelf(
            wides[n].at[block, :, core],
            ring_send.at[n, way, count - 1],
            ring_recv.at[n, way, count - 1],
            right if way == 0 else left,
        )

    def used(n, way, count):
        return count < 4 or n == way

    def gather_rows():
        for copy in swaps:
            copy.wait()
        for n in range(2):
            for way in range(2):
                hop(n, way, 1).start()
            pair(n, deep, core).start()
        for _, finish, size in (label_a[0], label_b[0]):
            lax.fori_loop(1, size, finish, 0)
        for start, _, size in (label_a[1], label_b[1]):
            lax.fori_loop(1, size, start, 0)
        for count in range(1, 5):
            for n in range(2):
                for way in range(2):
                    if not used(n, way, count):
                        continue
                    hop(n, way, count).wait_recv()
                    if count < 4 and used(n, way, count + 1):
                        hop(n, way, count + 1).start()
                    pair(n, (deep + 8 - count) % 8 if way == 0 else (deep + count) % 8, core).start()
        for _, finish, size in (label_a[1], label_b[1]):
            lax.fori_loop(1, size, finish, 0)
        for count in range(1, 5):
            for n in range(2):
                for way in range(2):
                    if used(n, way, count):
                        hop(n, way, count).wait_send()

        def settle(block, carry):
            for n in range(2):
                pair(n, block, 1 - core).wait_recv()
                pair(n, block, core).wait_send()
            return carry

        lax.fori_loop(0, 8, settle, 0)

    def prepare():
        unit = jnp.where(order == other, 1.0, 0.0).astype(jnp.bfloat16)
        dims = (((1,), (1,)), ((), ()))
        for n in range(shelves):
            wide = ctrl_all[n // 4, (n // 2) % 2, n % 2].astype(jnp.float32)
            ctrl_wide[n * 24 : n * 24 + 24] = wide
        for m in range(0, CTRL, 256):
            block = ctrl_wide[:, m : m + 256].astype(jnp.bfloat16)
            turned = lax.dot_general(unit, block, dims, preferred_element_type=jnp.float32)
            ctrl_ref[m : m + 256] = turned.astype(jnp.bfloat16)
        shelf_sum = jnp.zeros((SHELF, 1), jnp.float32)
        for m in range(0, SHELF, 256):
            block = shelf_all[:, :, :, :, m : m + 256].reshape(SHELF, 256)
            turned = lax.dot_general(unit, block, dims, preferred_element_type=jnp.float32)
            shelf_ref[m : m + 256] = turned.astype(jnp.bfloat16)
            shelf_sum += jnp.sum(block.astype(jnp.float32), axis=1, keepdims=True)
        shelf_cols_ref[...] = shelf_ref[
            pl.ds(pl.multiple_of(shelf * rows_s, 16), rows_s)
        ].astype(jnp.float32)

        ctrl_max = jnp.max(
            jnp.sum(ctrl_wide[...], axis=1, keepdims=True), axis=0, keepdims=True
        )
        shelf_max = jnp.max(shelf_sum, axis=0, keepdims=True)
        ones = jnp.ones((8, 256), jnp.bfloat16)
        disk_sum = lax.dot_general(ones, disk_ref[...], dims, preferred_element_type=jnp.float32)
        disk_max = jnp.max(disk_sum[0:1], axis=1, keepdims=True)
        base = 1.05 * (ctrl_max * shelf_max) * disk_max
        own_rows = ctrl_wide[pl.ds(pl.multiple_of(ctrl * rows_c, 8), rows_c)]
        ctrl_own[...] = own_rows.astype(jnp.bfloat16)
        own_c = jnp.sum(own_rows, axis=1, keepdims=True)
        own_s = jnp.sum(
            shelf_rows_ref[...].astype(jnp.bfloat16).astype(jnp.float32), axis=1, keepdims=True
        )
        rate_ref[...] = own_c * disk_sum[0:1] / base
        shelf_rate_ref[...] = jnp.broadcast_to(own_s, (rows_s, 256))
        scale_ref[...] = jnp.broadcast_to(1.0 / base, (8, 256))
        disk_row[...] = disk_sum
        base_ref[...] = jnp.broadcast_to(base, (8, lanes))

        spread_pairs(by_shelf, shelf_wide_rows)
        for z in range(8):
            shelf_labels_ref[:, z * lanes : (z + 1) * lanes] = shelf_wide_rows[z, 0:rows_c]
        for i in range(ctrls):
            tile = by_ctrl[i % 2, i // 2]
            for q in range(4):
                moved = tile if q == 0 else pltpu.roll(tile, lanes - 32 * q, 1)
                label_rows[i, pl.ds(q, 16, stride=4), :] = moved
        turned = jnp.transpose(label_rows[:, 0:rows_c, :].reshape(CTRL, lanes))
        ctrl_labels[...] = turned[0:rows_s]

    names = lax.broadcasted_iota(jnp.int32, (NBLK, CTRL), 0).astype(jnp.float32)

    def fill(slot):
        part = rows_s // 8

        def body(row, carry):
            have = jnp.broadcast_to(ctrl_labels[pl.ds(row, 1), :], (NBLK, CTRL))
            member = jnp.where(have == names, 1.0, 0.0).astype(jnp.bfloat16)
            first_ref[row] = lax.dot_general(
                ctrl_own[...], member, (((1,), (1,)), ((), ())), preferred_element_type=jnp.float32
            ).astype(first_ref.dtype)
            return carry

        lax.fori_loop(slot * part, slot * part + part, body, 0)

    def swapped(block):
        flat = jnp.dot(swap, block.reshape(256, lanes), preferred_element_type=jnp.float32)
        return flat.astype(jnp.bfloat16).reshape(16, 16, lanes)

    def exchange_rows(source, target):
        first, second = source.shape[0], source.shape[1]
        for p in range(0, first, 16):
            for q in range(0, second, 16):
                target[q : q + 16, p : p + 16, :] = swapped(source[p : p + 16, q : q + 16, :])

    def part_s(ref, owner):
        return ref.at[:, pl.ds(pl.multiple_of(owner * rows_s, 16), rows_s), :]

    def remote(source, target, stream, mine, theirs, device):
        return pltpu.make_async_remote_copy(
            src_ref=source, dst_ref=target,
            send_sem=send_sem.at[stream, theirs], recv_sem=recv_sem.at[stream, mine],
            device_id=device, device_id_type=MESH,
        )

    def remote_y(source, target, half, way, n, mine, peer):
        return pltpu.make_async_remote_copy(
            src_ref=source, dst_ref=target,
            send_sem=send_y.at[half, way, n, peer], recv_sem=recv_y.at[half, way, n, mine],
            device_id=(peer, shelf), device_id_type=MESH,
        )

    def each(count, first, act):
        def body(step, carry):
            act((first + step) % count)
            return carry

        lax.fori_loop(1, count, body, 0)

    def rows_of(ref, owner):
        return ref.at[pl.ds(pl.multiple_of(owner * rows_c, 16), rows_c), :]

    def y_forward(half):
        for n in range(per_y):

            def act(peer, n=n):
                remote_y(
                    home_y.at[half, peer * per_y + n], rows_of(at_y.at[half, n], ctrl),
                    half, 0, n, ctrl, peer,
                ).start()

            each(ctrls, ctrl, act)
            rows_of(at_y.at[half, n], ctrl)[...] = home_y[half, ctrl * per_y + n]

    def y_middle(half):
        for n in range(per_y):

            def arrived(peer, n=n):
                remote_y(
                    home_y.at[half, peer * per_y + n], rows_of(at_y.at[half, n], peer),
                    half, 0, n, peer, peer,
                ).wait()

            each(ctrls, ctrl, arrived)
            for m in range(0, ctrls * rows_c, 256):
                made = jnp.dot(
                    ctrl_ref[m : m + 256], at_y[half, n], preferred_element_type=jnp.float32
                )
                made_y[half, n, m : m + 256, :] = made.astype(jnp.bfloat16)

            def act(peer, n=n):
                remote_y(
                    rows_of(made_y.at[half, n], peer), back_y.at[half, ctrl * per_y + n],
                    half, 1, n, ctrl, peer,
                ).start()

            each(ctrls, ctrl, act)
            back_y[half, ctrl * per_y + n] = rows_of(made_y.at[half, n], ctrl)[...]

    def y_back_wait(half):
        for n in range(per_y):

            def act(peer, n=n):
                remote_y(
                    rows_of(made_y.at[half, n], peer), back_y.at[half, peer * per_y + n],
                    half, 1, n, peer, peer,
                ).wait()

            each(ctrls, ctrl, act)

    chunks = ((0, 2), (2, 1))

    def z_forward_copy(half, part, to):
        at, size = chunks[part]
        return remote(
            home_z.at[half, pl.ds(to * per_z + at, size)], part_s(at_z.at[pl.ds(at, size)], shelf),
            (2 * half) * 2 + part, shelf, to, (ctrl, 2 * to + half),
        )

    def z_forward(half):
        for part in range(2):
            at, size = chunks[part]
            each(chips, chip, lambda to: z_forward_copy(half, part, to).start())

            @pl.when(core != half)
            def _():
                z_forward_copy(half, part, chip).start()

            @pl.when(core == half)
            def _():
                part_s(at_z.at[pl.ds(at, size)], shelf)[...] = home_z[
                    half, pl.ds(chip * per_z + at, size)
                ]

    def z_forward_sent(half):
        for part in range(2):
            each(chips, chip, lambda to: z_forward_copy(half, part, to).wait_send())

            @pl.when(core != half)
            def _():
                z_forward_copy(half, part, chip).wait_send()

    def z_back_copy(half, part, peer):
        at, size = chunks[part]
        return remote(
            part_s(made_z.at[pl.ds(at, size)], peer),
            back_z.at[half, pl.ds(chip * per_z + at, size)],
            (2 * half + 1) * 2 + part, chip, peer, (ctrl, peer),
        )

    def z_middle(half):
        @pl.when(core == half)
        def _():
            for part in range(2):
                at, size = chunks[part]

                def arrived(peer):
                    remote(
                        home_z.at[half, pl.ds(0, size)], part_s(at_z.at[pl.ds(at, size)], peer),
                        (2 * half) * 2 + part, peer, 0, (ctrl, peer),
                    ).wait_recv()

                each(shelves, shelf, arrived)
                both = jnp.concatenate([at_z[at + n] for n in range(size)], axis=1)
                for m in range(0, shelves * rows_s, 256):
                    made = jnp.dot(shelf_ref[m : m + 256], both, preferred_element_type=jnp.float32)
                    for n in range(size):
                        made_z[at + n, m : m + 256, :] = made[
                            :, n * lanes : (n + 1) * lanes
                        ].astype(jnp.bfloat16)
                each(shelves, shelf, lambda peer: z_back_copy(half, part, peer).start())
                back_z[half, pl.ds(chip * per_z + at, size)] = part_s(
                    made_z.at[pl.ds(at, size)], shelf
                )[...]

    def z_back_from(half, part, source):
        at, size = chunks[part]
        return remote(
            part_s(made_z.at[pl.ds(at, size)], shelf),
            back_z.at[half, pl.ds(source * per_z + at, size)],
            (2 * half + 1) * 2 + part, source, 0, (ctrl, 2 * source + half),
        )

    def z_back_wait(half):
        for part in range(2):
            each(chips, chip, lambda source: z_back_from(half, part, source).wait_recv())

            @pl.when(core != half)
            def _():
                z_back_from(half, part, chip).wait_recv()

    def z_back_sent(half):
        @pl.when(core == half)
        def _():
            for part in range(2):
                each(shelves, shelf, lambda peer: z_back_copy(half, part, peer).wait_send())

    def one_step(repeat, carry):
        for p in range(0, rows_c, 16):
            rounded = state_ref[p : p + 16].astype(jnp.bfloat16).reshape(16 * rows_s, 256)
            made = jnp.dot(rounded, disk_ref[...], preferred_element_type=jnp.float32)
            made = made.astype(jnp.bfloat16).reshape(16, rows_s, 256)
            home_z[1, p : p + 16] = made[:, :, lanes:]
            for q in range(0, rows_s, 16):
                home_y[0, q : q + 16, p : p + 16, :] = swapped(made[:, q : q + 16, :lanes])
        z_forward(1)
        y_forward(0)

        @pl.when(repeat == 0)
        def _():
            gather_rows()
            prepare()

        fill(repeat * 4)
        z_middle(1)
        y_middle(0)
        fill(repeat * 4 + 1)
        y_back_wait(0)
        exchange_rows(back_y.at[0], home_z.at[0])
        z_forward(0)
        z_back_wait(1)
        exchange_rows(back_z.at[1], home_y.at[1])
        y_forward(1)
        fill(repeat * 4 + 2)
        z_middle(0)
        y_middle(1)
        fill(repeat * 4 + 3)
        z_back_wait(0)
        y_back_wait(1)
        z_forward_sent(1)
        exchange_rows(back_y.at[1], home_z.at[1])

        def update(row, inner):
            kept = 1.0 - rate_ref[pl.ds(row, 1), :] * shelf_rate_ref[...]
            third = jnp.concatenate([back_z[0, row], home_z[1, row]], axis=1)
            state_ref[row] = third.astype(jnp.float32) * scale_ref[0:1] + state_ref[row] * kept
            return inner

        lax.fori_loop(0, rows_c, update, 0)
        z_forward_sent(0)
        z_back_sent(0)
        z_back_sent(1)
        return carry

    lax.fori_loop(0, STEPS, one_step, 0)

    lead = lax.broadcasted_iota(jnp.int32, (8, 256), 0) == 0
    sums = jnp.where(lead, 1.0, disk_row[...])
    weight_ref[...] = jnp.zeros_like(weight_ref)
    mass_ref[...] = jnp.zeros_like(mass_ref)
    for r in range(rows_c // 4):
        both = lax.dot_general(
            sums,
            state_ref[4 * r : 4 * r + 4].reshape(4 * rows_s, 256),
            (((1,), (1,)), ((), ())),
            precision=HIGHEST,
            preferred_element_type=jnp.float32,
        )
        mass_ref[r : r + 1] = both[0:1]
        weight_ref[r : r + 1] = both[1:2]
    stages = spread_small(weight_ref[...], by_weight, shelf_stages(), send_w, recv_w)
    lax.fori_loop(1, stages[0][2], stages[0][0], 0)
    kept_ref[...] = jnp.zeros_like(kept_ref)
    ones = jnp.ones((8, 256), jnp.float32)
    for r in range(rows_c // 4):
        part = [
            state_ref[n] * (1.0 - rate_ref[n : n + 1] * shelf_rate_ref[...])
            for n in range(4 * r, 4 * r + 4)
        ]
        kept_ref[r : r + 1] = lax.dot_general(
            ones, jnp.concatenate(part, axis=0), NT,
            precision=HIGHEST, preferred_element_type=jnp.float32,
        )[0:1]
    lax.fori_loop(1, stages[0][2], stages[0][1], 0)
    lax.fori_loop(1, stages[1][2], stages[1][0], 0)
    lax.fori_loop(1, stages[1][2], stages[1][1], 0)
    spread_pairs(by_weight, shelf_wide_rows)
    for z in range(8):
        weight_wide_ref[:, z * lanes : (z + 1) * lanes] = shelf_wide_rows[z, 0:rows_c]
    reduce_part(
        groups,
        shelf_labels_ref, weight_wide_ref, shelf_cols_ref, first_ref, label_ref, mass_ref, kept_ref,
        base_ref, sum_ref, total_ref, part_ref, block_mass_ref, wide, held,
        rows, tiles, highs, deeps, blocks, mass_plane, mass_deep, mass_high, send_r, recv_r,
    )


def spread_pairs(tiles, wide):
    lane = lax.broadcasted_iota(jnp.int32, (16, 128), 1) // 32
    for z in range(8):
        for q in range(4):
            made = jnp.zeros((16, 128), jnp.float32)
            for p in range(4):
                tile = tiles[p, z]
                moved = tile if p == q else pltpu.roll(tile, (32 * (p - q)) % 128, 1)
                made = jnp.where(lane == p, moved, made)
            wide[z, pl.ds(q, 16, stride=4), :] = made


def power_steps(prob, ctrl_rows, shelf_rows, disk, label_tile):
    rows_c, rows_s, _ = prob.shape
    bf, f32 = jnp.bfloat16, jnp.float32
    outs = [(prob.shape, f32), ((NBLK, NBLK), f32), ((8, 128), f32)]
    dma = pltpu.SemaphoreType.DMA
    return pl.pallas_call(
        steps_kernel,
        out_shape=tuple(jax.ShapeDtypeStruct(*out) for out in outs),
        in_specs=[pl.BlockSpec(memory_space=VMEM)] * 5,
        out_specs=tuple([pl.BlockSpec(memory_space=VMEM)] * len(outs)),
        scratch_shapes=[
            pltpu.VMEM((rows_s, rows_c, NBLK), bf),
            pltpu.VMEM((rows_c, SHELF), f32),
            pltpu.VMEM((rows_s, SHELF), f32),
            pltpu.VMEM((rows_c, SHELF), f32),
            pltpu.VMEM((16, 128), f32),
            pltpu.VMEM((16, 128), f32),
            pltpu.VMEM((8, 128), f32),
            pltpu.VMEM((NBLK, NBLK), f32),
            pltpu.VMEM((8, 128), f32),
            pltpu.VMEM((2, 2 * rows_s, SHELF), bf),
            pltpu.VMEM((rows_s, rows_c, NBLK), f32),
            pltpu.VMEM((GROUP, 32, NBLK), f32),
            *[pltpu.VMEM((GROUP, 8, 128), f32)] * 7,
            pltpu.VMEM((16, 128), f32),
            pltpu.VMEM((4, 8, 16, 128), f32),
            pltpu.VMEM((8, 2, 2, 24, CTRL), bf),
            pltpu.VMEM((8, 2, 2, 32, SHELF), bf),
            pltpu.VMEM((4, 8, 16, 128), f32),
            pltpu.VMEM((2, 8, 16, 128), f32),
            pltpu.VMEM((CTRL, CTRL), f32),
            pltpu.VMEM((rows_c, CTRL), bf),
            pltpu.VMEM((CTRL, CTRL), bf),
            pltpu.VMEM((SHELF, SHELF), bf),
            pltpu.VMEM((DISK, DISK), bf),
            pltpu.VMEM((16, 64, 128), f32),
            pltpu.VMEM((8, 64, 128), f32),
            pltpu.VMEM((rows_s, CTRL), f32),
            pltpu.VMEM((rows_c, DISK), f32),
            pltpu.VMEM((rows_s, DISK), f32),
            pltpu.VMEM((8, DISK), f32),
            pltpu.VMEM((8, DISK), f32),
            pltpu.VMEM((2, rows_s, rows_c, 128), bf),
            pltpu.VMEM((2, rows_c, rows_s, 128), bf),
            pltpu.VMEM((2, 2, CTRL, 128), bf),
            pltpu.VMEM((2, 2, CTRL, 128), bf),
            pltpu.VMEM((3, SHELF, 128), bf),
            pltpu.VMEM((3, SHELF, 128), bf),
            pltpu.VMEM((2, rows_s, rows_c, 128), bf),
            pltpu.VMEM((2, rows_c, rows_s, 128), bf),
            dma((2,)), dma((2,)), dma((2, 2, 4)), dma((2, 2, 4)), dma((2, 8)), dma((2, 8)),
            dma((2, 8)), dma((2, 8)), dma((2, 8)), dma((2, 8)), dma((2, 8)), dma((2, 8)),
            dma((2, 2, 2, 16)), dma((2, 2, 2, 16)), dma((8, 32)), dma((8, 32)),
            dma((5, 2, GROUP)), dma((5, 2, GROUP)),
        ],
        compiler_params=pltpu.CompilerParams(
            collective_id=4, has_side_effects=True, vmem_limit_bytes=56 << 20
        ),
        name="power_steps",
    )(prob, ctrl_rows, shelf_rows, disk, label_tile)


def local(prob, ctrl_rates, shelf_rates, disk_rates, labels):
    label_tile = as_tile(labels.astype(jnp.float32))
    iterate, numer, total = power_steps(prob, ctrl_rates, shelf_rates, disk_rates, label_tile)
    refined, coarse = balance_of(numer, total, label_tile, iterate)
    return (refined, coarse[0])


def solution(mesh):
    placed = (P("ctrl", "shelf", None), P("shelf", None), P("shelf", None), P(), P("ctrl", "shelf"))
    return jax.shard_map(
        local,
        mesh=mesh,
        in_specs=placed,
        out_specs=(P("ctrl", "shelf", None), P()),
        check_vma=False,
    )
```

```python
import functools

import jax
import jax.numpy as jnp
from jax import lax
from jax.experimental import pallas as pl
from jax.experimental.pallas import tpu as pltpu
from jax.sharding import PartitionSpec as P

CTRL = 768
SHELF = 1024
DISK = 256
NBLK = 256
STEPS = 2
GROUP = 8
MESH = pl.DeviceIdType.MESH
VMEM = pltpu.MemorySpace.VMEM
HIGHEST = lax.Precision.HIGHEST


def place():
    ctrl = lax.axis_index("ctrl")
    shelf = lax.axis_index("shelf")
    plane_me = (ctrl % 2) * 4 + shelf % 4
    deep_me = shelf // 4
    high_me = ctrl // 2

    def plane(member):
        return (ctrl - ctrl % 2 + member // 4, shelf - shelf % 4 + member % 4)

    def deep(member):
        return (ctrl, member * 4 + shelf % 4)

    def high(member):
        return (member * 2 + ctrl % 2, shelf)

    return (plane_me, plane), (deep_me, deep), (high_me, high)


def exchange(group, streams, send_sem, recv_sem):
    me, peer = group

    def copy(step, index):
        source, target = streams[index]
        member = (me + step) % GROUP
        return pltpu.make_async_remote_copy(
            src_ref=source(member),
            dst_ref=target,
            send_sem=send_sem.at[index, step],
            recv_sem=recv_sem.at[index, step],
            device_id=peer(member),
            device_id_type=MESH,
        )

    def start(step, carry):
        for index in range(len(streams)):
            copy(step, index).start()
        return carry

    def finish(step, carry):
        for index in range(len(streams)):
            copy(step, index).wait()
        return carry

    lax.fori_loop(1, GROUP, start, 0)
    lax.fori_loop(1, GROUP, finish, 0)


NT = (((1,), (1,)), ((), ()))


def flow_part(labels_ref, weight_ref, factor_ref, first_ref, out_ref, wide, held):
    count = labels_ref.shape[1]
    depth = factor_ref.shape[0]
    blocks = lax.broadcasted_iota(jnp.int32, (NBLK, count), 0).astype(jnp.float32)

    def body(row, carry):
        names = jnp.broadcast_to(labels_ref[pl.ds(row, 1), :], (NBLK, count))
        member = jnp.where(names == blocks, 1.0, 0.0).astype(jnp.bfloat16)
        scaled = factor_ref[...] * weight_ref[pl.ds(row, 1), :]
        upper = scaled.astype(jnp.bfloat16)
        slot = row % 2
        wide[slot, 0:depth, :] = upper
        wide[slot, depth : 2 * depth, :] = (scaled - upper.astype(jnp.float32)).astype(jnp.bfloat16)
        both = lax.dot_general(wide[slot], member, NT, preferred_element_type=jnp.float32)
        held[:, pl.ds(row, 1), :] = (both[0:depth] + both[depth:]).reshape(depth, 1, NBLK)
        return carry

    lax.fori_loop(0, labels_ref.shape[0], body, 0, unroll=2)
    rows = held.shape[0] * held.shape[1]
    mine = held[...].reshape(rows, NBLK)
    first = first_ref[...].reshape(rows, NBLK)
    upper = mine.astype(jnp.bfloat16)
    lower = (mine - upper.astype(jnp.float32)).astype(jnp.bfloat16)
    dims = (((0,), (0,)), ((), ()))
    out_ref[...] = lax.dot_general(
        upper, first, dims, preferred_element_type=jnp.float32
    ) + lax.dot_general(lower, first, dims, preferred_element_type=jnp.float32)


def block_terms(label_ref, pair_mass_ref, pair_kept_ref):
    line = lax.broadcasted_iota(jnp.int32, (8, 128), 0)
    names = lax.broadcasted_iota(jnp.int32, (NBLK, 128), 0).astype(jnp.float32)
    terms = jnp.zeros((8, NBLK), jnp.float32)
    for r in range(12):
        have = jnp.broadcast_to(label_ref[r : r + 1], (NBLK, 128))
        member = jnp.where(have == names, 1.0, 0.0)
        pair = jnp.where(line == 0, pair_mass_ref[r : r + 1], 0.0)
        pair = jnp.where(line == 1, pair_kept_ref[r : r + 1], pair)
        terms += lax.dot_general(
            pair, member, NT, precision=HIGHEST, preferred_element_type=jnp.float32
        )
    return terms


def reduce_part(
    groups,
    labels_ref, weight_ref, factor_ref, first_ref, label_ref, pair_mass_ref, pair_kept_ref, base_ref,
    sum_ref, total_ref,
    part_ref, mass_ref, wide, held,
    rows, tiles, highs, deeps, blocks, mass_plane, mass_deep, mass_high,
    send_sem, recv_sem,
):
    plane, deep, high = groups
    plane_me, deep_me, high_me = plane[0], deep[0], high[0]

    flow_part(labels_ref, weight_ref, factor_ref, first_ref, part_ref, wide, held)
    terms = block_terms(label_ref, pair_mass_ref, pair_kept_ref)
    mass_ref[...] = jnp.zeros_like(mass_ref)
    mass_ref[0:1] = terms[0:1, 0:128]
    mass_ref[1:2] = terms[0:1, 128:256]
    row = lax.broadcasted_iota(jnp.int32, (NBLK, NBLK), 0)
    column = lax.broadcasted_iota(jnp.int32, (NBLK, NBLK), 1)
    kept = jnp.where(row == column, jnp.broadcast_to(terms[1:2], (NBLK, NBLK)), 0.0)
    part_ref[...] = part_ref[...] / base_ref[0:1, 0:1] + kept

    exchange(
        plane,
        (
            (lambda m: part_ref.at[pl.ds(pl.multiple_of(m * 32, 32), 32)], rows.at[plane_me]),
            (lambda m: mass_ref, mass_plane.at[plane_me]),
        ),
        send_sem.at[0], recv_sem.at[0],
    )
    rows[plane_me] = part_ref[pl.ds(pl.multiple_of(plane_me * 32, 32), 32)]
    mass_plane[plane_me] = mass_ref[...]
    mine = jnp.sum(rows[...], axis=0)
    for tile in range(GROUP):
        r, h = tile // 2, tile % 2
        tiles[tile] = mine[r * 8 : r * 8 + 8, h * 128 : h * 128 + 128]
    total_ref[...] = jnp.sum(mass_plane[...], axis=0)

    exchange(
        deep,
        (
            (lambda m: tiles.at[m], deeps.at[deep_me]),
            (lambda m: total_ref, mass_deep.at[deep_me]),
        ),
        send_sem.at[1], recv_sem.at[1],
    )
    deeps[deep_me] = tiles[deep_me]
    mass_deep[deep_me] = total_ref[...]
    highs[high_me] = jnp.sum(deeps[...], axis=0)
    mass_high[high_me] = jnp.sum(mass_deep[...], axis=0)

    exchange(
        high,
        (
            (lambda m: highs.at[high_me], highs.at[high_me]),
            (lambda m: mass_high.at[high_me], mass_high.at[high_me]),
        ),
        send_sem.at[2], recv_sem.at[2],
    )
    total_ref[...] = jnp.sum(mass_high[...], axis=0)
    blocks[deep_me] = jnp.sum(highs[...], axis=0)

    exchange(
        deep,
        ((lambda m: blocks.at[deep_me], blocks.at[deep_me]),),
        send_sem.at[3], recv_sem.at[3],
    )
    for tile in range(GROUP):
        r, h = tile // 2, tile % 2
        sum_ref[
            pl.ds(pl.multiple_of(plane_me * 32 + r * 8, 8), 8), h * 128 : h * 128 + 128
        ] = blocks[tile]
    own = sum_ref.at[pl.ds(pl.multiple_of(plane_me * 32, 32), 32)]
    exchange(plane, ((lambda m: own, own),), send_sem.at[4], recv_sem.at[4])


def balance_kernel(numer_ref, total_ref, label_ref, state_ref, refined_ref, coarse_ref, power, spread, held, sem):
    load = pltpu.make_async_copy(state_ref, held, sem)
    load.start()
    size = NBLK
    line = lax.broadcasted_iota(jnp.int32, (size, size), 0)
    column = lax.broadcasted_iota(jnp.int32, (size, size), 1)
    mass = jnp.concatenate([total_ref[0:1], total_ref[1:2]], axis=1)
    mass_column = jnp.sum(
        jnp.where(line == column, jnp.broadcast_to(mass, (size, size)), 0.0), axis=1, keepdims=True
    )
    power[...] = numer_ref[...] / mass_column - 1.0 / size
    start = jnp.full((8, size), 1.0 / size, jnp.float32)

    def going(state):
        turn, height, row = state
        return jnp.logical_and(turn < 40, height > 1e-10)

    def turn_once(state):
        turn, height, row = state
        now = power[...]
        row = row + jnp.dot(row, now, precision=HIGHEST, preferred_element_type=jnp.float32)
        after = jnp.dot(now, now, precision=HIGHEST, preferred_element_type=jnp.float32)
        power[...] = after
        return turn + 1, jnp.max(jnp.abs(after)), row

    state = (jnp.int32(0), jnp.max(jnp.abs(power[...])), start)
    balance = lax.while_loop(going, turn_once, state)[2]
    coarse_ref[...] = balance * float(size)

    share = balance[0:1] / mass
    spread[...] = jnp.zeros_like(spread)
    for q in range(4):
        tile = label_ref[...]
        spread[pl.ds(q, 16, stride=4), :] = tile if q == 0 else pltpu.roll(tile, 128 - 32 * q, 1)
    names = jnp.transpose(spread[...])[0:32]
    lane = lax.broadcasted_iota(jnp.int32, (32, size), 1).astype(jnp.float32)
    load.wait()
    for a in range(held.shape[0]):
        picked = jnp.where(names[:, a : a + 1] == lane, share, 0.0)
        factor = jnp.sum(picked, axis=1, keepdims=True)
        refined_ref[a] = held[a] * factor * float(CTRL * SHELF * DISK)


def balance_of(numer, total, label_tile, state):
    return pl.pallas_call(
        balance_kernel,
        out_shape=(
            jax.ShapeDtypeStruct(state.shape, jnp.float32),
            jax.ShapeDtypeStruct((8, NBLK), jnp.float32),
        ),
        in_specs=[pl.BlockSpec(memory_space=VMEM)] * 3 + [pl.BlockSpec(memory_space=pl.ANY)],
        out_specs=(pl.BlockSpec(memory_space=VMEM), pl.BlockSpec(memory_space=VMEM)),
        scratch_shapes=[
            pltpu.VMEM((NBLK, NBLK), jnp.float32),
            pltpu.VMEM((128, 128), jnp.float32),
            pltpu.VMEM(state.shape, jnp.float32),
            pltpu.SemaphoreType.DMA,
        ],
        compiler_params=pltpu.CompilerParams(vmem_limit_bytes=32 << 20),
        name="balance",
    )(numer, total, label_tile, state)


def spread_small(own, wide, stages, send_sem, recv_sem):
    (outer_me, outer_size, outer_peer), (inner_me, inner_size, inner_peer) = stages

    def stage(which, me, size, peer, piece):
        def copy(step):
            return pltpu.make_async_remote_copy(
                src_ref=piece,
                dst_ref=piece,
                send_sem=send_sem.at[which, step],
                recv_sem=recv_sem.at[which, step],
                device_id=peer((me + step) % size),
                device_id_type=MESH,
            )

        def start(step, carry):
            copy(step).start()
            return carry

        def finish(step, carry):
            copy(step).wait()
            return carry

        return start, finish, size

    wide[inner_me, outer_me] = own
    first = stage(0, outer_me, outer_size, outer_peer, wide.at[inner_me, outer_me])
    second = stage(1, inner_me, inner_size, inner_peer, wide.at[inner_me])
    return first, second


def shelf_stages():
    ctrl = lax.axis_index("ctrl")
    shelf = lax.axis_index("shelf")
    return (
        (shelf // 4, 8, lambda m: (ctrl, m * 4 + shelf % 4)),
        (shelf % 4, 4, lambda m: (ctrl, shelf - shelf % 4 + m)),
    )


def ctrl_stages():
    ctrl = lax.axis_index("ctrl")
    shelf = lax.axis_index("shelf")
    return (
        (ctrl // 2, 8, lambda m: (m * 2 + ctrl % 2, shelf)),
        (ctrl % 2, 2, lambda m: (ctrl - ctrl % 2 + m, shelf)),
    )


def as_tile(values):
    return jnp.pad(values.reshape(12, 128), ((0, 4), (0, 0)))


def steps_kernel(
    prob_ref, ctrl_rows_ref, shelf_rows_ref, disk_in_ref, label_ref,
    state_ref, sum_ref, total_ref,
    first_ref, shelf_labels_ref, shelf_cols_ref, weight_wide_ref, mass_ref, kept_ref, base_ref,
    part_ref, block_mass_ref, wide, held,
    rows, tiles, highs, deeps, blocks, mass_plane, mass_deep, mass_high,
    weight_ref, by_weight,
    ctrl_all, shelf_all, by_shelf, by_ctrl, ctrl_wide, ctrl_own, ctrl_ref, shelf_ref, disk_ref,
    label_rows, shelf_wide_rows, ctrl_labels, rate_ref, shelf_rate_ref, scale_ref, disk_row,
    home_y, home_z, at_y, made_y, at_z, made_z, back_y, back_z,
    swap_send, swap_recv, ring_send, ring_recv, pair_send, pair_recv,
    send_a, recv_a, send_b, recv_b, send_w, recv_w, send_y, recv_y, send_sem, recv_sem,
    send_r, recv_r,
):
    ctrl = lax.axis_index("ctrl")
    shelf = lax.axis_index("shelf")
    chip, core = shelf // 2, shelf % 2
    ctrls, shelves = 16, 32
    chips = shelves // 2
    rows_c, rows_s = state_ref.shape[0], state_ref.shape[1]
    per_y, per_z = rows_s // ctrls, rows_c // chips
    lanes = 128

    barrier = pltpu.get_barrier_semaphore()

    def signal_y(step, carry):
        target = ((ctrl + step) % ctrls, shelf)
        pl.semaphore_signal(barrier, inc=1, device_id=target, device_id_type=MESH)
        return carry

    def signal_z(step, carry):
        target = (ctrl, (shelf + step) % shelves)
        pl.semaphore_signal(barrier, inc=1, device_id=target, device_id_type=MESH)
        return carry

    lax.fori_loop(1, ctrls, signal_y, 0)
    lax.fori_loop(1, shelves, signal_z, 0)
    groups = place()
    plane_me, plane_peer = groups[0]

    def signal_plane(step, carry):
        target = plane_peer((plane_me + step) % GROUP)
        pl.semaphore_signal(barrier, inc=1, device_id=target, device_id_type=MESH)
        return carry

    lax.fori_loop(1, GROUP, signal_plane, 0)
    state_ref[...] = prob_ref[...]
    disk_ref[...] = disk_in_ref[...].astype(jnp.bfloat16)
    deep, side = shelf // 4, (shelf // 2) % 2
    wides = (ctrl_all, shelf_all)
    ctrl_all[deep, side, core] = ctrl_rows_ref[...].astype(jnp.bfloat16)
    shelf_all[deep, side, core] = shelf_rows_ref[...].astype(jnp.bfloat16)
    label_a = spread_small(label_ref[...], by_shelf, shelf_stages(), send_a, recv_a)
    label_b = spread_small(label_ref[...], by_ctrl, ctrl_stages(), send_b, recv_b)

    order = lax.broadcasted_iota(jnp.int32, (256, 256), 0)
    other = lax.broadcasted_iota(jnp.int32, (256, 256), 1)
    swap = jnp.where(
        jnp.logical_and(order // 16 == other % 16, order % 16 == other // 16), 1.0, 0.0
    ).astype(jnp.bfloat16)
    pl.semaphore_wait(barrier, ctrls - 1 + shelves - 1 + GROUP - 1)

    def along_shelf(piece, send, recv, target):
        return pltpu.make_async_remote_copy(
            src_ref=piece, dst_ref=piece, send_sem=send, recv_sem=recv,
            device_id=(ctrl, target), device_id_type=MESH,
        )

    swaps = [
        along_shelf(
            wide.at[deep, side, core], swap_send.at[n], swap_recv.at[n], shelf + 2 - 4 * side
        )
        for n, wide in enumerate(wides)
    ]
    for copy in swaps:
        copy.start()
    for start, _, size in (label_a[0], label_b[0]):
        lax.fori_loop(1, size, start, 0)

    right = ((deep + 1) % 8) * 4 + shelf % 4
    left = ((deep + 7) % 8) * 4 + shelf % 4
    sibling = shelf + 1 - 2 * core

    def pair(n, block, side_core):
        piece = wides[n].at[block, :, side_core]
        return along_shelf(piece, pair_send.at[n, block], pair_recv.at[n, block], sibling)

    def hop(n, way, count):
        block = (deep + 8 - count + 1) % 8 if way == 0 else (deep + count - 1) % 8
        return along_shelf(
            wides[n].at[block, :, core],
            ring_send.at[n, way, count - 1],
            ring_recv.at[n, way, count - 1],
            right if way == 0 else left,
        )

    def used(n, way, count):
        return count < 4 or n == way

    def gather_rows():
        for copy in swaps:
            copy.wait()
        for n in range(2):
            for way in range(2):
                hop(n, way, 1).start()
            pair(n, deep, core).start()
        for _, finish, size in (label_a[0], label_b[0]):
            lax.fori_loop(1, size, finish, 0)
        for start, _, size in (label_a[1], label_b[1]):
            lax.fori_loop(1, size, start, 0)
        for count in range(1, 5):
            for n in range(2):
                for way in range(2):
                    if not used(n, way, count):
                        continue
                    hop(n, way, count).wait_recv()
                    if count < 4 and used(n, way, count + 1):
                        hop(n, way, count + 1).start()
                    pair(n, (deep + 8 - count) % 8 if way == 0 else (deep + count) % 8, core).start()
        for _, finish, size in (label_a[1], label_b[1]):
            lax.fori_loop(1, size, finish, 0)
        for count in range(1, 5):
            for n in range(2):
                for way in range(2):
                    if used(n, way, count):
                        hop(n, way, count).wait_send()

        def settle(block, carry):
            for n in range(2):
                pair(n, block, 1 - core).wait_recv()
                pair(n, block, core).wait_send()
            return carry

        lax.fori_loop(0, 8, settle, 0)

    def prepare():
        unit = jnp.where(order == other, 1.0, 0.0).astype(jnp.bfloat16)
        dims = (((1,), (1,)), ((), ()))
        for n in range(shelves):
            wide = ctrl_all[n // 4, (n // 2) % 2, n % 2].astype(jnp.float32)
            ctrl_wide[n * 24 : n * 24 + 24] = wide
        for m in range(0, CTRL, 256):
            block = ctrl_wide[:, m : m + 256].astype(jnp.bfloat16)
            turned = lax.dot_general(unit, block, dims, preferred_element_type=jnp.float32)
            ctrl_ref[m : m + 256] = turned.astype(jnp.bfloat16)
        shelf_sum = jnp.zeros((SHELF, 1), jnp.float32)
        for m in range(0, SHELF, 256):
            block = shelf_all[:, :, :, :, m : m + 256].reshape(SHELF, 256)
            turned = lax.dot_general(unit, block, dims, preferred_element_type=jnp.float32)
            shelf_ref[m : m + 256] = turned.astype(jnp.bfloat16)
            shelf_sum += jnp.sum(block.astype(jnp.float32), axis=1, keepdims=True)
        shelf_cols_ref[...] = shelf_ref[
            pl.ds(pl.multiple_of(shelf * rows_s, 16), rows_s)
        ].astype(jnp.float32)

        ctrl_max = jnp.max(
            jnp.sum(ctrl_wide[...], axis=1, keepdims=True), axis=0, keepdims=True
        )
        shelf_max = jnp.max(shelf_sum, axis=0, keepdims=True)
        ones = jnp.ones((8, 256), jnp.bfloat16)
        disk_sum = lax.dot_general(ones, disk_ref[...], dims, preferred_element_type=jnp.float32)
        disk_max = jnp.max(disk_sum[0:1], axis=1, keepdims=True)
        base = 1.05 * (ctrl_max * shelf_max) * disk_max
        own_rows = ctrl_wide[pl.ds(pl.multiple_of(ctrl * rows_c, 8), rows_c)]
        ctrl_own[...] = own_rows.astype(jnp.bfloat16)
        own_c = jnp.sum(own_rows, axis=1, keepdims=True)
        own_s = jnp.sum(
            shelf_rows_ref[...].astype(jnp.bfloat16).astype(jnp.float32), axis=1, keepdims=True
        )
        rate_ref[...] = own_c * disk_sum[0:1] / base
        shelf_rate_ref[...] = jnp.broadcast_to(own_s, (rows_s, 256))
        scale_ref[...] = jnp.broadcast_to(1.0 / base, (8, 256))
        disk_row[...] = disk_sum
        base_ref[...] = jnp.broadcast_to(base, (8, lanes))

        spread_pairs(by_shelf, shelf_wide_rows)
        for z in range(8):
            shelf_labels_ref[:, z * lanes : (z + 1) * lanes] = shelf_wide_rows[z, 0:rows_c]
        for i in range(ctrls):
            tile = by_ctrl[i % 2, i // 2]
            for q in range(4):
                moved = tile if q == 0 else pltpu.roll(tile, lanes - 32 * q, 1)
                label_rows[i, pl.ds(q, 16, stride=4), :] = moved
        turned = jnp.transpose(label_rows[:, 0:rows_c, :].reshape(CTRL, lanes))
        ctrl_labels[...] = turned[0:rows_s]

    names = lax.broadcasted_iota(jnp.int32, (NBLK, CTRL), 0).astype(jnp.float32)

    def fill(slot):
        part = rows_s // 8

        def body(row, carry):
            have = jnp.broadcast_to(ctrl_labels[pl.ds(row, 1), :], (NBLK, CTRL))
            member = jnp.where(have == names, 1.0, 0.0).astype(jnp.bfloat16)
            first_ref[row] = lax.dot_general(
                ctrl_own[...], member, (((1,), (1,)), ((), ())), preferred_element_type=jnp.float32
            ).astype(first_ref.dtype)
            return carry

        lax.fori_loop(slot * part, slot * part + part, body, 0)

    def exchange_rows(source, target):
        first, second = source.shape[0], source.shape[1]
        blocks = [(p, q) for p in range(0, first, 16) for q in range(0, second, 16)]
        for n in range(0, len(blocks), 2):
            pieces = [
                source[p : p + 16, q : q + 16, :].reshape(256, lanes) for p, q in blocks[n : n + 2]
            ]
            flat = jnp.dot(
                swap, jnp.concatenate(pieces, axis=1), preferred_element_type=jnp.float32
            ).astype(jnp.bfloat16)
            for m, (p, q) in enumerate(blocks[n : n + 2]):
                target[q : q + 16, p : p + 16, :] = flat[:, m * lanes : (m + 1) * lanes].reshape(
                    16, 16, lanes
                )

    def part_s(ref, owner):
        return ref.at[:, pl.ds(pl.multiple_of(owner * rows_s, 16), rows_s), :]

    def remote(source, target, stream, mine, theirs, device):
        return pltpu.make_async_remote_copy(
            src_ref=source, dst_ref=target,
            send_sem=send_sem.at[stream, theirs], recv_sem=recv_sem.at[stream, mine],
            device_id=device, device_id_type=MESH,
        )

    def remote_y(source, target, half, way, n, mine, peer):
        return pltpu.make_async_remote_copy(
            src_ref=source, dst_ref=target,
            send_sem=send_y.at[half, way, n, peer], recv_sem=recv_y.at[half, way, n, mine],
            device_id=(peer, shelf), device_id_type=MESH,
        )

    def each(count, first, act):
        def body(step, carry):
            act((first + step) % count)
            return carry

        lax.fori_loop(1, count, body, 0)

    def rows_of(ref, owner):
        return ref.at[pl.ds(pl.multiple_of(owner * rows_c, 16), rows_c), :]

    def y_forward(half):
        for n in range(per_y):

            def act(peer, n=n):
                remote_y(
                    home_y.at[half, peer * per_y + n], rows_of(at_y.at[half, n], ctrl),
                    half, 0, n, ctrl, peer,
                ).start()

            each(ctrls, ctrl, act)
            rows_of(at_y.at[half, n], ctrl)[...] = home_y[half, ctrl * per_y + n]

    def y_middle(half):
        for n in range(per_y):

            def arrived(peer, n=n):
                remote_y(
                    home_y.at[half, peer * per_y + n], rows_of(at_y.at[half, n], peer),
                    half, 0, n, peer, peer,
                ).wait()

            each(ctrls, ctrl, arrived)
            for m in range(0, ctrls * rows_c, 256):
                made = jnp.dot(
                    ctrl_ref[m : m + 256], at_y[half, n], preferred_element_type=jnp.float32
                )
                made_y[half, n, m : m + 256, :] = made.astype(jnp.bfloat16)

            def act(peer, n=n):
                remote_y(
                    rows_of(made_y.at[half, n], peer), back_y.at[half, ctrl * per_y + n],
                    half, 1, n, ctrl, peer,
                ).start()

            each(ctrls, ctrl, act)
            back_y[half, ctrl * per_y + n] = rows_of(made_y.at[half, n], ctrl)[...]

    def y_back_wait(half):
        for n in range(per_y):

            def act(peer, n=n):
                remote_y(
                    rows_of(made_y.at[half, n], peer), back_y.at[half, peer * per_y + n],
                    half, 1, n, peer, peer,
                ).wait()

            each(ctrls, ctrl, act)

    chunks = ((0, 2), (2, 1))

    def z_forward_copy(half, part, to):
        at, size = chunks[part]
        return remote(
            home_z.at[half, pl.ds(to * per_z + at, size)], part_s(at_z.at[pl.ds(at, size)], shelf),
            (2 * half) * 2 + part, shelf, to, (ctrl, 2 * to + half),
        )

    def z_forward(half):
        for part in range(2):
            at, size = chunks[part]
            each(chips, chip, lambda to: z_forward_copy(half, part, to).start())

            @pl.when(core != half)
            def _():
                z_forward_copy(half, part, chip).start()

            @pl.when(core == half)
            def _():
                part_s(at_z.at[pl.ds(at, size)], shelf)[...] = home_z[
                    half, pl.ds(chip * per_z + at, size)
                ]

    def z_forward_sent(half):
        for part in range(2):
            each(chips, chip, lambda to: z_forward_copy(half, part, to).wait_send())

            @pl.when(core != half)
            def _():
                z_forward_copy(half, part, chip).wait_send()

    def z_back_copy(half, part, peer):
        at, size = chunks[part]
        return remote(
            part_s(made_z.at[pl.ds(at, size)], peer),
            back_z.at[half, pl.ds(chip * per_z + at, size)],
            (2 * half + 1) * 2 + part, chip, peer, (ctrl, peer),
        )

    def z_middle(half):
        @pl.when(core == half)
        def _():
            for part in range(2):
                at, size = chunks[part]

                def arrived(peer):
                    remote(
                        home_z.at[half, pl.ds(0, size)], part_s(at_z.at[pl.ds(at, size)], peer),
                        (2 * half) * 2 + part, peer, 0, (ctrl, peer),
                    ).wait_recv()

                each(shelves, shelf, arrived)
                both = jnp.concatenate([at_z[at + n] for n in range(size)], axis=1)
                for m in range(0, shelves * rows_s, 256):
                    made = jnp.dot(shelf_ref[m : m + 256], both, preferred_element_type=jnp.float32)
                    for n in range(size):
                        made_z[at + n, m : m + 256, :] = made[
                            :, n * lanes : (n + 1) * lanes
                        ].astype(jnp.bfloat16)
                each(shelves, shelf, lambda peer: z_back_copy(half, part, peer).start())
                back_z[half, pl.ds(chip * per_z + at, size)] = part_s(
                    made_z.at[pl.ds(at, size)], shelf
                )[...]

    def z_back_from(half, part, source):
        at, size = chunks[part]
        return remote(
            part_s(made_z.at[pl.ds(at, size)], shelf),
            back_z.at[half, pl.ds(source * per_z + at, size)],
            (2 * half + 1) * 2 + part, source, 0, (ctrl, 2 * source + half),
        )

    def z_back_wait(half):
        for part in range(2):
            each(chips, chip, lambda source: z_back_from(half, part, source).wait_recv())

            @pl.when(core != half)
            def _():
                z_back_from(half, part, chip).wait_recv()

    def z_back_sent(half):
        @pl.when(core == half)
        def _():
            for part in range(2):
                each(shelves, shelf, lambda peer: z_back_copy(half, part, peer).wait_send())

    def one_step(repeat, carry):
        for p in range(0, rows_c, 16):
            rounded = state_ref[p : p + 16].astype(jnp.bfloat16).reshape(16 * rows_s, 256)
            made = jnp.dot(rounded, disk_ref[...], preferred_element_type=jnp.float32)
            made = made.astype(jnp.bfloat16).reshape(16, rows_s, 256)
            home_z[1, p : p + 16] = made[:, :, lanes:]
            home_z[0, p : p + 16] = made[:, :, :lanes]
        z_forward(1)
        exchange_rows(home_z.at[0], home_y.at[0])
        y_forward(0)

        @pl.when(repeat == 0)
        def _():
            gather_rows()
            prepare()

        fill(repeat * 4)
        z_middle(1)
        y_middle(0)
        fill(repeat * 4 + 1)
        y_back_wait(0)
        exchange_rows(back_y.at[0], home_z.at[0])
        z_forward(0)
        z_back_wait(1)
        exchange_rows(back_z.at[1], home_y.at[1])
        y_forward(1)
        z_middle(0)
        y_middle(1)
        fill(repeat * 4 + 2)
        fill(repeat * 4 + 3)
        y_back_wait(1)
        z_forward_sent(1)
        exchange_rows(back_y.at[1], home_z.at[1])
        z_back_wait(0)

        def update(row, inner):
            kept = 1.0 - rate_ref[pl.ds(row, 1), :] * shelf_rate_ref[...]
            third = jnp.concatenate([back_z[0, row], home_z[1, row]], axis=1)
            state_ref[row] = third.astype(jnp.float32) * scale_ref[0:1] + state_ref[row] * kept
            return inner

        lax.fori_loop(0, rows_c, update, 0, unroll=4)
        z_forward_sent(0)
        z_back_sent(0)
        z_back_sent(1)
        return carry

    lax.fori_loop(0, STEPS, one_step, 0)

    lead = lax.broadcasted_iota(jnp.int32, (8, 256), 0) == 0
    sums = jnp.where(lead, 1.0, disk_row[...])
    weight_ref[...] = jnp.zeros_like(weight_ref)
    mass_ref[...] = jnp.zeros_like(mass_ref)
    for r in range(rows_c // 4):
        both = lax.dot_general(
            sums,
            state_ref[4 * r : 4 * r + 4].reshape(4 * rows_s, 256),
            (((1,), (1,)), ((), ())),
            precision=HIGHEST,
            preferred_element_type=jnp.float32,
        )
        mass_ref[r : r + 1] = both[0:1]
        weight_ref[r : r + 1] = both[1:2]
    stages = spread_small(weight_ref[...], by_weight, shelf_stages(), send_w, recv_w)
    lax.fori_loop(1, stages[0][2], stages[0][0], 0)
    kept_ref[...] = jnp.zeros_like(kept_ref)
    ones = jnp.ones((8, 256), jnp.float32)
    for r in range(rows_c // 4):
        part = [
            state_ref[n] * (1.0 - rate_ref[n : n + 1] * shelf_rate_ref[...])
            for n in range(4 * r, 4 * r + 4)
        ]
        kept_ref[r : r + 1] = lax.dot_general(
            ones, jnp.concatenate(part, axis=0), NT,
            precision=HIGHEST, preferred_element_type=jnp.float32,
        )[0:1]
    lax.fori_loop(1, stages[0][2], stages[0][1], 0)
    lax.fori_loop(1, stages[1][2], stages[1][0], 0)
    lax.fori_loop(1, stages[1][2], stages[1][1], 0)
    spread_pairs(by_weight, shelf_wide_rows)
    for z in range(8):
        weight_wide_ref[:, z * lanes : (z + 1) * lanes] = shelf_wide_rows[z, 0:rows_c]
    reduce_part(
        groups,
        shelf_labels_ref, weight_wide_ref, shelf_cols_ref, first_ref, label_ref, mass_ref, kept_ref,
        base_ref, sum_ref, total_ref, part_ref, block_mass_ref, wide, held,
        rows, tiles, highs, deeps, blocks, mass_plane, mass_deep, mass_high, send_r, recv_r,
    )


def spread_pairs(tiles, wide):
    lane = lax.broadcasted_iota(jnp.int32, (16, 128), 1) // 32
    for z in range(8):
        for q in range(4):
            made = jnp.zeros((16, 128), jnp.float32)
            for p in range(4):
                tile = tiles[p, z]
                moved = tile if p == q else pltpu.roll(tile, (32 * (p - q)) % 128, 1)
                made = jnp.where(lane == p, moved, made)
            wide[z, pl.ds(q, 16, stride=4), :] = made


def power_steps(prob, ctrl_rows, shelf_rows, disk, label_tile):
    rows_c, rows_s, _ = prob.shape
    bf, f32 = jnp.bfloat16, jnp.float32
    outs = [(prob.shape, f32), ((NBLK, NBLK), f32), ((8, 128), f32)]
    dma = pltpu.SemaphoreType.DMA
    return pl.pallas_call(
        steps_kernel,
        out_shape=tuple(jax.ShapeDtypeStruct(*out) for out in outs),
        in_specs=[pl.BlockSpec(memory_space=VMEM)] * 5,
        out_specs=tuple([pl.BlockSpec(memory_space=VMEM)] * len(outs)),
        scratch_shapes=[
            pltpu.VMEM((rows_s, rows_c, NBLK), bf),
            pltpu.VMEM((rows_c, SHELF), f32),
            pltpu.VMEM((rows_s, SHELF), f32),
            pltpu.VMEM((rows_c, SHELF), f32),
            pltpu.VMEM((16, 128), f32),
            pltpu.VMEM((16, 128), f32),
            pltpu.VMEM((8, 128), f32),
            pltpu.VMEM((NBLK, NBLK), f32),
            pltpu.VMEM((8, 128), f32),
            pltpu.VMEM((2, 2 * rows_s, SHELF), bf),
            pltpu.VMEM((rows_s, rows_c, NBLK), f32),
            pltpu.VMEM((GROUP, 32, NBLK), f32),
            *[pltpu.VMEM((GROUP, 8, 128), f32)] * 7,
            pltpu.VMEM((16, 128), f32),
            pltpu.VMEM((4, 8, 16, 128), f32),
            pltpu.VMEM((8, 2, 2, 24, CTRL), bf),
            pltpu.VMEM((8, 2, 2, 32, SHELF), bf),
            pltpu.VMEM((4, 8, 16, 128), f32),
            pltpu.VMEM((2, 8, 16, 128), f32),
            pltpu.VMEM((CTRL, CTRL), f32),
            pltpu.VMEM((rows_c, CTRL), bf),
            pltpu.VMEM((CTRL, CTRL), bf),
            pltpu.VMEM((SHELF, SHELF), bf),
            pltpu.VMEM((DISK, DISK), bf),
            pltpu.VMEM((16, 64, 128), f32),
            pltpu.VMEM((8, 64, 128), f32),
            pltpu.VMEM((rows_s, CTRL), f32),
            pltpu.VMEM((rows_c, DISK), f32),
            pltpu.VMEM((rows_s, DISK), f32),
            pltpu.VMEM((8, DISK), f32),
            pltpu.VMEM((8, DISK), f32),
            pltpu.VMEM((2, rows_s, rows_c, 128), bf),
            pltpu.VMEM((2, rows_c, rows_s, 128), bf),
            pltpu.VMEM((2, 2, CTRL, 128), bf),
            pltpu.VMEM((2, 2, CTRL, 128), bf),
            pltpu.VMEM((3, SHELF, 128), bf),
            pltpu.VMEM((3, SHELF, 128), bf),
            pltpu.VMEM((2, rows_s, rows_c, 128), bf),
            pltpu.VMEM((2, rows_c, rows_s, 128), bf),
            dma((2,)), dma((2,)), dma((2, 2, 4)), dma((2, 2, 4)), dma((2, 8)), dma((2, 8)),
            dma((2, 8)), dma((2, 8)), dma((2, 8)), dma((2, 8)), dma((2, 8)), dma((2, 8)),
            dma((2, 2, 2, 16)), dma((2, 2, 2, 16)), dma((8, 32)), dma((8, 32)),
            dma((5, 2, GROUP)), dma((5, 2, GROUP)),
        ],
        compiler_params=pltpu.CompilerParams(
            collective_id=4, has_side_effects=True, vmem_limit_bytes=56 << 20
        ),
        name="power_steps",
    )(prob, ctrl_rows, shelf_rows, disk, label_tile)


def local(prob, ctrl_rates, shelf_rates, disk_rates, labels):
    label_tile = as_tile(labels.astype(jnp.float32))
    iterate, numer, total = power_steps(prob, ctrl_rates, shelf_rates, disk_rates, label_tile)
    refined, coarse = balance_of(numer, total, label_tile, iterate)
    return (refined, coarse[0])


def solution(mesh):
    placed = (P("ctrl", "shelf", None), P("shelf", None), P("shelf", None), P(), P("ctrl", "shelf"))
    return jax.shard_map(
        local,
        mesh=mesh,
        in_specs=placed,
        out_specs=(P("ctrl", "shelf", None), P()),
        check_vma=False,
    )
```

```python
import functools

import jax
import jax.numpy as jnp
from jax import lax
from jax.experimental import pallas as pl
from jax.experimental.pallas import tpu as pltpu
from jax.sharding import PartitionSpec as P

CTRL = 768
SHELF = 1024
DISK = 256
NBLK = 256
STEPS = 2
GROUP = 8
MESH = pl.DeviceIdType.MESH
VMEM = pltpu.MemorySpace.VMEM
HBM = pltpu.MemorySpace.HBM
HIGHEST = lax.Precision.HIGHEST


def place():
    ctrl = lax.axis_index("ctrl")
    shelf = lax.axis_index("shelf")
    plane_me = (ctrl % 2) * 4 + shelf % 4
    deep_me = shelf // 4
    high_me = ctrl // 2

    def plane(member):
        return (ctrl - ctrl % 2 + member // 4, shelf - shelf % 4 + member % 4)

    def deep(member):
        return (ctrl, member * 4 + shelf % 4)

    def high(member):
        return (member * 2 + ctrl % 2, shelf)

    return (plane_me, plane), (deep_me, deep), (high_me, high)


def exchange(group, streams, send_sem, recv_sem):
    me, peer = group

    def copy(step, index):
        source, target = streams[index]
        member = (me + step) % GROUP
        return pltpu.make_async_remote_copy(
            src_ref=source(member),
            dst_ref=target,
            send_sem=send_sem.at[index, step],
            recv_sem=recv_sem.at[index, step],
            device_id=peer(member),
            device_id_type=MESH,
        )

    def start(step, carry):
        for index in range(len(streams)):
            copy(step, index).start()
        return carry

    def finish(step, carry):
        for index in range(len(streams)):
            copy(step, index).wait()
        return carry

    lax.fori_loop(1, GROUP, start, 0)
    lax.fori_loop(1, GROUP, finish, 0)


NT = (((1,), (1,)), ((), ()))


def flow_part(labels_ref, weight_ref, factor_ref, first_ref, out_ref, wide, held):
    count = labels_ref.shape[1]
    depth = factor_ref.shape[0]
    blocks = lax.broadcasted_iota(jnp.int32, (NBLK, count), 0).astype(jnp.float32)

    def body(row, carry):
        names = jnp.broadcast_to(labels_ref[pl.ds(row, 1), :], (NBLK, count))
        member = jnp.where(names == blocks, 1.0, 0.0).astype(jnp.bfloat16)
        scaled = factor_ref[...] * weight_ref[pl.ds(row, 1), :]
        upper = scaled.astype(jnp.bfloat16)
        slot = row % 4
        wide[slot, 0:depth, :] = upper
        wide[slot, depth : 2 * depth, :] = (scaled - upper.astype(jnp.float32)).astype(jnp.bfloat16)
        both = lax.dot_general(wide[slot], member, NT, preferred_element_type=jnp.float32)
        held[:, pl.ds(row, 1), :] = (both[0:depth] + both[depth:]).reshape(depth, 1, NBLK)
        return carry

    lax.fori_loop(0, labels_ref.shape[0], body, 0, unroll=4)
    rows = held.shape[0] * held.shape[1]
    mine = held[...].reshape(rows, NBLK)
    first = first_ref[...].reshape(rows, NBLK)
    upper = mine.astype(jnp.bfloat16)
    lower = (mine - upper.astype(jnp.float32)).astype(jnp.bfloat16)
    dims = (((0,), (0,)), ((), ()))
    out_ref[...] = lax.dot_general(
        upper, first, dims, preferred_element_type=jnp.float32
    ) + lax.dot_general(lower, first, dims, preferred_element_type=jnp.float32)


def block_terms(label_ref, pair_mass_ref, pair_kept_ref):
    line = lax.broadcasted_iota(jnp.int32, (8, 128), 0)
    names = lax.broadcasted_iota(jnp.int32, (NBLK, 128), 0).astype(jnp.float32)
    terms = jnp.zeros((8, NBLK), jnp.float32)
    for r in range(12):
        have = jnp.broadcast_to(label_ref[r : r + 1], (NBLK, 128))
        member = jnp.where(have == names, 1.0, 0.0)
        pair = jnp.where(line == 0, pair_mass_ref[r : r + 1], 0.0)
        pair = jnp.where(line == 1, pair_kept_ref[r : r + 1], pair)
        terms += lax.dot_general(
            pair, member, NT, precision=HIGHEST, preferred_element_type=jnp.float32
        )
    return terms


def reduce_part(
    groups,
    labels_ref, weight_ref, factor_ref, first_ref, terms, base_ref,
    sum_ref, total_ref,
    part_ref, mass_ref, wide, held,
    rows, tiles, highs, deeps, blocks, mass_plane, mass_deep, mass_high,
    send_sem, recv_sem,
):
    plane, deep, high = groups
    plane_me, deep_me, high_me = plane[0], deep[0], high[0]

    flow_part(labels_ref, weight_ref, factor_ref, first_ref, part_ref, wide, held)
    mass_ref[...] = jnp.zeros_like(mass_ref)
    mass_ref[0:1] = terms[0:1, 0:128]
    mass_ref[1:2] = terms[0:1, 128:256]
    row = lax.broadcasted_iota(jnp.int32, (NBLK, NBLK), 0)
    column = lax.broadcasted_iota(jnp.int32, (NBLK, NBLK), 1)
    kept = jnp.where(row == column, jnp.broadcast_to(terms[1:2], (NBLK, NBLK)), 0.0)
    part_ref[...] = part_ref[...] / base_ref[0:1, 0:1] + kept

    exchange(
        plane,
        (
            (lambda m: part_ref.at[pl.ds(pl.multiple_of(m * 32, 32), 32)], rows.at[plane_me]),
            (lambda m: mass_ref, mass_plane.at[plane_me]),
        ),
        send_sem.at[0], recv_sem.at[0],
    )
    rows[plane_me] = part_ref[pl.ds(pl.multiple_of(plane_me * 32, 32), 32)]
    mass_plane[plane_me] = mass_ref[...]
    mine = jnp.sum(rows[...], axis=0)
    for tile in range(GROUP):
        r, h = tile // 2, tile % 2
        tiles[tile] = mine[r * 8 : r * 8 + 8, h * 128 : h * 128 + 128]
    total_ref[...] = jnp.sum(mass_plane[...], axis=0)

    exchange(
        deep,
        (
            (lambda m: tiles.at[m], deeps.at[deep_me]),
            (lambda m: total_ref, mass_deep.at[deep_me]),
        ),
        send_sem.at[1], recv_sem.at[1],
    )
    deeps[deep_me] = tiles[deep_me]
    mass_deep[deep_me] = total_ref[...]
    highs[high_me] = jnp.sum(deeps[...], axis=0)
    mass_high[high_me] = jnp.sum(mass_deep[...], axis=0)

    exchange(
        high,
        (
            (lambda m: highs.at[high_me], highs.at[high_me]),
            (lambda m: mass_high.at[high_me], mass_high.at[high_me]),
        ),
        send_sem.at[2], recv_sem.at[2],
    )
    total_ref[...] = jnp.sum(mass_high[...], axis=0)
    blocks[deep_me] = jnp.sum(highs[...], axis=0)

    exchange(
        deep,
        ((lambda m: blocks.at[deep_me], blocks.at[deep_me]),),
        send_sem.at[3], recv_sem.at[3],
    )
    for tile in range(GROUP):
        r, h = tile // 2, tile % 2
        sum_ref[
            pl.ds(pl.multiple_of(plane_me * 32 + r * 8, 8), 8), h * 128 : h * 128 + 128
        ] = blocks[tile]
    own = sum_ref.at[pl.ds(pl.multiple_of(plane_me * 32, 32), 32)]
    exchange(plane, ((lambda m: own, own),), send_sem.at[4], recv_sem.at[4])


def balance_kernel(
    numer_hbm, total_hbm, label_ref, state_ref, refined_hbm, coarse_ref,
    numer_ref, total_ref, power, spread, held, ready, sem, done,
):
    loads = [
        pltpu.make_async_copy(source, target, sem.at[n])
        for n, (source, target) in enumerate(
            ((total_hbm, total_ref), (numer_hbm, numer_ref), (state_ref, held))
        )
    ]
    for load in loads:
        load.start()
    loads[0].wait()
    loads[1].wait()
    size = NBLK
    line = lax.broadcasted_iota(jnp.int32, (size, size), 0)
    column = lax.broadcasted_iota(jnp.int32, (size, size), 1)
    mass = jnp.concatenate([total_ref[0:1], total_ref[1:2]], axis=1)
    mass_column = jnp.sum(
        jnp.where(line == column, jnp.broadcast_to(mass, (size, size)), 0.0), axis=1, keepdims=True
    )
    power[...] = numer_ref[...] / mass_column - 1.0 / size
    start = jnp.full((8, size), 1.0 / size, jnp.float32)

    def going(state):
        turn, height, row = state
        return jnp.logical_and(turn < 40, height > 1e-10)

    def turn_once(state):
        turn, height, row = state
        now = power[...]
        row = row + jnp.dot(row, now, precision=HIGHEST, preferred_element_type=jnp.float32)
        after = jnp.dot(now, now, precision=HIGHEST, preferred_element_type=jnp.float32)
        power[...] = after
        return turn + 1, jnp.max(jnp.abs(after)), row

    state = (jnp.int32(0), jnp.max(jnp.abs(power[...])), start)
    balance = lax.while_loop(going, turn_once, state)[2]
    coarse_ref[...] = balance * float(size)

    share = balance[0:1] / mass
    spread[...] = jnp.zeros_like(spread)
    for q in range(4):
        tile = label_ref[...]
        spread[pl.ds(q, 16, stride=4), :] = tile if q == 0 else pltpu.roll(tile, 128 - 32 * q, 1)
    names = jnp.transpose(spread[...])[0:32]
    lane = lax.broadcasted_iota(jnp.int32, (32, size), 1).astype(jnp.float32)
    loads[2].wait()
    stores = []
    for a in range(held.shape[0]):
        picked = jnp.where(names[:, a : a + 1] == lane, share, 0.0)
        factor = jnp.sum(picked, axis=1, keepdims=True)
        ready[a] = held[a] * factor * float(CTRL * SHELF * DISK)
        if a % 12 == 11:
            rows = pl.ds(a - 11, 12)
            stores.append(
                pltpu.make_async_copy(ready.at[rows], refined_hbm.at[rows], done.at[a // 12])
            )
            stores[-1].start()
    for store in stores:
        store.wait()


def balance_of(numer, total, label_tile, state):
    return pl.pallas_call(
        balance_kernel,
        out_shape=(
            jax.ShapeDtypeStruct(state.shape, jnp.float32),
            jax.ShapeDtypeStruct((8, NBLK), jnp.float32),
        ),
        in_specs=[
            pl.BlockSpec(memory_space=HBM),
            pl.BlockSpec(memory_space=HBM),
            pl.BlockSpec(memory_space=VMEM),
            pl.BlockSpec(memory_space=HBM),
        ],
        out_specs=(pl.BlockSpec(memory_space=HBM), pl.BlockSpec(memory_space=VMEM)),
        scratch_shapes=[
            pltpu.VMEM((NBLK, NBLK), jnp.float32),
            pltpu.VMEM((8, 128), jnp.float32),
            pltpu.VMEM((NBLK, NBLK), jnp.float32),
            pltpu.VMEM((128, 128), jnp.float32),
            pltpu.VMEM(state.shape, jnp.float32),
            pltpu.VMEM(state.shape, jnp.float32),
            pltpu.SemaphoreType.DMA((3,)),
            pltpu.SemaphoreType.DMA((4,)),
        ],
        compiler_params=pltpu.CompilerParams(vmem_limit_bytes=32 << 20),
        name="balance",
    )(numer, total, label_tile, state)


def spread_small(own, wide, stages, send_sem, recv_sem):
    (outer_me, outer_size, outer_peer), (inner_me, inner_size, inner_peer) = stages

    def stage(which, me, size, peer, piece):
        def copy(step):
            return pltpu.make_async_remote_copy(
                src_ref=piece,
                dst_ref=piece,
                send_sem=send_sem.at[which, step],
                recv_sem=recv_sem.at[which, step],
                device_id=peer((me + step) % size),
                device_id_type=MESH,
            )

        def start(step, carry):
            copy(step).start()
            return carry

        def finish(step, carry):
            copy(step).wait()
            return carry

        return start, finish, size

    wide[inner_me, outer_me] = own
    first = stage(0, outer_me, outer_size, outer_peer, wide.at[inner_me, outer_me])
    second = stage(1, inner_me, inner_size, inner_peer, wide.at[inner_me])
    return first, second


def shelf_stages():
    ctrl = lax.axis_index("ctrl")
    shelf = lax.axis_index("shelf")
    return (
        (shelf // 4, 8, lambda m: (ctrl, m * 4 + shelf % 4)),
        (shelf % 4, 4, lambda m: (ctrl, shelf - shelf % 4 + m)),
    )


def ctrl_stages():
    ctrl = lax.axis_index("ctrl")
    shelf = lax.axis_index("shelf")
    return (
        (ctrl // 2, 8, lambda m: (m * 2 + ctrl % 2, shelf)),
        (ctrl % 2, 2, lambda m: (ctrl - ctrl % 2 + m, shelf)),
    )


def as_tile(values):
    return jnp.pad(values.reshape(12, 128), ((0, 4), (0, 0)))


def steps_kernel(
    prob_ref, ctrl_rows_ref, shelf_rows_ref, disk_in_ref, label_ref,
    state_ref, sum_ref, total_ref,
    first_ref, shelf_labels_ref, shelf_cols_ref, weight_wide_ref, mass_ref, kept_ref, base_ref,
    part_ref, block_mass_ref, wide, held,
    rows, tiles, highs, deeps, blocks, mass_plane, mass_deep, mass_high,
    weight_ref, by_weight,
    ctrl_all, shelf_all, by_shelf, by_ctrl, ctrl_wide, ctrl_own, ctrl_ref, shelf_ref, disk_ref,
    label_rows, shelf_wide_rows, ctrl_labels, rate_ref, shelf_rate_ref, scale_ref, disk_row,
    home_y, home_z, at_y, made_y, at_z, made_z, back_y, back_z,
    swap_send, swap_recv, ring_send, ring_recv, pair_send, pair_recv,
    send_a, recv_a, send_b, recv_b, send_w, recv_w, send_y, recv_y, send_sem, recv_sem,
    send_r, recv_r,
):
    ctrl = lax.axis_index("ctrl")
    shelf = lax.axis_index("shelf")
    chip, core = shelf // 2, shelf % 2
    ctrls, shelves = 16, 32
    chips = shelves // 2
    rows_c, rows_s = state_ref.shape[0], state_ref.shape[1]
    per_y, per_z = rows_s // ctrls, rows_c // chips
    lanes = 128

    barrier = pltpu.get_barrier_semaphore()

    def signal_y(step, carry):
        target = ((ctrl + step) % ctrls, shelf)
        pl.semaphore_signal(barrier, inc=1, device_id=target, device_id_type=MESH)
        return carry

    def signal_z(step, carry):
        target = (ctrl, (shelf + step) % shelves)
        pl.semaphore_signal(barrier, inc=1, device_id=target, device_id_type=MESH)
        return carry

    lax.fori_loop(1, ctrls, signal_y, 0)
    lax.fori_loop(1, shelves, signal_z, 0)
    groups = place()
    plane_me, plane_peer = groups[0]

    def signal_plane(step, carry):
        target = plane_peer((plane_me + step) % GROUP)
        pl.semaphore_signal(barrier, inc=1, device_id=target, device_id_type=MESH)
        return carry

    lax.fori_loop(1, GROUP, signal_plane, 0)
    state_ref[...] = prob_ref[...]
    disk_ref[...] = disk_in_ref[...].astype(jnp.bfloat16)
    deep, side = shelf // 4, (shelf // 2) % 2
    wides = (ctrl_all, shelf_all)
    ctrl_all[deep, side, core] = ctrl_rows_ref[...].astype(jnp.bfloat16)
    shelf_all[deep, side, core] = shelf_rows_ref[...].astype(jnp.bfloat16)
    label_a = spread_small(label_ref[...], by_shelf, shelf_stages(), send_a, recv_a)
    label_b = spread_small(label_ref[...], by_ctrl, ctrl_stages(), send_b, recv_b)

    order = lax.broadcasted_iota(jnp.int32, (256, 256), 0)
    other = lax.broadcasted_iota(jnp.int32, (256, 256), 1)
    swap = jnp.where(
        jnp.logical_and(order // 16 == other % 16, order % 16 == other // 16), 1.0, 0.0
    ).astype(jnp.bfloat16)
    pl.semaphore_wait(barrier, ctrls - 1 + shelves - 1 + GROUP - 1)

    def along_shelf(piece, send, recv, target):
        return pltpu.make_async_remote_copy(
            src_ref=piece, dst_ref=piece, send_sem=send, recv_sem=recv,
            device_id=(ctrl, target), device_id_type=MESH,
        )

    swaps = [
        along_shelf(
            wide.at[deep, side, core], swap_send.at[n], swap_recv.at[n], shelf + 2 - 4 * side
        )
        for n, wide in enumerate(wides)
    ]
    for copy in swaps:
        copy.start()
    for start, _, size in (label_a[0], label_b[0]):
        lax.fori_loop(1, size, start, 0)

    right = ((deep + 1) % 8) * 4 + shelf % 4
    left = ((deep + 7) % 8) * 4 + shelf % 4
    sibling = shelf + 1 - 2 * core

    def pair(n, block, side_core):
        piece = wides[n].at[block, :, side_core]
        return along_shelf(piece, pair_send.at[n, block], pair_recv.at[n, block], sibling)

    def hop(n, way, count):
        block = (deep + 8 - count + 1) % 8 if way == 0 else (deep + count - 1) % 8
        return along_shelf(
            wides[n].at[block, :, core],
            ring_send.at[n, way, count - 1],
            ring_recv.at[n, way, count - 1],
            right if way == 0 else left,
        )

    def used(n, way, count):
        return count < 4 or n == way

    def gather_rows():
        for copy in swaps:
            copy.wait()
        for n in range(2):
            for way in range(2):
                hop(n, way, 1).start()
            pair(n, deep, core).start()
        for _, finish, size in (label_a[0], label_b[0]):
            lax.fori_loop(1, size, finish, 0)
        for start, _, size in (label_a[1], label_b[1]):
            lax.fori_loop(1, size, start, 0)
        for count in range(1, 5):
            for n in range(2):
                for way in range(2):
                    if not used(n, way, count):
                        continue
                    hop(n, way, count).wait_recv()
                    if count < 4 and used(n, way, count + 1):
                        hop(n, way, count + 1).start()
                    pair(n, (deep + 8 - count) % 8 if way == 0 else (deep + count) % 8, core).start()
        for _, finish, size in (label_a[1], label_b[1]):
            lax.fori_loop(1, size, finish, 0)
        for count in range(1, 5):
            for n in range(2):
                for way in range(2):
                    if used(n, way, count):
                        hop(n, way, count).wait_send()

        def settle(block, carry):
            for n in range(2):
                pair(n, block, 1 - core).wait_recv()
                pair(n, block, core).wait_send()
            return carry

        lax.fori_loop(0, 8, settle, 0)

    def prepare():
        unit = jnp.where(order == other, 1.0, 0.0).astype(jnp.bfloat16)
        dims = (((1,), (1,)), ((), ()))
        for n in range(shelves):
            wide = ctrl_all[n // 4, (n // 2) % 2, n % 2].astype(jnp.float32)
            ctrl_wide[n * 24 : n * 24 + 24] = wide
        for m in range(0, CTRL, 256):
            block = ctrl_wide[:, m : m + 256].astype(jnp.bfloat16)
            turned = lax.dot_general(unit, block, dims, preferred_element_type=jnp.float32)
            ctrl_ref[m : m + 256] = turned.astype(jnp.bfloat16)
        shelf_sum = jnp.zeros((SHELF, 1), jnp.float32)
        for m in range(0, SHELF, 256):
            block = shelf_all[:, :, :, :, m : m + 256].reshape(SHELF, 256)
            turned = lax.dot_general(unit, block, dims, preferred_element_type=jnp.float32)
            shelf_ref[m : m + 256] = turned.astype(jnp.bfloat16)
            shelf_sum += jnp.sum(block.astype(jnp.float32), axis=1, keepdims=True)
        shelf_cols_ref[...] = shelf_ref[
            pl.ds(pl.multiple_of(shelf * rows_s, 16), rows_s)
        ].astype(jnp.float32)

        ctrl_max = jnp.max(
            jnp.sum(ctrl_wide[...], axis=1, keepdims=True), axis=0, keepdims=True
        )
        shelf_max = jnp.max(shelf_sum, axis=0, keepdims=True)
        ones = jnp.ones((8, 256), jnp.bfloat16)
        disk_sum = lax.dot_general(ones, disk_ref[...], dims, preferred_element_type=jnp.float32)
        disk_max = jnp.max(disk_sum[0:1], axis=1, keepdims=True)
        base = 1.05 * (ctrl_max * shelf_max) * disk_max
        own_rows = ctrl_wide[pl.ds(pl.multiple_of(ctrl * rows_c, 8), rows_c)]
        ctrl_own[...] = own_rows.astype(jnp.bfloat16)
        own_c = jnp.sum(own_rows, axis=1, keepdims=True)
        own_s = jnp.sum(
            shelf_rows_ref[...].astype(jnp.bfloat16).astype(jnp.float32), axis=1, keepdims=True
        )
        rate_ref[...] = own_c * disk_sum[0:1] / base
        shelf_rate_ref[...] = jnp.broadcast_to(own_s, (rows_s, 256))
        scale_ref[...] = jnp.broadcast_to(1.0 / base, (8, 256))
        disk_row[...] = disk_sum
        base_ref[...] = jnp.broadcast_to(base, (8, lanes))

        spread_pairs(by_shelf, shelf_wide_rows)
        for z in range(8):
            shelf_labels_ref[:, z * lanes : (z + 1) * lanes] = shelf_wide_rows[z, 0:rows_c]
        for i in range(ctrls):
            tile = by_ctrl[i % 2, i // 2]
            for q in range(4):
                moved = tile if q == 0 else pltpu.roll(tile, lanes - 32 * q, 1)
                label_rows[i, pl.ds(q, 16, stride=4), :] = moved
        turned = jnp.transpose(label_rows[:, 0:rows_c, :].reshape(CTRL, lanes))
        ctrl_labels[...] = turned[0:rows_s]

    names = lax.broadcasted_iota(jnp.int32, (NBLK, CTRL), 0).astype(jnp.float32)

    def fill(slot):
        part = rows_s // 8

        def body(row, carry):
            have = jnp.broadcast_to(ctrl_labels[pl.ds(row, 1), :], (NBLK, CTRL))
            member = jnp.where(have == names, 1.0, 0.0).astype(jnp.bfloat16)
            first_ref[row] = lax.dot_general(
                ctrl_own[...], member, (((1,), (1,)), ((), ())), preferred_element_type=jnp.float32
            ).astype(first_ref.dtype)
            return carry

        lax.fori_loop(slot * part, slot * part + part, body, 0)

    def exchange_rows(source, target):
        first, second = source.shape[0], source.shape[1]
        blocks = [(p, q) for p in range(0, first, 16) for q in range(0, second, 16)]
        for n in range(0, len(blocks), 2):
            pieces = [
                source[p : p + 16, q : q + 16, :].reshape(256, lanes) for p, q in blocks[n : n + 2]
            ]
            flat = jnp.dot(
                swap, jnp.concatenate(pieces, axis=1), preferred_element_type=jnp.float32
            ).astype(jnp.bfloat16)
            for m, (p, q) in enumerate(blocks[n : n + 2]):
                target[q : q + 16, p : p + 16, :] = flat[:, m * lanes : (m + 1) * lanes].reshape(
                    16, 16, lanes
                )

    def part_s(ref, owner):
        return ref.at[:, pl.ds(pl.multiple_of(owner * rows_s, 16), rows_s), :]

    def remote(source, target, stream, mine, theirs, device):
        return pltpu.make_async_remote_copy(
            src_ref=source, dst_ref=target,
            send_sem=send_sem.at[stream, theirs], recv_sem=recv_sem.at[stream, mine],
            device_id=device, device_id_type=MESH,
        )

    def remote_y(source, target, half, way, n, mine, peer):
        return pltpu.make_async_remote_copy(
            src_ref=source, dst_ref=target,
            send_sem=send_y.at[half, way, n, peer], recv_sem=recv_y.at[half, way, n, mine],
            device_id=(peer, shelf), device_id_type=MESH,
        )

    def each(count, first, act):
        def body(step, carry):
            away = count // 2 + (step // 2) * (1 - 2 * (step % 2))
            act((first + away) % count)
            return carry

        lax.fori_loop(1, count, body, 0)

    def rows_of(ref, owner):
        return ref.at[pl.ds(pl.multiple_of(owner * rows_c, 16), rows_c), :]

    def y_forward(half):
        for n in range(per_y):

            def act(peer, n=n):
                remote_y(
                    home_y.at[half, peer * per_y + n], rows_of(at_y.at[half, n], ctrl),
                    half, 0, n, ctrl, peer,
                ).start()

            each(ctrls, ctrl, act)
            rows_of(at_y.at[half, n], ctrl)[...] = home_y[half, ctrl * per_y + n]

    def y_middle(half):
        for n in range(per_y):

            def arrived(peer, n=n):
                remote_y(
                    home_y.at[half, peer * per_y + n], rows_of(at_y.at[half, n], peer),
                    half, 0, n, peer, peer,
                ).wait()

            each(ctrls, ctrl, arrived)
            for m in range(0, ctrls * rows_c, 256):
                made = jnp.dot(
                    ctrl_ref[m : m + 256], at_y[half, n], preferred_element_type=jnp.float32
                )
                made_y[half, n, m : m + 256, :] = made.astype(jnp.bfloat16)

            def act(peer, n=n):
                remote_y(
                    rows_of(made_y.at[half, n], peer), back_y.at[half, ctrl * per_y + n],
                    half, 1, n, ctrl, peer,
                ).start()

            each(ctrls, ctrl, act)
            back_y[half, ctrl * per_y + n] = rows_of(made_y.at[half, n], ctrl)[...]

    def y_back_wait(half):
        for n in range(per_y):

            def act(peer, n=n):
                remote_y(
                    rows_of(made_y.at[half, n], peer), back_y.at[half, peer * per_y + n],
                    half, 1, n, peer, peer,
                ).wait()

            each(ctrls, ctrl, act)

    chunks = ((0, 2), (2, 1))

    def z_forward_copy(half, part, to):
        at, size = chunks[part]
        return remote(
            home_z.at[half, pl.ds(to * per_z + at, size)], part_s(at_z.at[pl.ds(at, size)], shelf),
            (2 * half) * 2 + part, shelf, to, (ctrl, 2 * to + half),
        )

    def z_forward(half):
        for part in range(2):
            at, size = chunks[part]
            each(chips, chip, lambda to: z_forward_copy(half, part, to).start())

            @pl.when(core != half)
            def _():
                z_forward_copy(half, part, chip).start()

            @pl.when(core == half)
            def _():
                part_s(at_z.at[pl.ds(at, size)], shelf)[...] = home_z[
                    half, pl.ds(chip * per_z + at, size)
                ]

    def z_forward_sent(half):
        for part in range(2):
            each(chips, chip, lambda to: z_forward_copy(half, part, to).wait_send())

            @pl.when(core != half)
            def _():
                z_forward_copy(half, part, chip).wait_send()

    def z_back_copy(half, part, peer):
        at, size = chunks[part]
        return remote(
            part_s(made_z.at[pl.ds(at, size)], peer),
            back_z.at[half, pl.ds(chip * per_z + at, size)],
            (2 * half + 1) * 2 + part, chip, peer, (ctrl, peer),
        )

    def z_middle(half):
        @pl.when(core == half)
        def _():
            for part in range(2):
                at, size = chunks[part]

                def arrived(peer):
                    remote(
                        home_z.at[half, pl.ds(0, size)], part_s(at_z.at[pl.ds(at, size)], peer),
                        (2 * half) * 2 + part, peer, 0, (ctrl, peer),
                    ).wait_recv()

                each(shelves, shelf, arrived)
                both = jnp.concatenate([at_z[at + n] for n in range(size)], axis=1)
                for m in range(0, shelves * rows_s, 256):
                    made = jnp.dot(shelf_ref[m : m + 256], both, preferred_element_type=jnp.float32)
                    for n in range(size):
                        made_z[at + n, m : m + 256, :] = made[
                            :, n * lanes : (n + 1) * lanes
                        ].astype(jnp.bfloat16)
                each(shelves, shelf, lambda peer: z_back_copy(half, part, peer).start())
                back_z[half, pl.ds(chip * per_z + at, size)] = part_s(
                    made_z.at[pl.ds(at, size)], shelf
                )[...]

    def z_back_from(half, part, source):
        at, size = chunks[part]
        return remote(
            part_s(made_z.at[pl.ds(at, size)], shelf),
            back_z.at[half, pl.ds(source * per_z + at, size)],
            (2 * half + 1) * 2 + part, source, 0, (ctrl, 2 * source + half),
        )

    def z_back_wait(half):
        for part in range(2):
            each(chips, chip, lambda source: z_back_from(half, part, source).wait_recv())

            @pl.when(core != half)
            def _():
                z_back_from(half, part, chip).wait_recv()

    def z_back_sent(half):
        @pl.when(core == half)
        def _():
            for part in range(2):
                each(shelves, shelf, lambda peer: z_back_copy(half, part, peer).wait_send())

    def one_step(repeat, carry):
        for p in range(0, rows_c, 16):
            rounded = state_ref[p : p + 16].astype(jnp.bfloat16).reshape(16 * rows_s, 256)
            made = jnp.dot(rounded, disk_ref[...], preferred_element_type=jnp.float32)
            made = made.astype(jnp.bfloat16).reshape(16, rows_s, 256)
            home_z[1, p : p + 16] = made[:, :, lanes:]
            home_z[0, p : p + 16] = made[:, :, :lanes]
        z_forward(1)
        exchange_rows(home_z.at[0], home_y.at[0])
        y_forward(0)

        @pl.when(repeat == 0)
        def _():
            gather_rows()
            prepare()

        fill(repeat * 4)
        z_middle(1)
        y_middle(0)
        fill(repeat * 4 + 1)
        y_back_wait(0)
        exchange_rows(back_y.at[0], home_z.at[0])
        z_forward(0)
        z_back_wait(1)
        exchange_rows(back_z.at[1], home_y.at[1])
        y_forward(1)
        z_middle(0)
        y_middle(1)
        fill(repeat * 4 + 2)
        fill(repeat * 4 + 3)
        y_back_wait(1)
        z_forward_sent(1)
        exchange_rows(back_y.at[1], home_z.at[1])
        z_back_wait(0)

        def update(row, inner):
            kept = 1.0 - rate_ref[pl.ds(row, 1), :] * shelf_rate_ref[...]
            third = jnp.concatenate([back_z[0, row], home_z[1, row]], axis=1)
            state_ref[row] = third.astype(jnp.float32) * scale_ref[0:1] + state_ref[row] * kept
            return inner

        lax.fori_loop(0, rows_c, update, 0, unroll=4)
        z_forward_sent(0)
        z_back_sent(0)
        z_back_sent(1)
        return carry

    lax.fori_loop(0, STEPS, one_step, 0)

    lead = lax.broadcasted_iota(jnp.int32, (8, 256), 0) == 0
    sums = jnp.where(lead, 1.0, disk_row[...])
    weight_ref[...] = jnp.zeros_like(weight_ref)
    mass_ref[...] = jnp.zeros_like(mass_ref)
    for r in range(rows_c // 4):
        both = lax.dot_general(
            sums,
            state_ref[4 * r : 4 * r + 4].reshape(4 * rows_s, 256),
            (((1,), (1,)), ((), ())),
            precision=HIGHEST,
            preferred_element_type=jnp.float32,
        )
        mass_ref[r : r + 1] = both[0:1]
        weight_ref[r : r + 1] = both[1:2]
    stages = spread_small(weight_ref[...], by_weight, shelf_stages(), send_w, recv_w)
    lax.fori_loop(1, stages[0][2], stages[0][0], 0)
    kept_ref[...] = jnp.zeros_like(kept_ref)
    ones = jnp.ones((8, 256), jnp.float32)
    for r in range(rows_c // 4):
        part = [
            state_ref[n] * (1.0 - rate_ref[n : n + 1] * shelf_rate_ref[...])
            for n in range(4 * r, 4 * r + 4)
        ]
        kept_ref[r : r + 1] = lax.dot_general(
            ones, jnp.concatenate(part, axis=0), NT,
            precision=HIGHEST, preferred_element_type=jnp.float32,
        )[0:1]
    lax.fori_loop(1, stages[0][2], stages[0][1], 0)
    lax.fori_loop(1, stages[1][2], stages[1][0], 0)
    terms = block_terms(label_ref, mass_ref, kept_ref)
    lax.fori_loop(1, stages[1][2], stages[1][1], 0)
    spread_pairs(by_weight, shelf_wide_rows)
    for z in range(8):
        weight_wide_ref[:, z * lanes : (z + 1) * lanes] = shelf_wide_rows[z, 0:rows_c]
    reduce_part(
        groups,
        shelf_labels_ref, weight_wide_ref, shelf_cols_ref, first_ref, terms,
        base_ref, sum_ref, total_ref, part_ref, block_mass_ref, wide, held,
        rows, tiles, highs, deeps, blocks, mass_plane, mass_deep, mass_high, send_r, recv_r,
    )


def spread_pairs(tiles, wide):
    lane = lax.broadcasted_iota(jnp.int32, (16, 128), 1) // 32
    for z in range(8):
        for q in range(4):
            made = jnp.zeros((16, 128), jnp.float32)
            for p in range(4):
                tile = tiles[p, z]
                moved = tile if p == q else pltpu.roll(tile, (32 * (p - q)) % 128, 1)
                made = jnp.where(lane == p, moved, made)
            wide[z, pl.ds(q, 16, stride=4), :] = made


def power_steps(prob, ctrl_rows, shelf_rows, disk, label_tile):
    rows_c, rows_s, _ = prob.shape
    bf, f32 = jnp.bfloat16, jnp.float32
    outs = [(prob.shape, f32), ((NBLK, NBLK), f32), ((8, 128), f32)]
    dma = pltpu.SemaphoreType.DMA
    return pl.pallas_call(
        steps_kernel,
        out_shape=tuple(jax.ShapeDtypeStruct(*out) for out in outs),
        in_specs=[pl.BlockSpec(memory_space=VMEM)] * 5,
        out_specs=tuple([pl.BlockSpec(memory_space=VMEM)] * len(outs)),
        scratch_shapes=[
            pltpu.VMEM((rows_s, rows_c, NBLK), bf),
            pltpu.VMEM((rows_c, SHELF), f32),
            pltpu.VMEM((rows_s, SHELF), f32),
            pltpu.VMEM((rows_c, SHELF), f32),
            pltpu.VMEM((16, 128), f32),
            pltpu.VMEM((16, 128), f32),
            pltpu.VMEM((8, 128), f32),
            pltpu.VMEM((NBLK, NBLK), f32),
            pltpu.VMEM((8, 128), f32),
            pltpu.VMEM((4, 2 * rows_s, SHELF), bf),
            pltpu.VMEM((rows_s, rows_c, NBLK), f32),
            pltpu.VMEM((GROUP, 32, NBLK), f32),
            *[pltpu.VMEM((GROUP, 8, 128), f32)] * 7,
            pltpu.VMEM((16, 128), f32),
            pltpu.VMEM((4, 8, 16, 128), f32),
            pltpu.VMEM((8, 2, 2, 24, CTRL), bf),
            pltpu.VMEM((8, 2, 2, 32, SHELF), bf),
            pltpu.VMEM((4, 8, 16, 128), f32),
            pltpu.VMEM((2, 8, 16, 128), f32),
            pltpu.VMEM((CTRL, CTRL), f32),
            pltpu.VMEM((rows_c, CTRL), bf),
            pltpu.VMEM((CTRL, CTRL), bf),
            pltpu.VMEM((SHELF, SHELF), bf),
            pltpu.VMEM((DISK, DISK), bf),
            pltpu.VMEM((16, 64, 128), f32),
            pltpu.VMEM((8, 64, 128), f32),
            pltpu.VMEM((rows_s, CTRL), f32),
            pltpu.VMEM((rows_c, DISK), f32),
            pltpu.VMEM((rows_s, DISK), f32),
            pltpu.VMEM((8, DISK), f32),
            pltpu.VMEM((8, DISK), f32),
            pltpu.VMEM((2, rows_s, rows_c, 128), bf),
            pltpu.VMEM((2, rows_c, rows_s, 128), bf),
            pltpu.VMEM((2, 2, CTRL, 128), bf),
            pltpu.VMEM((2, 2, CTRL, 128), bf),
            pltpu.VMEM((3, SHELF, 128), bf),
            pltpu.VMEM((3, SHELF, 128), bf),
            pltpu.VMEM((2, rows_s, rows_c, 128), bf),
            pltpu.VMEM((2, rows_c, rows_s, 128), bf),
            dma((2,)), dma((2,)), dma((2, 2, 4)), dma((2, 2, 4)), dma((2, 8)), dma((2, 8)),
            dma((2, 8)), dma((2, 8)), dma((2, 8)), dma((2, 8)), dma((2, 8)), dma((2, 8)),
            dma((2, 2, 2, 16)), dma((2, 2, 2, 16)), dma((8, 32)), dma((8, 32)),
            dma((5, 2, GROUP)), dma((5, 2, GROUP)),
        ],
        compiler_params=pltpu.CompilerParams(
            collective_id=4, has_side_effects=True, vmem_limit_bytes=56 << 20
        ),
        name="power_steps",
    )(prob, ctrl_rows, shelf_rows, disk, label_tile)


def local(prob, ctrl_rates, shelf_rates, disk_rates, labels):
    label_tile = as_tile(labels.astype(jnp.float32))
    iterate, numer, total = power_steps(prob, ctrl_rates, shelf_rates, disk_rates, label_tile)
    refined, coarse = balance_of(numer, total, label_tile, iterate)
    return (refined, coarse[0])


def solution(mesh):
    placed = (P("ctrl", "shelf", None), P("shelf", None), P("shelf", None), P(), P("ctrl", "shelf"))
    return jax.shard_map(
        local,
        mesh=mesh,
        in_specs=placed,
        out_specs=(P("ctrl", "shelf", None), P()),
        check_vma=False,
    )
```

```python
import functools

import jax
import jax.numpy as jnp
from jax import lax
from jax.experimental import pallas as pl
from jax.experimental.pallas import tpu as pltpu
from jax.sharding import PartitionSpec as P

CTRL = 768
SHELF = 1024
DISK = 256
NBLK = 256
STEPS = 2
GROUP = 8
MESH = pl.DeviceIdType.MESH
VMEM = pltpu.MemorySpace.VMEM
HBM = pltpu.MemorySpace.HBM
HIGHEST = lax.Precision.HIGHEST


def place():
    ctrl = lax.axis_index("ctrl")
    shelf = lax.axis_index("shelf")
    plane_me = (ctrl % 2) * 4 + shelf % 4
    deep_me = shelf // 4
    high_me = ctrl // 2

    def plane(member):
        return (ctrl - ctrl % 2 + member // 4, shelf - shelf % 4 + member % 4)

    def deep(member):
        return (ctrl, member * 4 + shelf % 4)

    def high(member):
        return (member * 2 + ctrl % 2, shelf)

    return (plane_me, plane), (deep_me, deep), (high_me, high)


def far_first(step, count):
    return count // 2 + (step // 2) * (1 - 2 * (step % 2))


def exchange(group, streams, send_sem, recv_sem):
    me, peer = group

    def copy(step, index):
        source, target = streams[index]
        member = (me + step) % GROUP
        return pltpu.make_async_remote_copy(
            src_ref=source(member),
            dst_ref=target,
            send_sem=send_sem.at[index, step],
            recv_sem=recv_sem.at[index, step],
            device_id=peer(member),
            device_id_type=MESH,
        )

    def start(step, carry):
        for index in range(len(streams)):
            copy(far_first(step, GROUP), index).start()
        return carry

    def finish(step, carry):
        for index in range(len(streams)):
            copy(step, index).wait()
        return carry

    lax.fori_loop(1, GROUP, start, 0)
    lax.fori_loop(1, GROUP, finish, 0)


NT = (((1,), (1,)), ((), ()))


def flow_part(labels_ref, weight_ref, factor_ref, first_ref, out_ref, wide, held):
    count = labels_ref.shape[1]
    depth = factor_ref.shape[0]
    blocks = lax.broadcasted_iota(jnp.int32, (NBLK, count), 0).astype(jnp.float32)

    def body(row, carry):
        names = jnp.broadcast_to(labels_ref[pl.ds(row, 1), :], (NBLK, count))
        member = jnp.where(names == blocks, 1.0, 0.0).astype(jnp.bfloat16)
        scaled = factor_ref[...] * weight_ref[pl.ds(row, 1), :]
        upper = scaled.astype(jnp.bfloat16)
        slot = row % 4
        wide[slot, 0:depth, :] = upper
        wide[slot, depth : 2 * depth, :] = (scaled - upper.astype(jnp.float32)).astype(jnp.bfloat16)
        both = lax.dot_general(wide[slot], member, NT, preferred_element_type=jnp.float32)
        held[:, pl.ds(row, 1), :] = (both[0:depth] + both[depth:]).reshape(depth, 1, NBLK)
        return carry

    lax.fori_loop(0, labels_ref.shape[0], body, 0, unroll=4)
    rows = held.shape[0] * held.shape[1]
    mine = held[...].reshape(rows, NBLK)
    first = first_ref[...].reshape(rows, NBLK)
    upper = mine.astype(jnp.bfloat16)
    lower = (mine - upper.astype(jnp.float32)).astype(jnp.bfloat16)
    dims = (((0,), (0,)), ((), ()))
    out_ref[...] = lax.dot_general(
        upper, first, dims, preferred_element_type=jnp.float32
    ) + lax.dot_general(lower, first, dims, preferred_element_type=jnp.float32)


def block_terms(label_ref, pair_mass_ref, pair_kept_ref):
    line = lax.broadcasted_iota(jnp.int32, (8, 128), 0)
    names = lax.broadcasted_iota(jnp.int32, (NBLK, 128), 0).astype(jnp.float32)
    terms = jnp.zeros((8, NBLK), jnp.float32)
    for r in range(12):
        have = jnp.broadcast_to(label_ref[r : r + 1], (NBLK, 128))
        member = jnp.where(have == names, 1.0, 0.0)
        pair = jnp.where(line == 0, pair_mass_ref[r : r + 1], 0.0)
        pair = jnp.where(line == 1, pair_kept_ref[r : r + 1], pair)
        terms += lax.dot_general(
            pair, member, NT, precision=HIGHEST, preferred_element_type=jnp.float32
        )
    return terms


def reduce_part(
    groups,
    labels_ref, weight_ref, factor_ref, first_ref, terms, base_ref,
    sum_ref, total_ref,
    part_ref, mass_ref, wide, held,
    rows, tiles, highs, deeps, blocks, mass_plane, mass_deep, mass_high,
    send_sem, recv_sem,
):
    plane, deep, high = groups
    plane_me, deep_me, high_me = plane[0], deep[0], high[0]

    flow_part(labels_ref, weight_ref, factor_ref, first_ref, part_ref, wide, held)
    mass_ref[...] = jnp.zeros_like(mass_ref)
    mass_ref[0:1] = terms[0:1, 0:128]
    mass_ref[1:2] = terms[0:1, 128:256]
    row = lax.broadcasted_iota(jnp.int32, (NBLK, NBLK), 0)
    column = lax.broadcasted_iota(jnp.int32, (NBLK, NBLK), 1)
    kept = jnp.where(row == column, jnp.broadcast_to(terms[1:2], (NBLK, NBLK)), 0.0)
    part_ref[...] = part_ref[...] / base_ref[0:1, 0:1] + kept

    exchange(
        plane,
        (
            (lambda m: part_ref.at[pl.ds(pl.multiple_of(m * 32, 32), 32)], rows.at[plane_me]),
            (lambda m: mass_ref, mass_plane.at[plane_me]),
        ),
        send_sem.at[0], recv_sem.at[0],
    )
    rows[plane_me] = part_ref[pl.ds(pl.multiple_of(plane_me * 32, 32), 32)]
    mass_plane[plane_me] = mass_ref[...]
    mine = jnp.sum(rows[...], axis=0)
    for tile in range(GROUP):
        r, h = tile // 2, tile % 2
        tiles[tile] = mine[r * 8 : r * 8 + 8, h * 128 : h * 128 + 128]
    total_ref[...] = jnp.sum(mass_plane[...], axis=0)

    exchange(
        deep,
        (
            (lambda m: tiles.at[m], deeps.at[deep_me]),
            (lambda m: total_ref, mass_deep.at[deep_me]),
        ),
        send_sem.at[1], recv_sem.at[1],
    )
    deeps[deep_me] = tiles[deep_me]
    mass_deep[deep_me] = total_ref[...]
    highs[high_me] = jnp.sum(deeps[...], axis=0)
    mass_high[high_me] = jnp.sum(mass_deep[...], axis=0)

    exchange(
        high,
        (
            (lambda m: highs.at[high_me], highs.at[high_me]),
            (lambda m: mass_high.at[high_me], mass_high.at[high_me]),
        ),
        send_sem.at[2], recv_sem.at[2],
    )
    total_ref[...] = jnp.sum(mass_high[...], axis=0)
    blocks[deep_me] = jnp.sum(highs[...], axis=0)

    exchange(
        deep,
        ((lambda m: blocks.at[deep_me], blocks.at[deep_me]),),
        send_sem.at[3], recv_sem.at[3],
    )
    for tile in range(GROUP):
        r, h = tile // 2, tile % 2
        sum_ref[
            pl.ds(pl.multiple_of(plane_me * 32 + r * 8, 8), 8), h * 128 : h * 128 + 128
        ] = blocks[tile]
    own = sum_ref.at[pl.ds(pl.multiple_of(plane_me * 32, 32), 32)]
    exchange(plane, ((lambda m: own, own),), send_sem.at[4], recv_sem.at[4])


def balance_kernel(
    numer_hbm, total_hbm, label_ref, state_ref, refined_hbm, coarse_ref,
    numer_ref, total_ref, power, spread, held, ready, sem, done,
):
    loads = [
        pltpu.make_async_copy(source, target, sem.at[n])
        for n, (source, target) in enumerate(
            ((total_hbm, total_ref), (numer_hbm, numer_ref), (state_ref, held))
        )
    ]
    for load in loads:
        load.start()
    loads[0].wait()
    loads[1].wait()
    size = NBLK
    line = lax.broadcasted_iota(jnp.int32, (size, size), 0)
    column = lax.broadcasted_iota(jnp.int32, (size, size), 1)
    mass = jnp.concatenate([total_ref[0:1], total_ref[1:2]], axis=1)
    mass_column = jnp.sum(
        jnp.where(line == column, jnp.broadcast_to(mass, (size, size)), 0.0), axis=1, keepdims=True
    )
    power[...] = numer_ref[...] / mass_column - 1.0 / size
    start = jnp.full((8, size), 1.0 / size, jnp.float32)

    def going(state):
        turn, height, row = state
        return jnp.logical_and(turn < 40, height > 1e-10)

    def turn_once(state):
        turn, height, row = state
        now = power[...]
        row = row + jnp.dot(row, now, precision=HIGHEST, preferred_element_type=jnp.float32)
        after = jnp.dot(now, now, precision=HIGHEST, preferred_element_type=jnp.float32)
        power[...] = after
        return turn + 1, jnp.max(jnp.abs(after)), row

    state = (jnp.int32(0), jnp.max(jnp.abs(power[...])), start)
    balance = lax.while_loop(going, turn_once, state)[2]
    coarse_ref[...] = balance * float(size)

    share = balance[0:1] / mass
    spread[...] = jnp.zeros_like(spread)
    for q in range(4):
        tile = label_ref[...]
        spread[pl.ds(q, 16, stride=4), :] = tile if q == 0 else pltpu.roll(tile, 128 - 32 * q, 1)
    names = jnp.transpose(spread[...])[0:32]
    lane = lax.broadcasted_iota(jnp.int32, (32, size), 1).astype(jnp.float32)
    loads[2].wait()
    stores = []
    for a in range(held.shape[0]):
        picked = jnp.where(names[:, a : a + 1] == lane, share, 0.0)
        factor = jnp.sum(picked, axis=1, keepdims=True)
        ready[a] = held[a] * factor * float(CTRL * SHELF * DISK)
        if a % 12 == 11:
            rows = pl.ds(a - 11, 12)
            stores.append(
                pltpu.make_async_copy(ready.at[rows], refined_hbm.at[rows], done.at[a // 12])
            )
            stores[-1].start()
    for store in stores:
        store.wait()


def balance_of(numer, total, label_tile, state):
    return pl.pallas_call(
        balance_kernel,
        out_shape=(
            jax.ShapeDtypeStruct(state.shape, jnp.float32),
            jax.ShapeDtypeStruct((8, NBLK), jnp.float32),
        ),
        in_specs=[
            pl.BlockSpec(memory_space=HBM),
            pl.BlockSpec(memory_space=HBM),
            pl.BlockSpec(memory_space=VMEM),
            pl.BlockSpec(memory_space=HBM),
        ],
        out_specs=(pl.BlockSpec(memory_space=HBM), pl.BlockSpec(memory_space=VMEM)),
        scratch_shapes=[
            pltpu.VMEM((NBLK, NBLK), jnp.float32),
            pltpu.VMEM((8, 128), jnp.float32),
            pltpu.VMEM((NBLK, NBLK), jnp.float32),
            pltpu.VMEM((128, 128), jnp.float32),
            pltpu.VMEM(state.shape, jnp.float32),
            pltpu.VMEM(state.shape, jnp.float32),
            pltpu.SemaphoreType.DMA((3,)),
            pltpu.SemaphoreType.DMA((4,)),
        ],
        compiler_params=pltpu.CompilerParams(vmem_limit_bytes=32 << 20),
        name="balance",
    )(numer, total, label_tile, state)


def spread_small(own, wide, stages, send_sem, recv_sem):
    (outer_me, outer_size, outer_peer), (inner_me, inner_size, inner_peer) = stages

    def stage(which, me, size, peer, piece):
        def copy(step):
            return pltpu.make_async_remote_copy(
                src_ref=piece,
                dst_ref=piece,
                send_sem=send_sem.at[which, step],
                recv_sem=recv_sem.at[which, step],
                device_id=peer((me + step) % size),
                device_id_type=MESH,
            )

        def start(step, carry):
            copy(far_first(step, size)).start()
            return carry

        def finish(step, carry):
            copy(step).wait()
            return carry

        return start, finish, size

    wide[inner_me, outer_me] = own
    first = stage(0, outer_me, outer_size, outer_peer, wide.at[inner_me, outer_me])
    second = stage(1, inner_me, inner_size, inner_peer, wide.at[inner_me])
    return first, second


def shelf_stages():
    ctrl = lax.axis_index("ctrl")
    shelf = lax.axis_index("shelf")
    return (
        (shelf // 4, 8, lambda m: (ctrl, m * 4 + shelf % 4)),
        (shelf % 4, 4, lambda m: (ctrl, shelf - shelf % 4 + m)),
    )


def ctrl_stages():
    ctrl = lax.axis_index("ctrl")
    shelf = lax.axis_index("shelf")
    return (
        (ctrl // 2, 8, lambda m: (m * 2 + ctrl % 2, shelf)),
        (ctrl % 2, 2, lambda m: (ctrl - ctrl % 2 + m, shelf)),
    )


def as_tile(values):
    return jnp.pad(values.reshape(12, 128), ((0, 4), (0, 0)))


def steps_kernel(
    prob_ref, ctrl_rows_ref, shelf_rows_ref, disk_in_ref, label_ref,
    state_ref, sum_ref, total_ref,
    first_ref, shelf_labels_ref, shelf_cols_ref, weight_wide_ref, mass_ref, kept_ref, base_ref,
    part_ref, block_mass_ref, wide, held,
    rows, tiles, highs, deeps, blocks, mass_plane, mass_deep, mass_high,
    weight_ref, by_weight,
    ctrl_all, shelf_all, by_shelf, by_ctrl, ctrl_wide, ctrl_own, ctrl_ref, shelf_ref, disk_ref,
    label_rows, shelf_wide_rows, ctrl_labels, rate_ref, shelf_rate_ref, scale_ref, disk_row,
    home_y, home_z, at_y, made_y, at_z, made_z, back_y, back_z,
    swap_send, swap_recv, ring_send, ring_recv, pair_send, pair_recv,
    send_a, recv_a, send_b, recv_b, send_w, recv_w, send_y, recv_y, send_sem, recv_sem,
    send_r, recv_r,
):
    ctrl = lax.axis_index("ctrl")
    shelf = lax.axis_index("shelf")
    chip, core = shelf // 2, shelf % 2
    ctrls, shelves = 16, 32
    chips = shelves // 2
    rows_c, rows_s = state_ref.shape[0], state_ref.shape[1]
    per_y, per_z = rows_s // ctrls, rows_c // chips
    lanes = 128

    barrier = pltpu.get_barrier_semaphore()

    def signal_y(step, carry):
        target = ((ctrl + step) % ctrls, shelf)
        pl.semaphore_signal(barrier, inc=1, device_id=target, device_id_type=MESH)
        return carry

    def signal_z(step, carry):
        target = (ctrl, (shelf + step) % shelves)
        pl.semaphore_signal(barrier, inc=1, device_id=target, device_id_type=MESH)
        return carry

    lax.fori_loop(1, ctrls, signal_y, 0)
    lax.fori_loop(1, shelves, signal_z, 0)
    groups = place()
    plane_me, plane_peer = groups[0]

    def signal_plane(step, carry):
        target = plane_peer((plane_me + step) % GROUP)
        pl.semaphore_signal(barrier, inc=1, device_id=target, device_id_type=MESH)
        return carry

    lax.fori_loop(1, GROUP, signal_plane, 0)
    state_ref[...] = prob_ref[...]
    disk_ref[...] = disk_in_ref[...].astype(jnp.bfloat16)
    deep, side = shelf // 4, (shelf // 2) % 2
    wides = (ctrl_all, shelf_all)
    ctrl_all[deep, side, core] = ctrl_rows_ref[...].astype(jnp.bfloat16)
    shelf_all[deep, side, core] = shelf_rows_ref[...].astype(jnp.bfloat16)
    label_a = spread_small(label_ref[...], by_shelf, shelf_stages(), send_a, recv_a)
    label_b = spread_small(label_ref[...], by_ctrl, ctrl_stages(), send_b, recv_b)

    order = lax.broadcasted_iota(jnp.int32, (256, 256), 0)
    other = lax.broadcasted_iota(jnp.int32, (256, 256), 1)
    swap = jnp.where(
        jnp.logical_and(order // 16 == other % 16, order % 16 == other // 16), 1.0, 0.0
    ).astype(jnp.bfloat16)
    pl.semaphore_wait(barrier, ctrls - 1 + shelves - 1 + GROUP - 1)

    def along_shelf(piece, send, recv, target):
        return pltpu.make_async_remote_copy(
            src_ref=piece, dst_ref=piece, send_sem=send, recv_sem=recv,
            device_id=(ctrl, target), device_id_type=MESH,
        )

    swaps = [
        along_shelf(
            wide.at[deep, side, core], swap_send.at[n], swap_recv.at[n], shelf + 2 - 4 * side
        )
        for n, wide in enumerate(wides)
    ]
    for copy in swaps:
        copy.start()
    for start, _, size in (label_a[0], label_b[0]):
        lax.fori_loop(1, size, start, 0)

    right = ((deep + 1) % 8) * 4 + shelf % 4
    left = ((deep + 7) % 8) * 4 + shelf % 4
    sibling = shelf + 1 - 2 * core

    def pair(n, block, side_core):
        piece = wides[n].at[block, :, side_core]
        return along_shelf(piece, pair_send.at[n, block], pair_recv.at[n, block], sibling)

    def hop(n, way, count):
        block = (deep + 8 - count + 1) % 8 if way == 0 else (deep + count - 1) % 8
        return along_shelf(
            wides[n].at[block, :, core],
            ring_send.at[n, way, count - 1],
            ring_recv.at[n, way, count - 1],
            right if way == 0 else left,
        )

    def used(n, way, count):
        return count < 4 or n == way

    def gather_rows():
        for copy in swaps:
            copy.wait()
        for n in range(2):
            for way in range(2):
                hop(n, way, 1).start()
            pair(n, deep, core).start()
        for _, finish, size in (label_a[0], label_b[0]):
            lax.fori_loop(1, size, finish, 0)
        for start, _, size in (label_a[1], label_b[1]):
            lax.fori_loop(1, size, start, 0)
        for count in range(1, 5):
            for n in range(2):
                for way in range(2):
                    if not used(n, way, count):
                        continue
                    hop(n, way, count).wait_recv()
                    if count < 4 and used(n, way, count + 1):
                        hop(n, way, count + 1).start()
                    pair(n, (deep + 8 - count) % 8 if way == 0 else (deep + count) % 8, core).start()
        for _, finish, size in (label_a[1], label_b[1]):
            lax.fori_loop(1, size, finish, 0)
        for count in range(1, 5):
            for n in range(2):
                for way in range(2):
                    if used(n, way, count):
                        hop(n, way, count).wait_send()

        def settle(block, carry):
            for n in range(2):
                pair(n, block, 1 - core).wait_recv()
                pair(n, block, core).wait_send()
            return carry

        lax.fori_loop(0, 8, settle, 0)

    def prepare():
        unit = jnp.where(order == other, 1.0, 0.0).astype(jnp.bfloat16)
        dims = (((1,), (1,)), ((), ()))
        for n in range(shelves):
            wide = ctrl_all[n // 4, (n // 2) % 2, n % 2].astype(jnp.float32)
            ctrl_wide[n * 24 : n * 24 + 24] = wide
        for m in range(0, CTRL, 256):
            block = ctrl_wide[:, m : m + 256].astype(jnp.bfloat16)
            turned = lax.dot_general(unit, block, dims, preferred_element_type=jnp.float32)
            ctrl_ref[m : m + 256] = turned.astype(jnp.bfloat16)
        shelf_sum = jnp.zeros((SHELF, 1), jnp.float32)
        for m in range(0, SHELF, 256):
            block = shelf_all[:, :, :, :, m : m + 256].reshape(SHELF, 256)
            turned = lax.dot_general(unit, block, dims, preferred_element_type=jnp.float32)
            shelf_ref[m : m + 256] = turned.astype(jnp.bfloat16)
            shelf_sum += jnp.sum(block.astype(jnp.float32), axis=1, keepdims=True)
        shelf_cols_ref[...] = shelf_ref[
            pl.ds(pl.multiple_of(shelf * rows_s, 16), rows_s)
        ].astype(jnp.float32)

        ctrl_max = jnp.max(
            jnp.sum(ctrl_wide[...], axis=1, keepdims=True), axis=0, keepdims=True
        )
        shelf_max = jnp.max(shelf_sum, axis=0, keepdims=True)
        ones = jnp.ones((8, 256), jnp.bfloat16)
        disk_sum = lax.dot_general(ones, disk_ref[...], dims, preferred_element_type=jnp.float32)
        disk_max = jnp.max(disk_sum[0:1], axis=1, keepdims=True)
        base = 1.05 * (ctrl_max * shelf_max) * disk_max
        own_rows = ctrl_wide[pl.ds(pl.multiple_of(ctrl * rows_c, 8), rows_c)]
        ctrl_own[...] = own_rows.astype(jnp.bfloat16)
        own_c = jnp.sum(own_rows, axis=1, keepdims=True)
        own_s = jnp.sum(
            shelf_rows_ref[...].astype(jnp.bfloat16).astype(jnp.float32), axis=1, keepdims=True
        )
        rate_ref[...] = own_c * disk_sum[0:1] / base
        shelf_rate_ref[...] = jnp.broadcast_to(own_s, (rows_s, 256))
        scale_ref[...] = jnp.broadcast_to(1.0 / base, (8, 256))
        disk_row[...] = disk_sum
        base_ref[...] = jnp.broadcast_to(base, (8, lanes))

        spread_pairs(by_shelf, shelf_wide_rows)
        for z in range(8):
            shelf_labels_ref[:, z * lanes : (z + 1) * lanes] = shelf_wide_rows[z, 0:rows_c]
        for i in range(ctrls):
            tile = by_ctrl[i % 2, i // 2]
            for q in range(4):
                moved = tile if q == 0 else pltpu.roll(tile, lanes - 32 * q, 1)
                label_rows[i, pl.ds(q, 16, stride=4), :] = moved
        turned = jnp.transpose(label_rows[:, 0:rows_c, :].reshape(CTRL, lanes))
        ctrl_labels[...] = turned[0:rows_s]

    names = lax.broadcasted_iota(jnp.int32, (NBLK, CTRL), 0).astype(jnp.float32)

    def fill(slot):
        part = rows_s // 8

        def body(row, carry):
            have = jnp.broadcast_to(ctrl_labels[pl.ds(row, 1), :], (NBLK, CTRL))
            member = jnp.where(have == names, 1.0, 0.0).astype(jnp.bfloat16)
            first_ref[row] = lax.dot_general(
                ctrl_own[...], member, (((1,), (1,)), ((), ())), preferred_element_type=jnp.float32
            ).astype(first_ref.dtype)
            return carry

        lax.fori_loop(slot * part, slot * part + part, body, 0)

    def exchange_rows(source, target):
        first, second = source.shape[0], source.shape[1]
        blocks = [(p, q) for p in range(0, first, 16) for q in range(0, second, 16)]
        for n in range(0, len(blocks), 2):
            pieces = [
                source[p : p + 16, q : q + 16, :].reshape(256, lanes) for p, q in blocks[n : n + 2]
            ]
            flat = jnp.dot(
                swap, jnp.concatenate(pieces, axis=1), preferred_element_type=jnp.float32
            ).astype(jnp.bfloat16)
            for m, (p, q) in enumerate(blocks[n : n + 2]):
                target[q : q + 16, p : p + 16, :] = flat[:, m * lanes : (m + 1) * lanes].reshape(
                    16, 16, lanes
                )

    def part_s(ref, owner):
        return ref.at[:, pl.ds(pl.multiple_of(owner * rows_s, 16), rows_s), :]

    def remote(source, target, stream, mine, theirs, device):
        return pltpu.make_async_remote_copy(
            src_ref=source, dst_ref=target,
            send_sem=send_sem.at[stream, theirs], recv_sem=recv_sem.at[stream, mine],
            device_id=device, device_id_type=MESH,
        )

    def remote_y(source, target, half, way, n, mine, peer):
        return pltpu.make_async_remote_copy(
            src_ref=source, dst_ref=target,
            send_sem=send_y.at[half, way, n, peer], recv_sem=recv_y.at[half, way, n, mine],
            device_id=(peer, shelf), device_id_type=MESH,
        )

    def each(count, first, act):
        def body(step, carry):
            act((first + far_first(step, count)) % count)
            return carry

        lax.fori_loop(1, count, body, 0)

    def rows_of(ref, owner):
        return ref.at[pl.ds(pl.multiple_of(owner * rows_c, 16), rows_c), :]

    def y_forward(half):
        for n in range(per_y):

            def act(peer, n=n):
                remote_y(
                    home_y.at[half, peer * per_y + n], rows_of(at_y.at[half, n], ctrl),
                    half, 0, n, ctrl, peer,
                ).start()

            each(ctrls, ctrl, act)
            rows_of(at_y.at[half, n], ctrl)[...] = home_y[half, ctrl * per_y + n]

    def y_middle(half):
        for n in range(per_y):

            def arrived(peer, n=n):
                remote_y(
                    home_y.at[half, peer * per_y + n], rows_of(at_y.at[half, n], peer),
                    half, 0, n, peer, peer,
                ).wait()

            each(ctrls, ctrl, arrived)
            for m in range(0, ctrls * rows_c, 256):
                made = jnp.dot(
                    ctrl_ref[m : m + 256], at_y[half, n], preferred_element_type=jnp.float32
                )
                made_y[half, n, m : m + 256, :] = made.astype(jnp.bfloat16)

            def act(peer, n=n):
                remote_y(
                    rows_of(made_y.at[half, n], peer), back_y.at[half, ctrl * per_y + n],
                    half, 1, n, ctrl, peer,
                ).start()

            each(ctrls, ctrl, act)
            back_y[half, ctrl * per_y + n] = rows_of(made_y.at[half, n], ctrl)[...]

    def y_back_wait(half):
        for n in range(per_y):

            def act(peer, n=n):
                remote_y(
                    rows_of(made_y.at[half, n], peer), back_y.at[half, peer * per_y + n],
                    half, 1, n, peer, peer,
                ).wait()

            each(ctrls, ctrl, act)

    chunks = ((0, 2), (2, 1))

    def z_forward_copy(half, part, to):
        at, size = chunks[part]
        return remote(
            home_z.at[half, pl.ds(to * per_z + at, size)], part_s(at_z.at[pl.ds(at, size)], shelf),
            (2 * half) * 2 + part, shelf, to, (ctrl, 2 * to + half),
        )

    def z_forward(half):
        for part in range(2):
            at, size = chunks[part]
            each(chips, chip, lambda to: z_forward_copy(half, part, to).start())

            @pl.when(core != half)
            def _():
                z_forward_copy(half, part, chip).start()

            @pl.when(core == half)
            def _():
                part_s(at_z.at[pl.ds(at, size)], shelf)[...] = home_z[
                    half, pl.ds(chip * per_z + at, size)
                ]

    def z_forward_sent(half):
        for part in range(2):
            each(chips, chip, lambda to: z_forward_copy(half, part, to).wait_send())

            @pl.when(core != half)
            def _():
                z_forward_copy(half, part, chip).wait_send()

    def z_back_copy(half, part, peer):
        at, size = chunks[part]
        return remote(
            part_s(made_z.at[pl.ds(at, size)], peer),
            back_z.at[half, pl.ds(chip * per_z + at, size)],
            (2 * half + 1) * 2 + part, chip, peer, (ctrl, peer),
        )

    def z_middle(half):
        @pl.when(core == half)
        def _():
            for part in range(2):
                at, size = chunks[part]

                def arrived(peer):
                    remote(
                        home_z.at[half, pl.ds(0, size)], part_s(at_z.at[pl.ds(at, size)], peer),
                        (2 * half) * 2 + part, peer, 0, (ctrl, peer),
                    ).wait_recv()

                each(shelves, shelf, arrived)
                both = jnp.concatenate([at_z[at + n] for n in range(size)], axis=1)
                for m in range(0, shelves * rows_s, 256):
                    made = jnp.dot(shelf_ref[m : m + 256], both, preferred_element_type=jnp.float32)
                    for n in range(size):
                        made_z[at + n, m : m + 256, :] = made[
                            :, n * lanes : (n + 1) * lanes
                        ].astype(jnp.bfloat16)
                each(shelves, shelf, lambda peer: z_back_copy(half, part, peer).start())
                back_z[half, pl.ds(chip * per_z + at, size)] = part_s(
                    made_z.at[pl.ds(at, size)], shelf
                )[...]

    def z_back_from(half, part, source):
        at, size = chunks[part]
        return remote(
            part_s(made_z.at[pl.ds(at, size)], shelf),
            back_z.at[half, pl.ds(source * per_z + at, size)],
            (2 * half + 1) * 2 + part, source, 0, (ctrl, 2 * source + half),
        )

    def z_back_wait(half):
        for part in range(2):
            each(chips, chip, lambda source: z_back_from(half, part, source).wait_recv())

            @pl.when(core != half)
            def _():
                z_back_from(half, part, chip).wait_recv()

    def z_back_sent(half):
        @pl.when(core == half)
        def _():
            for part in range(2):
                each(shelves, shelf, lambda peer: z_back_copy(half, part, peer).wait_send())

    def one_step(repeat, carry):
        for p in range(0, rows_c, 16):
            rounded = state_ref[p : p + 16].astype(jnp.bfloat16).reshape(16 * rows_s, 256)
            made = jnp.dot(rounded, disk_ref[...], preferred_element_type=jnp.float32)
            made = made.astype(jnp.bfloat16).reshape(16, rows_s, 256)
            home_z[1, p : p + 16] = made[:, :, lanes:]
            home_z[0, p : p + 16] = made[:, :, :lanes]
        z_forward(1)
        exchange_rows(home_z.at[0], home_y.at[0])
        y_forward(0)

        @pl.when(repeat == 0)
        def _():
            gather_rows()
            prepare()

        fill(repeat * 4)
        z_middle(1)
        y_middle(0)
        fill(repeat * 4 + 1)
        y_back_wait(0)
        exchange_rows(back_y.at[0], home_z.at[0])
        z_forward(0)
        z_back_wait(1)
        exchange_rows(back_z.at[1], home_y.at[1])
        y_forward(1)
        z_middle(0)
        y_middle(1)
        fill(repeat * 4 + 2)
        fill(repeat * 4 + 3)
        y_back_wait(1)
        z_forward_sent(1)
        exchange_rows(back_y.at[1], home_z.at[1])
        z_back_wait(0)

        def update(row, inner):
            kept = 1.0 - rate_ref[pl.ds(row, 1), :] * shelf_rate_ref[...]
            third = jnp.concatenate([back_z[0, row], home_z[1, row]], axis=1)
            state_ref[row] = third.astype(jnp.float32) * scale_ref[0:1] + state_ref[row] * kept
            return inner

        lax.fori_loop(0, rows_c, update, 0, unroll=4)
        z_forward_sent(0)
        z_back_sent(0)
        z_back_sent(1)
        return carry

    lax.fori_loop(0, STEPS, one_step, 0)

    lead = lax.broadcasted_iota(jnp.int32, (8, 256), 0) == 0
    sums = jnp.where(lead, 1.0, disk_row[...])
    weight_ref[...] = jnp.zeros_like(weight_ref)
    mass_ref[...] = jnp.zeros_like(mass_ref)
    for r in range(rows_c // 4):
        both = lax.dot_general(
            sums,
            state_ref[4 * r : 4 * r + 4].reshape(4 * rows_s, 256),
            (((1,), (1,)), ((), ())),
            precision=HIGHEST,
            preferred_element_type=jnp.float32,
        )
        mass_ref[r : r + 1] = both[0:1]
        weight_ref[r : r + 1] = both[1:2]
    stages = spread_small(weight_ref[...], by_weight, shelf_stages(), send_w, recv_w)
    lax.fori_loop(1, stages[0][2], stages[0][0], 0)
    kept_ref[...] = jnp.zeros_like(kept_ref)
    ones = jnp.ones((8, 256), jnp.float32)
    for r in range(rows_c // 4):
        part = [
            state_ref[n] * (1.0 - rate_ref[n : n + 1] * shelf_rate_ref[...])
            for n in range(4 * r, 4 * r + 4)
        ]
        kept_ref[r : r + 1] = lax.dot_general(
            ones, jnp.concatenate(part, axis=0), NT,
            precision=HIGHEST, preferred_element_type=jnp.float32,
        )[0:1]
    lax.fori_loop(1, stages[0][2], stages[0][1], 0)
    lax.fori_loop(1, stages[1][2], stages[1][0], 0)
    terms = block_terms(label_ref, mass_ref, kept_ref)
    lax.fori_loop(1, stages[1][2], stages[1][1], 0)
    spread_pairs(by_weight, shelf_wide_rows)
    for z in range(8):
        weight_wide_ref[:, z * lanes : (z + 1) * lanes] = shelf_wide_rows[z, 0:rows_c]
    reduce_part(
        groups,
        shelf_labels_ref, weight_wide_ref, shelf_cols_ref, first_ref, terms,
        base_ref, sum_ref, total_ref, part_ref, block_mass_ref, wide, held,
        rows, tiles, highs, deeps, blocks, mass_plane, mass_deep, mass_high, send_r, recv_r,
    )


def spread_pairs(tiles, wide):
    lane = lax.broadcasted_iota(jnp.int32, (16, 128), 1) // 32
    for z in range(8):
        for q in range(4):
            made = jnp.zeros((16, 128), jnp.float32)
            for p in range(4):
                tile = tiles[p, z]
                moved = tile if p == q else pltpu.roll(tile, (32 * (p - q)) % 128, 1)
                made = jnp.where(lane == p, moved, made)
            wide[z, pl.ds(q, 16, stride=4), :] = made


def power_steps(prob, ctrl_rows, shelf_rows, disk, label_tile):
    rows_c, rows_s, _ = prob.shape
    bf, f32 = jnp.bfloat16, jnp.float32
    outs = [(prob.shape, f32), ((NBLK, NBLK), f32), ((8, 128), f32)]
    dma = pltpu.SemaphoreType.DMA
    return pl.pallas_call(
        steps_kernel,
        out_shape=tuple(jax.ShapeDtypeStruct(*out) for out in outs),
        in_specs=[pl.BlockSpec(memory_space=VMEM)] * 5,
        out_specs=tuple([pl.BlockSpec(memory_space=VMEM)] * len(outs)),
        scratch_shapes=[
            pltpu.VMEM((rows_s, rows_c, NBLK), bf),
            pltpu.VMEM((rows_c, SHELF), f32),
            pltpu.VMEM((rows_s, SHELF), f32),
            pltpu.VMEM((rows_c, SHELF), f32),
            pltpu.VMEM((16, 128), f32),
            pltpu.VMEM((16, 128), f32),
            pltpu.VMEM((8, 128), f32),
            pltpu.VMEM((NBLK, NBLK), f32),
            pltpu.VMEM((8, 128), f32),
            pltpu.VMEM((4, 2 * rows_s, SHELF), bf),
            pltpu.VMEM((rows_s, rows_c, NBLK), f32),
            pltpu.VMEM((GROUP, 32, NBLK), f32),
            *[pltpu.VMEM((GROUP, 8, 128), f32)] * 7,
            pltpu.VMEM((16, 128), f32),
            pltpu.VMEM((4, 8, 16, 128), f32),
            pltpu.VMEM((8, 2, 2, 24, CTRL), bf),
            pltpu.VMEM((8, 2, 2, 32, SHELF), bf),
            pltpu.VMEM((4, 8, 16, 128), f32),
            pltpu.VMEM((2, 8, 16, 128), f32),
            pltpu.VMEM((CTRL, CTRL), f32),
            pltpu.VMEM((rows_c, CTRL), bf),
            pltpu.VMEM((CTRL, CTRL), bf),
            pltpu.VMEM((SHELF, SHELF), bf),
            pltpu.VMEM((DISK, DISK), bf),
            pltpu.VMEM((16, 64, 128), f32),
            pltpu.VMEM((8, 64, 128), f32),
            pltpu.VMEM((rows_s, CTRL), f32),
            pltpu.VMEM((rows_c, DISK), f32),
            pltpu.VMEM((rows_s, DISK), f32),
            pltpu.VMEM((8, DISK), f32),
            pltpu.VMEM((8, DISK), f32),
            pltpu.VMEM((2, rows_s, rows_c, 128), bf),
            pltpu.VMEM((2, rows_c, rows_s, 128), bf),
            pltpu.VMEM((2, 2, CTRL, 128), bf),
            pltpu.VMEM((2, 2, CTRL, 128), bf),
            pltpu.VMEM((3, SHELF, 128), bf),
            pltpu.VMEM((3, SHELF, 128), bf),
            pltpu.VMEM((2, rows_s, rows_c, 128), bf),
            pltpu.VMEM((2, rows_c, rows_s, 128), bf),
            dma((2,)), dma((2,)), dma((2, 2, 4)), dma((2, 2, 4)), dma((2, 8)), dma((2, 8)),
            dma((2, 8)), dma((2, 8)), dma((2, 8)), dma((2, 8)), dma((2, 8)), dma((2, 8)),
            dma((2, 2, 2, 16)), dma((2, 2, 2, 16)), dma((8, 32)), dma((8, 32)),
            dma((5, 2, GROUP)), dma((5, 2, GROUP)),
        ],
        compiler_params=pltpu.CompilerParams(
            collective_id=4, has_side_effects=True, vmem_limit_bytes=56 << 20
        ),
        name="power_steps",
    )(prob, ctrl_rows, shelf_rows, disk, label_tile)


def local(prob, ctrl_rates, shelf_rates, disk_rates, labels):
    label_tile = as_tile(labels.astype(jnp.float32))
    iterate, numer, total = power_steps(prob, ctrl_rates, shelf_rates, disk_rates, label_tile)
    refined, coarse = balance_of(numer, total, label_tile, iterate)
    return (refined, coarse[0])


def solution(mesh):
    placed = (P("ctrl", "shelf", None), P("shelf", None), P("shelf", None), P(), P("ctrl", "shelf"))
    return jax.shard_map(
        local,
        mesh=mesh,
        in_specs=placed,
        out_specs=(P("ctrl", "shelf", None), P()),
        check_vma=False,
    )
```
